512 devices in a mesh: gx: 32 (over y_hi, z, core), gy: 16 (over y_lo, x).
Axes of the slice: x: 4, y: 8 (y_hi: 2, y_lo: 4; y = y_hi * 4 + y_lo), z: 8, core: 2. Of those that a mesh axis runs over, the one named last changes fastest.
Arguments:
- pressure0: float32 [4, 512, 2048], P(None, 'gx', 'gy'), may hold values from -6 to 6
- saturation0: float32 [4, 512, 2048], P(None, 'gx', 'gy'), may hold values from 0.1 to 0.9
- trans_x: float32 [4, 512, 2048], P(None, 'gx', 'gy'), may hold values from 0.1 to 2
- trans_y: float32 [4, 512, 2048], P(None, 'gx', 'gy'), may hold values from 0.1 to 2
- trans_z: float32 [3, 512, 2048], P(None, 'gx', 'gy'), may hold values from 0.05 to 1
- pore_volume: float32 [4, 512, 2048], P(None, 'gx', 'gy'), may hold values from 0.5 to 2
- upwind: int32 [4, 512, 2048], P(None, 'gx', 'gy'), may hold values from 0 to 63
- well_cell: int32 [32, 16, 64], P('gx', 'gy'), may hold values from 0 to 8191
- well_rate: float32 [32, 16, 64], P('gx', 'gy'), may hold values from -8 to 8
- plan: int32 [2, 32, 16, 64], P(None, 'gx', 'gy'), may hold values from 0 to 2
- observed: float32 [2, 2, 32, 16, 64], P(None, None, 'gx', 'gy'), may hold values from -6 to 6
Outputs:
- grad_x: float32 [4, 512, 2048], P(None, 'gx', 'gy')
- grad_y: float32 [4, 512, 2048], P(None, 'gx', 'gy')
- grad_z: float32 [3, 512, 2048], P(None, 'gx', 'gy')
The draws below stay inside these ranges and needn't reach their ends.
Inputs may be any that keep to these rules, and one draw needn't show every extreme that they name: `upwind`: bit 3 n + d of an entry is 1 where the cell itself is upstream of its forward face along x, y or layers (d = 0, 1, 2) in step n, 0 where the next cell is. `well_cell`: a cell of the well's own tile, numbered layer by layer, then row, then column. `plan`: 0 shut, 1 half rate, 2 full rate.
All inputs are finite; a program needn't handle non-finite values.
Results may differ from the reference program's by a relative error of at most 0.0001.
Values sent between devices are 32-bit elements; how exact they have to be, the bound alone decides.
A program may use at most 64 MiB of HBM per device.

```python
import math
import jax
import jax.numpy as jnp
from jax import lax

LAYERS = 4
CX = 16
CY = 128
STEPS = 2
WELL_DEV = 64
NX = 512
NY = 2048
TILES_X = 32
TILES_Y = 16


def set_ends(values, rng, low, largest):
    index_at = [jax.random.randint(jax.random.fold_in(rng, axis), (), 0, length) for axis, length in enumerate(values.shape)]
    main_axis = values.shape.index(max(values.shape))
    beside = index_at[:main_axis] + [(index_at[main_axis] + 1) % values.shape[main_axis]] + index_at[main_axis + 1:]
    return values.at[tuple(index_at)].set(low).at[tuple(beside)].set(largest)


def block_scale(stream_key, dims, cuts, smallest, top_value):
    factor_of = 1.0
    for dim, shards_of in cuts:
        draws = jax.random.uniform(jax.random.fold_in(jax.random.fold_in(stream_key, 6), dim), (shards_of,), jnp.float32, smallest / len(cuts), top_value / len(cuts))
        factor_of = factor_of * jnp.repeat(jnp.exp(draws), dims[dim] // shards_of).reshape((-1,) + (1,) * (len(dims) - 1 - dim))
    return factor_of


def noise(stream_key, dims, spread, reach, shards=(), held_as=jnp.bfloat16):
    values = spread * jax.random.normal(stream_key, dims, jnp.float32)
    if shards:
        values = values * block_scale(stream_key, dims, shards, -0.22, 0.18)
    return jnp.clip(values, -reach, reach).astype(held_as)


def setup_inputs(seed: int = 0) -> dict:
    keys = jax.random.split(jax.random.key(seed), 12)
    pressure0 = noise(keys[0], (LAYERS, NX, NY), 1.0, 6.0, ((1, 32), (2, 16)), jnp.float32)
    saturation0 = jnp.clip(0.1 + 0.79999997 * jax.random.uniform(keys[1], (LAYERS, NX, NY), jnp.float32) ** block_scale(keys[1], (LAYERS, NX, NY), ((1, 32), (2, 16)), -0.2, 0.2), 0.1, 0.9)
    trans_x = jnp.clip(jnp.exp(math.log(2.0) - 2.9957323 * jax.random.uniform(keys[2], (LAYERS, NX, NY), jnp.float32) ** block_scale(keys[2], (LAYERS, NX, NY), ((1, 32), (2, 16)), -0.2, 0.2)), 0.1, 2.0)
    trans_y = jnp.clip(jnp.exp(math.log(2.0) - 2.9957323 * jax.random.uniform(keys[3], (LAYERS, NX, NY), jnp.float32) ** block_scale(keys[3], (LAYERS, NX, NY), ((1, 32), (2, 16)), -0.2, 0.2)), 0.1, 2.0)
    trans_z = jnp.clip(jnp.exp(math.log(1.0) - 2.9957323 * jax.random.uniform(keys[4], (LAYERS - 1, NX, NY), jnp.float32) ** block_scale(keys[4], (LAYERS - 1, NX, NY), ((1, 32), (2, 16)), -0.2, 0.2)), 0.05, 1.0)
    pore_volume = jnp.clip(jnp.exp(math.log(2.0) - 1.3862944 * jax.random.uniform(keys[5], (LAYERS, NX, NY), jnp.float32) ** block_scale(keys[5], (LAYERS, NX, NY), ((1, 32), (2, 16)), -0.2, 0.2)), 0.5, 2.0)
    upwind = set_ends(jax.random.randint(keys[6], (LAYERS, NX, NY), 0, 2 ** (3 * STEPS)), jax.random.fold_in(keys[6], 1), 0, (2 ** (3 * STEPS)) - 1).astype(jnp.int32)
    well_cell = set_ends(jax.random.randint(keys[7], (TILES_X, TILES_Y, WELL_DEV), 0, LAYERS * CX * CY), jax.random.fold_in(keys[7], 1), 0, (LAYERS * CX * CY) - 1).astype(jnp.int32)
    well_rate = noise(keys[8], (TILES_X, TILES_Y, WELL_DEV), 2.0, 8.0, ((0, 32), (1, 16)), jnp.float32)
    plan = set_ends(jax.random.randint(keys[9], (STEPS, TILES_X, TILES_Y, WELL_DEV), 0, 3), jax.random.fold_in(keys[9], 1), 0, 2).astype(jnp.int32)
    observed = noise(keys[10], (STEPS, 2, TILES_X, TILES_Y, WELL_DEV), 1.0, 6.0, ((2, 32), (3, 16)), jnp.float32)
    return dict(pressure0=pressure0, saturation0=saturation0, trans_x=trans_x, trans_y=trans_y, trans_z=trans_z, pore_volume=pore_volume, upwind=upwind, well_cell=well_cell, well_rate=well_rate, plan=plan, observed=observed)


storage_coef = 1.0
time_step = 0.05

def mobility(saturation):
    wetted = saturation * saturation
    return wetted / (wetted + 0.5 * (1.0 - saturation) * (1.0 - saturation))

def vertical(center, faces):
    empty_layer = jnp.zeros_like(center[:1])
    upper_cells = jnp.concatenate([center[1:], empty_layer], axis=0)
    lower_cells = jnp.concatenate([empty_layer, center[:-1]], axis=0)
    face_up = jnp.concatenate([faces, empty_layer], axis=0)
    face_down = jnp.concatenate([empty_layer, faces], axis=0)
    return (face_up, face_down, upper_cells, lower_cells)

def jacobi(pressure, pressure_old, trans_x, trans_y, trans_z, pore_space, source, outside):
    center = pressure[:, 1:-1, 1:-1]
    east_face = trans_x[:, 1:-1, 1:-1]
    west_face = trans_x[:, :-2, 1:-1]
    north_face = trans_y[:, 1:-1, 1:-1]
    south_face = trans_y[:, 1:-1, :-2]
    face_up, face_down, upper_cells, lower_cells = vertical(center, trans_z[:, 1:-1, 1:-1])
    storage = storage_coef * pore_space[:, 1:-1, 1:-1]
    numerator = storage * pressure_old[:, 1:-1, 1:-1] + source[:, 1:-1, 1:-1] + east_face * pressure[:, 2:, 1:-1] + west_face * pressure[:, :-2, 1:-1] + north_face * pressure[:, 1:-1, 2:] + south_face * pressure[:, 1:-1, :-2] + face_up * upper_cells + face_down * lower_cells
    denominator = storage + east_face + west_face + north_face + south_face + face_up + face_down + outside[:, 1:-1, 1:-1]
    return numerator / denominator

def transport(pressure, saturation, trans_x, trans_y, trans_z, upwind_x, upwind_y, upwind_z, pore_space, outside):
    mobile = mobility(saturation)
    flux_x = (pressure[:, :-1, :] - pressure[:, 1:, :]) * (upwind_x[:, :-1, :] * mobile[:, :-1, :] + (trans_x[:, :-1, :] - upwind_x[:, :-1, :]) * mobile[:, 1:, :])
    flux_y = (pressure[:, :, :-1] - pressure[:, :, 1:]) * (upwind_y[:, :, :-1] * mobile[:, :, :-1] + (trans_y[:, :, :-1] - upwind_y[:, :, :-1]) * mobile[:, :, 1:])
    mid_pressure = pressure[:, 1:-1, 1:-1]
    mid_mobile = mobile[:, 1:-1, 1:-1]
    rise_upwind = upwind_z[:, 1:-1, 1:-1]
    rise_trans = trans_z[:, 1:-1, 1:-1]
    flux_z = (mid_pressure[:-1] - mid_pressure[1:]) * (rise_upwind * mid_mobile[:-1] + (rise_trans - rise_upwind) * mid_mobile[1:])
    empty_layer = jnp.zeros_like(mid_pressure[:1])
    net_outflow = flux_x[:, 1:, 1:-1] - flux_x[:, :-1, 1:-1] + flux_y[:, 1:-1, 1:] - flux_y[:, 1:-1, :-1] + jnp.concatenate([flux_z, empty_layer], axis=0) - jnp.concatenate([empty_layer, flux_z], axis=0)
    return saturation[:, 1:-1, 1:-1] - time_step * net_outflow / (pore_space[:, 1:-1, 1:-1] + outside[:, 1:-1, 1:-1])

def widen(array):
    return jnp.pad(array, ((0, 0), (1, 1), (1, 1)))

def advance(pressure, saturation, trans_x, trans_y, trans_z, upwind_x, upwind_y, upwind_z, pore_space, source, outside):
    padded = widen(pressure)
    first = jacobi(padded, padded, trans_x, trans_y, trans_z, pore_space, source, outside)
    second = jacobi(widen(first), padded, trans_x, trans_y, trans_z, pore_space, source, outside)
    moved = transport(widen(second), widen(saturation), trans_x, trans_y, trans_z, upwind_x, upwind_y, upwind_z, pore_space, outside)
    return (second, moved)

def reference(pressure0, saturation0, trans_x, trans_y, trans_z, pore_volume, upwind, well_cell, well_rate, plan, observed):
    grid_shape = pressure0.shape
    row_ids = lax.broadcasted_iota(jnp.int32, grid_shape, 1)
    col_ids = lax.broadcasted_iota(jnp.int32, grid_shape, 2)
    keep_x = row_ids < NX - 1
    keep_y = col_ids < NY - 1
    tile_rows = lax.broadcasted_iota(jnp.int32, well_cell.shape, 0)
    tile_cols = lax.broadcasted_iota(jnp.int32, well_cell.shape, 1)
    layer_of = well_cell // (CX * CY)
    row_of = tile_rows * CX + well_cell // CY % CX
    col_of = tile_cols * CY + well_cell % CY
    cells = (layer_of * (NX * NY) + row_of * NY + col_of).reshape(-1).astype(jnp.int32)
    outside = jnp.zeros((1, NX + 2, NY + 2), jnp.float32)
    pore_space = widen(pore_volume)

    def mismatch(trans_x, trans_y, trans_z):
        trans_xe = widen(jnp.where(keep_x, trans_x, 0.0))
        trans_ye = widen(jnp.where(keep_y, trans_y, 0.0))
        trans_zp = widen(trans_z)
        pressure, saturation = (pressure0, saturation0)
        total = jnp.zeros((), jnp.float32)
        for step_index in range(STEPS):
            rates = (well_rate * plan[step_index].astype(jnp.float32) * 0.5).reshape(-1)
            source = widen(jnp.zeros((LAYERS * NX * NY,), jnp.float32).at[cells].add(rates).reshape(grid_shape))
            bits = [jnp.bitwise_and(jnp.right_shift(upwind, 3 * step_index + direction), 1).astype(jnp.float32) for direction in range(3)]
            pressure, saturation = jax.checkpoint(advance)(pressure, saturation, trans_xe, trans_ye, trans_zp, trans_xe * widen(bits[0]), trans_ye * widen(bits[1]), trans_zp * widen(bits[2][:LAYERS - 1]), pore_space, source, outside)
            miss_p = pressure.reshape(-1)[cells] - observed[step_index, 0].reshape(-1)
            miss_s = saturation.reshape(-1)[cells] - observed[step_index, 1].reshape(-1)
            total = total + 0.5 * jnp.sum(miss_p * miss_p) + 0.5 * jnp.sum(miss_s * miss_s)
        return total
    gradients = jax.grad(mismatch, argnums=(0, 1, 2))(trans_x, trans_y, trans_z)
    return (gradients[0], gradients[1], gradients[2])
```

```python
import jax
import jax.numpy as jnp
from jax import lax
from jax.experimental import pallas as pl
from jax.experimental.pallas import tpu as pltpu
from jax.sharding import PartitionSpec as P

MESH = pl.DeviceIdType.MESH
time_step = 0.05

P0, S0, TX, TY, TZ, PV, UP, SLOTS = 0, 4, 8, 12, 16, 19, 23, 27
GROUPS = 4
WELLS = 64


def exchange_kernel(
    p0, s0, tx, ty, tz, pv, up, cell, rate, plan, observed,
    own, own_list, from_n, from_s, ext_n, ext_s, from_e, from_w, from_ne, from_nw, from_se, from_sw,
    up_int, cell_v, rate_v, plan_v, obs_v, xtra_n, xtra_s, pack_e, pack_w, in_sem, send_sem, recv_sem,
):
    gx, gy = lax.axis_index("gx"), lax.axis_index("gy")
    nx, ny = lax.axis_size("gx"), lax.axis_size("gy")
    north, south = lax.rem(gx + nx - 1, nx), lax.rem(gx + 1, nx)
    west, east = lax.rem(gy + ny - 1, ny), lax.rem(gy + 1, ny)

    barrier = pltpu.get_barrier_semaphore()
    for peer in (
        (north, gy), (south, gy), (gx, east), (gx, west),
        (south, east), (south, west), (north, east), (north, west),
    ):
        pl.semaphore_signal(barrier, inc=1, device_id=peer, device_id_type=MESH)

    loads = [
        (p0, own.at[pl.ds(P0, 4)]),
        (s0, own.at[pl.ds(S0, 4)]),
        (tx, own.at[pl.ds(TX, 4)]),
        (ty, own.at[pl.ds(TY, 4)]),
        (tz, own.at[pl.ds(TZ, 3)]),
        (pv, own.at[pl.ds(PV, 4)]),
        (up, up_int),
        (cell, cell_v),
        (rate, rate_v),
        (plan, plan_v),
        (observed, obs_v),
    ]
    loads = [pltpu.make_async_copy(a, b, in_sem.at[i]) for i, (a, b) in enumerate(loads)]
    for load in loads:
        load.start()
    for load in loads:
        load.wait()

    own[UP:SLOTS] = up_int[...].astype(jnp.float32)

    rates = rate_v[0] * 0.5
    rows = [
        cell_v[0].astype(jnp.float32),
        rates * plan_v[0, 0].astype(jnp.float32),
        rates * plan_v[1, 0].astype(jnp.float32),
        obs_v[0, 0, 0],
        obs_v[0, 1, 0],
        obs_v[1, 0, 0],
        obs_v[1, 1, 0],
        jnp.zeros((1, WELLS), jnp.float32),
    ]
    wells = jnp.concatenate(rows, axis=0)
    wells = jnp.concatenate([wells, wells], axis=1)
    own_list[...] = wells

    for layer in range(4):
        xtra_s[0, layer : layer + 1] = own[P0 + layer, 8:9]
        xtra_s[0, 4 + layer : 5 + layer] = own[TY + layer, 8:9]
        xtra_s[1, layer : layer + 1] = own[P0 + layer, 7:8]
        xtra_s[1, 4 + layer : 5 + layer] = own[P0 + layer, 9:10]
        xtra_s[2, layer : layer + 1] = own[TX + layer, 7:8]
        xtra_s[2, 4 + layer : 5 + layer] = own[TX + layer, 8:9]
        xtra_s[3, layer : layer + 1] = own[PV + layer, 8:9]
        if layer < 3:
            xtra_s[3, 4 + layer : 5 + layer] = own[TZ + layer, 8:9]
        xtra_n[0, layer : layer + 1] = own[P0 + layer, 7:8]
        xtra_n[0, 4 + layer : 5 + layer] = own[TX + layer, 7:8]
    xtra_s[3, 7:8] = jnp.zeros((1, 128), jnp.float32)
    xtra_s[4] = wells
    xtra_n[1] = wells

    block = lax.broadcasted_iota(jnp.int32, (8, 128), 1) // 16
    for pack in (pack_e, pack_w):
        pack[0] = xtra_s[0]
        pack[1] = wells
        pack[10] = wells
    for half in range(2):
        for group in range(GROUPS):
            first = second = None
            for k in range(min(8, SLOTS - 8 * group)):
                tile = own[8 * group + k, 8 * half : 8 * half + 8]
                if k:
                    tile = pltpu.roll(tile, 16 * k, axis=1)
                first = tile if first is None else jnp.where(block == k, tile, first)
                second = tile if second is None else jnp.where(block == (k + 7) % 8, tile, second)
            pack_e[2 + 4 * half + group] = first
            pack_w[2 + 4 * half + group] = second

    pl.semaphore_wait(barrier, 8)

    sends = [
        (own.at[:, pl.ds(0, 8), :], from_s, (north, gy)),
        (own.at[:, pl.ds(8, 8), :], from_n, (south, gy)),
        (xtra_s, ext_s, (north, gy)),
        (xtra_n, ext_n, (south, gy)),
        (pack_w.at[pl.ds(1, 9)], from_w, (gx, east)),
        (pack_e.at[pl.ds(1, 9)], from_e, (gx, west)),
        (pack_w.at[pl.ds(6, 5)], from_nw, (south, east)),
        (pack_e.at[pl.ds(6, 5)], from_ne, (south, west)),
        (pack_w.at[pl.ds(0, 6)], from_sw, (north, east)),
        (pack_e.at[pl.ds(0, 6)], from_se, (north, west)),
    ]
    sends = [
        pltpu.make_async_remote_copy(
            src_ref=src, dst_ref=dst, send_sem=send_sem.at[i], recv_sem=recv_sem.at[i],
            device_id=peer, device_id_type=MESH,
        )
        for i, (src, dst, peer) in enumerate(sends)
    ]
    for send in sends:
        send.start()
    for send in sends:
        send.wait()


def exchange(*args):
    f32 = jnp.float32
    tile = lambda *lead: jax.ShapeDtypeStruct(lead + (8, 128), f32)
    outs = (
        jax.ShapeDtypeStruct((SLOTS, 16, 128), f32),
        tile(),
        tile(SLOTS), tile(SLOTS), tile(2), tile(5),
        tile(9), tile(9),
        tile(5), tile(5), tile(6), tile(6),
    )
    return pl.pallas_call(
        exchange_kernel,
        out_shape=outs,
        in_specs=[pl.BlockSpec(memory_space=pl.ANY)] * 11,
        out_specs=[pl.BlockSpec(memory_space=pltpu.VMEM)] * 12,
        scratch_shapes=[
            pltpu.VMEM((4, 16, 128), jnp.int32),
            pltpu.VMEM((1, 1, WELLS), jnp.int32),
            pltpu.VMEM((1, 1, WELLS), f32),
            pltpu.VMEM((2, 1, 1, WELLS), jnp.int32),
            pltpu.VMEM((2, 2, 1, 1, WELLS), f32),
            pltpu.VMEM((2, 8, 128), f32),
            pltpu.VMEM((5, 8, 128), f32),
            pltpu.VMEM((11, 8, 128), f32),
            pltpu.VMEM((11, 8, 128), f32),
            pltpu.SemaphoreType.DMA((11,)),
            pltpu.SemaphoreType.DMA((10,)),
            pltpu.SemaphoreType.DMA((10,)),
        ],
        compiler_params=pltpu.CompilerParams(collective_id=0, has_side_effects=True),
    )(*args)


def x_next(v):
    return pltpu.roll(v, v.shape[0] - 1, axis=0)


def x_prev(v):
    return pltpu.roll(v, 1, axis=0)


def y_next(v):
    return pltpu.roll(v, v.shape[1] - 1, axis=1)


def y_prev(v):
    return pltpu.roll(v, 1, axis=1)


def main_tile(v):
    return v[8:24, 0:128]


def well_grids(lists_main, lists_side, missing_n, missing_s, missing_e, missing_w):
    lane = lax.broadcasted_iota(jnp.int32, (1, 128), 1)
    low = lane < 64
    side = [jnp.where(low, e, w) for e, w in lists_side]

    def ids(cells, drop):
        cells = cells.astype(jnp.int32)
        row = lax.shift_right_logical(cells, 7)
        col = jnp.bitwise_and(cells, 127)
        return row - 1024 * drop, col

    def columns(col):
        at = lax.broadcasted_iota(jnp.int32, (128, 128), 0)
        return jnp.where(at == col, 1.0, 0.0).astype(jnp.bfloat16)

    def split(v):
        hi = v.astype(jnp.bfloat16).astype(jnp.float32)
        mid = (v - hi).astype(jnp.bfloat16).astype(jnp.float32)
        return hi, mid, v - hi - mid

    def product(row, col_hot, value_rows, first, extra):
        count = 32 + (8 if extra else 0)
        at = lax.broadcasted_iota(jnp.int32, (32, 128), 0)
        at = lax.shift_right_logical(at, 3) * 16 + jnp.bitwise_and(at, 7) + first
        hit = row == at
        lhs = []
        for blocks in value_rows:
            lhs.append(
                jnp.concatenate([jnp.where(hit, b, 0.0) for b in blocks], axis=1)
            )
        if extra:
            at = lax.broadcasted_iota(jnp.int32, (8, 128), 0) * 16 + 8
            hit = row == at
            lhs.append(jnp.concatenate([jnp.where(hit, b, 0.0) for b in value_rows[0]], axis=1))
        lhs = jnp.concatenate(lhs, axis=0).astype(jnp.bfloat16)
        rhs = jnp.concatenate([col_hot] * len(value_rows[0]), axis=1)
        return lax.dot_general(
            lhs, rhs, (((1,), (1,)), ((), ())), preferred_element_type=jnp.float32
        )

    zero = jnp.zeros((1, 128), jnp.float32)

    def main_values(tile):
        out = []
        for q in range(1, 7):
            hi, mid, lo = split(tile[q : q + 1])
            out.append([jnp.where(low, hi, mid), jnp.where(low, lo, zero)])
        out.append([jnp.where(low, zero + 1.0, zero), zero])
        return out

    def side_values(tile):
        out = []
        for q in range(1, 7):
            out.append(list(split(tile[q : q + 1])))
        out.append([zero + 1.0, zero, zero])
        return out

    def main_part(tile, drop):
        row, col = ids(tile[0:1], drop)
        return row, columns(col), main_values(tile)

    def side_part(tile, drop):
        row, col = ids(tile[0:1], drop + jnp.where(low, missing_e, missing_w))
        col = jnp.where(low, jnp.where(col < 64, col, -1), jnp.where(col < 64, -1, col))
        return row, columns(col), side_values(tile)

    n, c, s = [main_part(t, d) for t, d in zip(lists_main, (missing_n, 0, missing_s))]
    sn, sc, ss = [side_part(t, d) for t, d in zip(side, (missing_n, 0, missing_s))]
    mains = [
        product(*n, 8, False), product(*c, 0, False), product(*c, 8, False), product(*s, 0, True)
    ]
    sides = [
        product(*sn, 8, False), product(*sc, 0, False), product(*sc, 8, False),
        product(*ss, 0, False),
    ]
    grids = []
    for q in range(7):
        layers = []
        for layer in range(4):
            at = (q * 4 + layer) * 8
            layers.append(
                jnp.concatenate(
                    [
                        jnp.concatenate([m[at : at + 8], d[at : at + 8]], axis=1)
                        for m, d in zip(mains, sides)
                    ],
                    axis=0,
                )
            )
        grids.append(layers)
    return grids, mains[3][224:232]


def compute_kernel(
    own, own_list, from_n, from_s, ext_n, ext_s, from_e, from_w, from_ne, from_nw, from_se, from_sw,
    out_x, out_y, out_z,
):
    gx, gy = lax.axis_index("gx"), lax.axis_index("gy")
    nx, ny = lax.axis_size("gx"), lax.axis_size("gy")
    miss_n, miss_s = gx == 0, gx == nx - 1
    miss_w, miss_e = gy == 0, gy == ny - 1
    shape = (32, 256)
    row = lax.broadcasted_iota(jnp.int32, shape, 0)
    lane = lax.broadcasted_iota(jnp.int32, shape, 1)

    row_low = jnp.where(miss_n, 8, 0)
    row_high = jnp.where(miss_s, 24, 32)
    lane_low = jnp.where(miss_e, 192, 128)
    lane_high = jnp.where(miss_w, 192, 256)
    row_ok = (row >= row_low) & (row < row_high)
    lane_ok = (lane < 128) | ((lane >= lane_low) & (lane < lane_high))
    valid = row_ok & lane_ok
    keep_x = valid & jnp.logical_not((row == 23) & miss_s)
    keep_y = valid & jnp.logical_not((lane == 127) & miss_e)

    block = lax.broadcasted_iota(jnp.int32, (8, 128), 1) // 16
    even = jnp.bitwise_and(block, 1) == 0
    merged = []
    for e_ref, w_ref, base in (
        (from_ne, from_nw, 0), (from_e, from_w, 1), (from_e, from_w, 5), (from_se, from_sw, 2)
    ):
        pairs = []
        for group in range(GROUPS):
            e, w = e_ref[base + group], w_ref[base + group]
            pairs.append((jnp.where(even, e, w), jnp.where(even, w, e)))
        merged.append(pairs)

    def field(slot, mask, fill):
        group, k = slot // 8, slot % 8
        sides = []
        for j in range(4):
            tile = merged[j][group][k % 2]
            sides.append(pltpu.roll(tile, 128 - 16 * k, axis=1) if k else tile)
        mains = [from_n[slot], own[slot], from_s[slot]]
        whole = jnp.concatenate(
            [jnp.concatenate(mains, axis=0), jnp.concatenate(sides, axis=0)], axis=1
        )
        return jnp.where(mask, whole, fill)

    L = range(4)
    p0 = [field(P0 + l, valid, 0.0) for l in L]
    s0 = [field(S0 + l, valid, 0.0) for l in L]
    tx = [field(TX + l, keep_x, 0.0) for l in L]
    ty = [field(TY + l, keep_y, 0.0) for l in L]
    tz = [field(TZ + l, valid, 0.0) for l in range(3)]
    pv = [field(PV + l, valid, 1.0) for l in L]
    up = [field(UP + l, valid, 0.0).astype(jnp.int32) for l in L]

    (src0, src1, obs_p0, obs_s0, obs_p1, obs_s1, count), src0_extra = well_grids(
        (ext_n[1], own_list[...], ext_s[4]),
        ((from_ne[4], from_nw[4]), (from_e[0], from_w[0]), (from_se[1], from_sw[1])),
        *[jnp.where(miss, 1, 0) for miss in (miss_n, miss_s, miss_e, miss_w)],
    )
    src, obs_p, obs_s = (src0, src1), (obs_p0, obs_p1), (obs_s0, obs_s1)

    row8 = lax.broadcasted_iota(jnp.int32, (8, 256), 0)

    def first_row(v, extra):
        top = jnp.where(row8 == 0, jnp.concatenate([extra, extra], axis=1), v[0:8])
        return jnp.concatenate([top, v[8:32]], axis=0)

    def last_row(v, extra):
        tail = jnp.where(row8 == 7, jnp.concatenate([extra, extra], axis=1), v[24:32])
        return jnp.concatenate([v[0:24], tail], axis=0)

    edge_n = jnp.where(miss_n, 0.0, ext_n[0])
    txw = [first_row(x_prev(tx[l]), edge_n[4 + l : 5 + l]) for l in L]
    tyw = [y_prev(ty[l]) for l in L]

    def z_sum(faces, values, l):
        total = None
        if l < 3:
            total = faces[l] * values[l + 1]
        if l > 0:
            term = faces[l - 1] * values[l - 1]
            total = term if total is None else total + term
        return total

    ones = [None] * 4
    inv = []
    for l in L:
        den = pv[l] + tx[l] + txw[l] + ty[l] + tyw[l]
        if l < 3:
            den = den + tz[l]
        if l > 0:
            den = den + tz[l - 1]
        inv.append(1.0 / den)

    def gather(values, nexts, prevs):
        out = []
        for l in L:
            total = tx[l] * nexts[l] + txw[l] * prevs[l]
            total = total + ty[l] * y_next(values[l]) + tyw[l] * y_prev(values[l])
            out.append(total + z_sum(tz, values, l))
        return out

    sub8 = lax.broadcasted_iota(jnp.int32, (8, 128), 0)
    cut = lambda t: jnp.where(miss_s, 0.0, t)
    t0 = ext_s[0]
    lane8 = lax.broadcasted_iota(jnp.int32, (8, 128), 1)
    side0 = jnp.where(lane8 < 64, jnp.where(miss_e, 0.0, from_se[0]), jnp.where(miss_w, 0.0, from_sw[0]))
    t0 = jnp.concatenate([cut(t0), cut(side0)], axis=1)
    t0n, t0p = y_next(t0)[:, 0:128], y_prev(t0)[:, 0:128]
    t0 = t0[:, 0:128]
    t1, t2, t3 = cut(ext_s[1]), cut(ext_s[2]), cut(ext_s[3])
    low4 = lambda t: pltpu.roll(t, 4, axis=0)
    ty_x = jnp.where((lane8 == 127) & miss_e, 0.0, low4(t0))
    tyw_x = low4(t0p)
    tx_x, txw_x = low4(t2), t2
    pv_x = jnp.where(miss_s, 1.0, t3)
    tz_x = jnp.where(sub8 < 3, low4(t3), 0.0)
    tzw_x = jnp.where((sub8 >= 1) & (sub8 < 4), pltpu.roll(low4(t3), 1, axis=0), 0.0)
    num_x = (
        pv_x * t0 + src0_extra + tx_x * low4(t1) + txw_x * t1 + ty_x * t0n + tyw_x * t0p
        + tz_x * pltpu.roll(t0, 7, axis=0) + tzw_x * pltpu.roll(t0, 1, axis=0)
    )
    q_extra = num_x / (pv_x + tx_x + txw_x + ty_x + tyw_x + tz_x + tzw_x)

    bits = [[[jnp.bitwise_and(up[l], 1 << (3 * n + d)) != 0 for d in range(3)] for l in L] for n in range(2)]

    ipv = [time_step / pv[l] for l in L]
    saved = []
    p, s = p0, s0
    for n in range(2):
        p_next = [x_next(p[l]) for l in L]
        p_prev = [x_prev(p[l]) for l in L]
        if n == 0:
            p_prev = [first_row(p_prev[l], edge_n[l : l + 1]) for l in L]
        base = [pv[l] * p[l] + src[n][l] for l in L]
        total = gather(p, p_next, p_prev)
        q = [(base[l] + total[l]) * inv[l] for l in L]
        q_next = [x_next(q[l]) for l in L]
        if n == 0:
            q_next = [last_row(q_next[l], q_extra[l : l + 1]) for l in L]
        total = gather(q, q_next, [x_prev(q[l]) for l in L])
        r = [(base[l] + total[l]) * inv[l] for l in L]

        den = []
        mob = []
        for l in L:
            wet = s[l] * s[l]
            dry = 1.0 - s[l]
            scale = 1.0 / (wet + 0.5 * dry * dry)
            den.append(scale)
            mob.append(wet * scale)
        dx = [r[l] - x_next(r[l]) for l in L]
        dy = [r[l] - y_next(r[l]) for l in L]
        dz = [r[l] - r[l + 1] for l in range(3)]
        fx = [jnp.where(bits[n][l][0], mob[l], x_next(mob[l])) for l in L]
        fy = [jnp.where(bits[n][l][1], mob[l], y_next(mob[l])) for l in L]
        fz = [jnp.where(bits[n][l][2], mob[l], mob[l + 1]) for l in range(3)]
        flow_x = [tx[l] * dx[l] * fx[l] for l in L]
        flow_y = [ty[l] * dy[l] * fy[l] for l in L]
        flow_z = [tz[l] * dz[l] * fz[l] for l in range(3)]
        moved = []
        for l in L:
            net = flow_x[l] - x_prev(flow_x[l]) + flow_y[l] - y_prev(flow_y[l])
            if l < 3:
                net = net + flow_z[l]
            if l > 0:
                net = net - flow_z[l - 1]
            moved.append(s[l] - ipv[l] * net)
        saved.append((p, q, r, s, den, dx, dy, dz, fx, fy, fz))
        p, s = r, moved

    grad_x = [None] * 4
    grad_y = [None] * 4
    grad_z = [None] * 3

    def accumulate(total, term):
        return term if total is None else total + term

    carried_p = [count[l] * p[l] - obs_p[1][l] for l in L]
    carried_s = [count[l] * s[l] - obs_s[1][l] for l in L]
    for n in (1, 0):
        p, q, r, s, den, dx, dy, dz, fx, fy, fz = saved[n]
        nu = [ipv[l] * carried_s[l] for l in L]
        mx = [x_next(nu[l]) - nu[l] for l in L]
        my = [y_next(nu[l]) - nu[l] for l in L]
        mz = [nu[l + 1] - nu[l] for l in range(3)]
        for l in L:
            grad_x[l] = accumulate(
                grad_x[l], main_tile(mx[l]) * main_tile(dx[l]) * main_tile(fx[l])
            )
            grad_y[l] = accumulate(
                grad_y[l], main_tile(my[l]) * main_tile(dy[l]) * main_tile(fy[l])
            )
            if l < 3:
                grad_z[l] = accumulate(
                    grad_z[l], main_tile(mz[l]) * main_tile(dz[l]) * main_tile(fz[l])
                )
        gx_ = [mx[l] * tx[l] for l in L]
        gy_ = [my[l] * ty[l] for l in L]
        gz_ = [mz[l] * tz[l] for l in range(3)]
        hx = [gx_[l] * fx[l] for l in L]
        hy = [gy_[l] * fy[l] for l in L]
        hz = [gz_[l] * fz[l] for l in range(3)]
        pi = []
        for l in L:
            total = carried_p[l] + hx[l] - x_prev(hx[l]) + hy[l] - y_prev(hy[l])
            if l < 3:
                total = total + hz[l]
            if l > 0:
                total = total - hz[l - 1]
            pi.append(total)
        if n:
            kx = [gx_[l] * dx[l] for l in L]
            ky = [gy_[l] * dy[l] for l in L]
            kz = [gz_[l] * dz[l] for l in range(3)]
            back_s = []
            for l in L:
                here = jnp.where(bits[n][l][0], kx[l], 0.0)
                there = kx[l] - here
                total = here + x_prev(there)
                here = jnp.where(bits[n][l][1], ky[l], 0.0)
                there = ky[l] - here
                total = total + here + y_prev(there)
                if l < 3:
                    total = total + jnp.where(bits[n][l][2], kz[l], 0.0)
                if l > 0:
                    total = total + jnp.where(bits[n][l - 1][2], 0.0, kz[l - 1])
                slope = (s[l] * den[l]) * ((1.0 - s[l]) * den[l])
                back_s.append(
                    carried_s[l] + slope * total + (count[l] * s[l] - obs_s[0][l])
                )
            carried_s = back_s

        w2 = [pi[l] * inv[l] for l in L]
        w2_next = [x_next(w2[l]) for l in L]
        rho = gather(w2, w2_next, [x_prev(w2[l]) for l in L])
        w1 = [rho[l] * inv[l] for l in L]
        w1_next = [x_next(w1[l]) for l in L]
        m = main_tile
        for l in L:
            a2, a1 = m(w2[l]), m(w1[l])
            rm, qm, pm = m(r[l]), m(q[l]), m(p[l])
            grad_x[l] = (
                grad_x[l]
                + a2 * (m(x_next(q[l])) - rm)
                + m(w2_next[l]) * (qm - m(x_next(r[l])))
                + a1 * (m(x_next(p[l])) - qm)
                + m(w1_next[l]) * (pm - m(x_next(q[l])))
            )
            grad_y[l] = (
                grad_y[l]
                + a2 * (m(y_next(q[l])) - rm)
                + m(y_next(w2[l])) * (qm - m(y_next(r[l])))
                + a1 * (m(y_next(p[l])) - qm)
                + m(y_next(w1[l])) * (pm - m(y_next(q[l])))
            )
            if l < 3:
                grad_z[l] = (
                    grad_z[l]
                    + a2 * (m(q[l + 1]) - rm)
                    + m(w2[l + 1]) * (qm - m(r[l + 1]))
                    + a1 * (m(p[l + 1]) - qm)
                    + m(w1[l + 1]) * (pm - m(q[l + 1]))
                )
        if n:
            back = gather(w1, w1_next, [x_prev(w1[l]) for l in L])
            carried_p = [
                back[l] + pv[l] * (w1[l] + w2[l]) + (count[l] * p[l] - obs_p[0][l]) for l in L
            ]

    for l in L:
        out_x[l] = jnp.where(main_tile(keep_x), grad_x[l], 0.0)
        out_y[l] = jnp.where(main_tile(keep_y), grad_y[l], 0.0)
        if l < 3:
            out_z[l] = grad_z[l]


def compute(*args):
    f32 = jnp.float32
    return pl.pallas_call(
        compute_kernel,
        out_shape=(
            jax.ShapeDtypeStruct((4, 16, 128), f32),
            jax.ShapeDtypeStruct((4, 16, 128), f32),
            jax.ShapeDtypeStruct((3, 16, 128), f32),
        ),
        in_specs=[pl.BlockSpec(memory_space=pltpu.VMEM)] * 12,
        out_specs=[pl.BlockSpec(memory_space=pltpu.VMEM)] * 3,
    )(*args)


def on_device(*args):
    return compute(*exchange(*args))


def solution(mesh):
    field = P(None, "gx", "gy")
    in_specs = (field,) * 7 + (
        P("gx", "gy", None),
        P("gx", "gy", None),
        P(None, "gx", "gy", None),
        P(None, None, "gx", "gy", None),
    )
    return jax.shard_map(
        on_device, mesh=mesh, in_specs=in_specs, out_specs=(field,) * 3, check_vma=False
    )
```

```python
import jax
import jax.numpy as jnp
from jax import lax
from jax.experimental import pallas as pl
from jax.experimental.pallas import tpu as pltpu
from jax.sharding import PartitionSpec as P

MESH = pl.DeviceIdType.MESH
time_step = 0.05

P0, S0, TX, TY, TZ, PV, UP, SLOTS = 0, 4, 8, 12, 16, 19, 23, 27
GROUPS = 4
WELLS = 64


def exchange_kernel(
    p0, s0, tx, ty, tz, pv, up, cell, rate, plan, observed,
    own, own_up, own_list, from_n, from_s, up_n, up_s, ext_n, ext_s,
    from_e, from_w, from_ne, from_nw, from_se, from_sw,
    cell_v, rate_v, plan_v, obs_v, xtra_n, xtra_s, pack_e, pack_w, in_sem, send_sem, recv_sem,
):
    gx, gy = lax.axis_index("gx"), lax.axis_index("gy")
    nx, ny = lax.axis_size("gx"), lax.axis_size("gy")
    has_n, has_s = gx > 0, gx < nx - 1
    has_w, has_e = gy > 0, gy < ny - 1
    both = jnp.logical_and
    peers = (
        (has_n, (gx - 1, gy)),
        (has_s, (gx + 1, gy)),
        (has_e, (gx, gy + 1)),
        (has_w, (gx, gy - 1)),
        (both(has_n, has_e), (gx - 1, gy + 1)),
        (both(has_n, has_w), (gx - 1, gy - 1)),
        (both(has_s, has_e), (gx + 1, gy + 1)),
        (both(has_s, has_w), (gx + 1, gy - 1)),
    )
    N, S, E, W, NE, NW, SE, SW = range(8)

    barrier = pltpu.get_barrier_semaphore()
    for here, peer in peers:
        @pl.when(here)
        def _():
            pl.semaphore_signal(barrier, inc=1, device_id=peer, device_id_type=MESH)

    fields = ((p0, P0, 4), (tx, TX, 4), (ty, TY, 4), (tz, TZ, 3), (pv, PV, 4), (s0, S0, 4))
    loads = [(ref, own.at[pl.ds(slot, n)]) for ref, slot, n in fields]
    loads += [(up, own_up), (cell, cell_v), (rate, rate_v), (plan, plan_v), (observed, obs_v)]
    loads = [pltpu.make_async_copy(a, b, in_sem.at[i]) for i, (a, b) in enumerate(loads)]
    for load in loads:
        load.start()

    rows = jnp.where(has_n, 1, 0) + jnp.where(has_s, 1, 0) + 1
    columns = jnp.where(has_e, 1, 0) + jnp.where(has_w, 1, 0) + 1
    pl.semaphore_wait(barrier, rows * columns - 1)

    sends = []

    def send(src, dst, to, origin):
        at = len(sends)
        here, peer = peers[to]
        copy = pltpu.make_async_remote_copy(
            src_ref=src, dst_ref=dst, send_sem=send_sem.at[at], recv_sem=recv_sem.at[at],
            device_id=peer, device_id_type=MESH,
        )
        sends.append((copy, here, peers[origin][0]))

        @pl.when(here)
        def _():
            copy.start()

    for ref, slot, n in fields:
        send(ref.at[:, pl.ds(0, 8), :], from_s.at[pl.ds(slot, n)], N, S)
        send(ref.at[:, pl.ds(8, 8), :], from_n.at[pl.ds(slot, n)], S, N)
    send(up.at[:, pl.ds(0, 8), :], up_s, N, S)
    send(up.at[:, pl.ds(8, 8), :], up_n, S, N)

    for load in loads:
        load.wait()

    rates = rate_v[0] * 0.5
    rows = [
        cell_v[0].astype(jnp.float32),
        rates * plan_v[0, 0].astype(jnp.float32),
        rates * plan_v[1, 0].astype(jnp.float32),
        obs_v[0, 0, 0],
        obs_v[0, 1, 0],
        obs_v[1, 0, 0],
        obs_v[1, 1, 0],
        jnp.zeros((1, WELLS), jnp.float32),
    ]
    wells = jnp.concatenate(rows, axis=0)
    wells = jnp.concatenate([wells, wells], axis=1)
    own_list[...] = wells

    for layer in range(4):
        xtra_s[0, layer : layer + 1] = own[P0 + layer, 8:9]
        xtra_s[0, 4 + layer : 5 + layer] = own[TY + layer, 8:9]
        xtra_s[1, layer : layer + 1] = own[P0 + layer, 7:8]
        xtra_s[1, 4 + layer : 5 + layer] = own[P0 + layer, 9:10]
        xtra_s[2, layer : layer + 1] = own[TX + layer, 7:8]
        xtra_s[2, 4 + layer : 5 + layer] = own[TX + layer, 8:9]
        xtra_s[3, layer : layer + 1] = own[PV + layer, 8:9]
        if layer < 3:
            xtra_s[3, 4 + layer : 5 + layer] = own[TZ + layer, 8:9]
        xtra_n[0, layer : layer + 1] = own[P0 + layer, 7:8]
        xtra_n[0, 4 + layer : 5 + layer] = own[TX + layer, 7:8]
    xtra_s[3, 7:8] = jnp.zeros((1, 128), jnp.float32)
    xtra_s[4] = wells
    xtra_n[1] = wells
    send(xtra_s, ext_s, N, S)
    send(xtra_n, ext_n, S, N)

    block = lax.broadcasted_iota(jnp.int32, (8, 128), 1) // 16
    for pack in (pack_e, pack_w):
        pack[0] = xtra_s[0]
        pack[1] = wells
        pack[10] = wells
    for half in range(2):
        for group in range(GROUPS):
            first = second = None
            for k in range(min(8, SLOTS - 8 * group)):
                slot = 8 * group + k
                if slot < UP:
                    tile = own[slot, 8 * half : 8 * half + 8]
                else:
                    tile = own_up[slot - UP, 8 * half : 8 * half + 8].astype(jnp.float32)
                if k:
                    tile = pltpu.roll(tile, 16 * k, axis=1)
                first = tile if first is None else jnp.where(block == k, tile, first)
                second = tile if second is None else jnp.where(block == (k + 7) % 8, tile, second)
            pack_e[2 + 4 * half + group] = first
            pack_w[2 + 4 * half + group] = second

    send(pack_w.at[pl.ds(1, 9)], from_w, E, W)
    send(pack_e.at[pl.ds(1, 9)], from_e, W, E)
    send(pack_w.at[pl.ds(6, 5)], from_nw, SE, NW)
    send(pack_e.at[pl.ds(6, 5)], from_ne, SW, NE)
    send(pack_w.at[pl.ds(0, 6)], from_sw, NE, SW)
    send(pack_e.at[pl.ds(0, 6)], from_se, NW, SE)
    for copy, here, origin in sends:
        @pl.when(origin)
        def _():
            copy.wait_recv()
    for copy, here, origin in sends:
        @pl.when(here)
        def _():
            copy.wait_send()


def exchange(*args):
    f32 = jnp.float32
    tile = lambda *lead: jax.ShapeDtypeStruct(lead + (8, 128), f32)
    ints = lambda *shape: jax.ShapeDtypeStruct(shape, jnp.int32)
    outs = (
        jax.ShapeDtypeStruct((UP, 16, 128), f32),
        ints(4, 16, 128),
        tile(),
        tile(UP), tile(UP), ints(4, 8, 128), ints(4, 8, 128), tile(2), tile(5),
        tile(9), tile(9),
        tile(5), tile(5), tile(6), tile(6),
    )
    return pl.pallas_call(
        exchange_kernel,
        out_shape=outs,
        in_specs=[pl.BlockSpec(memory_space=pl.ANY)] * 11,
        out_specs=[pl.BlockSpec(memory_space=pltpu.VMEM)] * len(outs),
        scratch_shapes=[
            pltpu.VMEM((1, 1, WELLS), jnp.int32),
            pltpu.VMEM((1, 1, WELLS), f32),
            pltpu.VMEM((2, 1, 1, WELLS), jnp.int32),
            pltpu.VMEM((2, 2, 1, 1, WELLS), f32),
            pltpu.VMEM((2, 8, 128), f32),
            pltpu.VMEM((5, 8, 128), f32),
            pltpu.VMEM((11, 8, 128), f32),
            pltpu.VMEM((11, 8, 128), f32),
            pltpu.SemaphoreType.DMA((11,)),
            pltpu.SemaphoreType.DMA((22,)),
            pltpu.SemaphoreType.DMA((22,)),
        ],
        compiler_params=pltpu.CompilerParams(collective_id=0, has_side_effects=True),
    )(*args)


def x_next(v):
    return pltpu.roll(v, v.shape[0] - 1, axis=0)


def x_prev(v):
    return pltpu.roll(v, 1, axis=0)


def y_next(v):
    return pltpu.roll(v, v.shape[1] - 1, axis=1)


def y_prev(v):
    return pltpu.roll(v, 1, axis=1)


def main_tile(v):
    return v[8:24, 0:128]


def well_grids(lists_main, lists_side, missing_n, missing_s, missing_e, missing_w):
    lane = lax.broadcasted_iota(jnp.int32, (1, 128), 1)
    low = lane < 64
    side = [jnp.where(low, e, w) for e, w in lists_side]

    def ids(cells, drop):
        cells = cells.astype(jnp.int32)
        row = lax.shift_right_logical(cells, 7)
        col = jnp.bitwise_and(cells, 127)
        return row - 1024 * drop, col

    def columns(col):
        at = lax.broadcasted_iota(jnp.int32, (128, 128), 0)
        return jnp.where(at == col, 1.0, 0.0).astype(jnp.bfloat16)

    def split(v):
        hi = v.astype(jnp.bfloat16).astype(jnp.float32)
        mid = (v - hi).astype(jnp.bfloat16).astype(jnp.float32)
        return hi, mid, v - hi - mid

    def product(row, col_hot, value_rows, first, extra):
        count = 32 + (8 if extra else 0)
        at = lax.broadcasted_iota(jnp.int32, (32, 128), 0)
        at = lax.shift_right_logical(at, 3) * 16 + jnp.bitwise_and(at, 7) + first
        hit = row == at
        lhs = []
        for blocks in value_rows:
            lhs.append(
                jnp.concatenate([jnp.where(hit, b, 0.0) for b in blocks], axis=1)
            )
        if extra:
            at = lax.broadcasted_iota(jnp.int32, (8, 128), 0) * 16 + 8
            hit = row == at
            lhs.append(jnp.concatenate([jnp.where(hit, b, 0.0) for b in value_rows[0]], axis=1))
        lhs = jnp.concatenate(lhs, axis=0).astype(jnp.bfloat16)
        rhs = jnp.concatenate([col_hot] * len(value_rows[0]), axis=1)
        return lax.dot_general(
            lhs, rhs, (((1,), (1,)), ((), ())), preferred_element_type=jnp.float32
        )

    zero = jnp.zeros((1, 128), jnp.float32)

    def main_values(tile):
        out = []
        for q in range(1, 7):
            hi, mid, lo = split(tile[q : q + 1])
            out.append([jnp.where(low, hi, mid), jnp.where(low, lo, zero)])
        out.append([jnp.where(low, zero + 1.0, zero), zero])
        return out

    def side_values(tile):
        out = []
        for q in range(1, 7):
            out.append(list(split(tile[q : q + 1])))
        out.append([zero + 1.0, zero, zero])
        return out

    def main_part(tile, drop):
        row, col = ids(tile[0:1], drop)
        return row, columns(col), main_values(tile)

    def side_part(tile, drop):
        row, col = ids(tile[0:1], drop + jnp.where(low, missing_e, missing_w))
        col = jnp.where(low, jnp.where(col < 64, col, -1), jnp.where(col < 64, -1, col))
        return row, columns(col), side_values(tile)

    n, c, s = [main_part(t, d) for t, d in zip(lists_main, (missing_n, 0, missing_s))]
    sn, sc, ss = [side_part(t, d) for t, d in zip(side, (missing_n, 0, missing_s))]
    mains = [
        product(*n, 8, False), product(*c, 0, False), product(*c, 8, False), product(*s, 0, True)
    ]
    sides = [
        product(*sn, 8, False), product(*sc, 0, False), product(*sc, 8, False),
        product(*ss, 0, False),
    ]
    grids = []
    for q in range(7):
        layers = []
        for layer in range(4):
            at = (q * 4 + layer) * 8
            layers.append(
                jnp.concatenate(
                    [
                        jnp.concatenate([m[at : at + 8], d[at : at + 8]], axis=1)
                        for m, d in zip(mains, sides)
                    ],
                    axis=0,
                )
            )
        grids.append(layers)
    return grids, mains[3][224:232]


def compute_kernel(
    own, own_up, own_list, from_n, from_s, up_n, up_s, ext_n, ext_s,
    from_e, from_w, from_ne, from_nw, from_se, from_sw,
    out_x, out_y, out_z,
):
    gx, gy = lax.axis_index("gx"), lax.axis_index("gy")
    nx, ny = lax.axis_size("gx"), lax.axis_size("gy")
    miss_n, miss_s = gx == 0, gx == nx - 1
    miss_w, miss_e = gy == 0, gy == ny - 1
    shape = (32, 256)
    row = lax.broadcasted_iota(jnp.int32, shape, 0)
    lane = lax.broadcasted_iota(jnp.int32, shape, 1)

    row_low = jnp.where(miss_n, 8, 0)
    row_high = jnp.where(miss_s, 24, 32)
    lane_low = jnp.where(miss_e, 192, 128)
    lane_high = jnp.where(miss_w, 192, 256)
    row_ok = (row >= row_low) & (row < row_high)
    lane_ok = (lane < 128) | ((lane >= lane_low) & (lane < lane_high))
    valid = row_ok & lane_ok
    keep_x = valid & jnp.logical_not((row == 23) & miss_s)
    keep_y = valid & jnp.logical_not((lane == 127) & miss_e)

    block = lax.broadcasted_iota(jnp.int32, (8, 128), 1) // 16
    even = jnp.bitwise_and(block, 1) == 0
    merged = []
    for e_ref, w_ref, base in (
        (from_ne, from_nw, 0), (from_e, from_w, 1), (from_e, from_w, 5), (from_se, from_sw, 2)
    ):
        pairs = []
        for group in range(GROUPS):
            e, w = e_ref[base + group], w_ref[base + group]
            pairs.append((jnp.where(even, e, w), jnp.where(even, w, e)))
        merged.append(pairs)

    def field(slot, mask, fill):
        group, k = slot // 8, slot % 8
        sides = []
        for j in range(4):
            tile = merged[j][group][k % 2]
            sides.append(pltpu.roll(tile, 128 - 16 * k, axis=1) if k else tile)
        if slot < UP:
            mains = [from_n[slot], own[slot], from_s[slot]]
        else:
            mains = [up_n[slot - UP], own_up[slot - UP], up_s[slot - UP]]
            sides = [side.astype(jnp.int32) for side in sides]
        whole = jnp.concatenate(
            [jnp.concatenate(mains, axis=0), jnp.concatenate(sides, axis=0)], axis=1
        )
        return jnp.where(mask, whole, fill)

    L = range(4)
    p0 = [field(P0 + l, valid, 0.0) for l in L]
    s0 = [field(S0 + l, valid, 0.0) for l in L]
    tx = [field(TX + l, keep_x, 0.0) for l in L]
    ty = [field(TY + l, keep_y, 0.0) for l in L]
    tz = [field(TZ + l, valid, 0.0) for l in range(3)]
    pv = [field(PV + l, valid, 1.0) for l in L]
    up = [field(UP + l, valid, 0) for l in L]

    (src0, src1, obs_p0, obs_s0, obs_p1, obs_s1, count), src0_extra = well_grids(
        (ext_n[1], own_list[...], ext_s[4]),
        ((from_ne[4], from_nw[4]), (from_e[0], from_w[0]), (from_se[1], from_sw[1])),
        *[jnp.where(miss, 1, 0) for miss in (miss_n, miss_s, miss_e, miss_w)],
    )
    src, obs_p, obs_s = (src0, src1), (obs_p0, obs_p1), (obs_s0, obs_s1)

    row8 = lax.broadcasted_iota(jnp.int32, (8, 256), 0)

    def first_row(v, extra):
        top = jnp.where(row8 == 0, jnp.concatenate([extra, extra], axis=1), v[0:8])
        return jnp.concatenate([top, v[8:32]], axis=0)

    def last_row(v, extra):
        tail = jnp.where(row8 == 7, jnp.concatenate([extra, extra], axis=1), v[24:32])
        return jnp.concatenate([v[0:24], tail], axis=0)

    edge_n = jnp.where(miss_n, 0.0, ext_n[0])
    txw = [first_row(x_prev(tx[l]), edge_n[4 + l : 5 + l]) for l in L]
    tyw = [y_prev(ty[l]) for l in L]

    def z_sum(faces, values, l):
        total = None
        if l < 3:
            total = faces[l] * values[l + 1]
        if l > 0:
            term = faces[l - 1] * values[l - 1]
            total = term if total is None else total + term
        return total

    ones = [None] * 4
    inv = []
    for l in L:
        den = pv[l] + tx[l] + txw[l] + ty[l] + tyw[l]
        if l < 3:
            den = den + tz[l]
        if l > 0:
            den = den + tz[l - 1]
        inv.append(1.0 / den)

    def gather(values, nexts, prevs):
        out = []
        for l in L:
            total = tx[l] * nexts[l] + txw[l] * prevs[l]
            total = total + ty[l] * y_next(values[l]) + tyw[l] * y_prev(values[l])
            out.append(total + z_sum(tz, values, l))
        return out

    sub8 = lax.broadcasted_iota(jnp.int32, (8, 128), 0)
    cut = lambda t: jnp.where(miss_s, 0.0, t)
    t0 = ext_s[0]
    lane8 = lax.broadcasted_iota(jnp.int32, (8, 128), 1)
    side0 = jnp.where(lane8 < 64, jnp.where(miss_e, 0.0, from_se[0]), jnp.where(miss_w, 0.0, from_sw[0]))
    t0 = jnp.concatenate([cut(t0), cut(side0)], axis=1)
    t0n, t0p = y_next(t0)[:, 0:128], y_prev(t0)[:, 0:128]
    t0 = t0[:, 0:128]
    t1, t2, t3 = cut(ext_s[1]), cut(ext_s[2]), cut(ext_s[3])
    low4 = lambda t: pltpu.roll(t, 4, axis=0)
    ty_x = jnp.where((lane8 == 127) & miss_e, 0.0, low4(t0))
    tyw_x = low4(t0p)
    tx_x, txw_x = low4(t2), t2
    pv_x = jnp.where(miss_s, 1.0, t3)
    tz_x = jnp.where(sub8 < 3, low4(t3), 0.0)
    tzw_x = jnp.where((sub8 >= 1) & (sub8 < 4), pltpu.roll(low4(t3), 1, axis=0), 0.0)
    num_x = (
        pv_x * t0 + src0_extra + tx_x * low4(t1) + txw_x * t1 + ty_x * t0n + tyw_x * t0p
        + tz_x * pltpu.roll(t0, 7, axis=0) + tzw_x * pltpu.roll(t0, 1, axis=0)
    )
    q_extra = num_x / (pv_x + tx_x + txw_x + ty_x + tyw_x + tz_x + tzw_x)

    bits = [[[jnp.bitwise_and(up[l], 1 << (3 * n + d)) != 0 for d in range(3)] for l in L] for n in range(2)]

    ipv = [time_step / pv[l] for l in L]
    saved = []
    p, s = p0, s0
    for n in range(2):
        p_next = [x_next(p[l]) for l in L]
        p_prev = [x_prev(p[l]) for l in L]
        if n == 0:
            p_prev = [first_row(p_prev[l], edge_n[l : l + 1]) for l in L]
        base = [pv[l] * p[l] + src[n][l] for l in L]
        total = gather(p, p_next, p_prev)
        q = [(base[l] + total[l]) * inv[l] for l in L]
        q_next = [x_next(q[l]) for l in L]
        if n == 0:
            q_next = [last_row(q_next[l], q_extra[l : l + 1]) for l in L]
        total = gather(q, q_next, [x_prev(q[l]) for l in L])
        r = [(base[l] + total[l]) * inv[l] for l in L]

        den = []
        mob = []
        for l in L:
            wet = s[l] * s[l]
            dry = 1.0 - s[l]
            scale = 1.0 / (wet + 0.5 * dry * dry)
            den.append(scale)
            mob.append(wet * scale)
        dx = [r[l] - x_next(r[l]) for l in L]
        dy = [r[l] - y_next(r[l]) for l in L]
        dz = [r[l] - r[l + 1] for l in range(3)]
        fx = [jnp.where(bits[n][l][0], mob[l], x_next(mob[l])) for l in L]
        fy = [jnp.where(bits[n][l][1], mob[l], y_next(mob[l])) for l in L]
        fz = [jnp.where(bits[n][l][2], mob[l], mob[l + 1]) for l in range(3)]
        flow_x = [tx[l] * dx[l] * fx[l] for l in L]
        flow_y = [ty[l] * dy[l] * fy[l] for l in L]
        flow_z = [tz[l] * dz[l] * fz[l] for l in range(3)]
        moved = []
        for l in L:
            net = flow_x[l] - x_prev(flow_x[l]) + flow_y[l] - y_prev(flow_y[l])
            if l < 3:
                net = net + flow_z[l]
            if l > 0:
                net = net - flow_z[l - 1]
            moved.append(s[l] - ipv[l] * net)
        saved.append((p, q, r, s, den, dx, dy, dz, fx, fy, fz))
        p, s = r, moved

    grad_x = [None] * 4
    grad_y = [None] * 4
    grad_z = [None] * 3

    def accumulate(total, term):
        return term if total is None else total + term

    carried_p = [count[l] * p[l] - obs_p[1][l] for l in L]
    carried_s = [count[l] * s[l] - obs_s[1][l] for l in L]
    for n in (1, 0):
        p, q, r, s, den, dx, dy, dz, fx, fy, fz = saved[n]
        nu = [ipv[l] * carried_s[l] for l in L]
        mx = [x_next(nu[l]) - nu[l] for l in L]
        my = [y_next(nu[l]) - nu[l] for l in L]
        mz = [nu[l + 1] - nu[l] for l in range(3)]
        for l in L:
            grad_x[l] = accumulate(
                grad_x[l], main_tile(mx[l]) * main_tile(dx[l]) * main_tile(fx[l])
            )
            grad_y[l] = accumulate(
                grad_y[l], main_tile(my[l]) * main_tile(dy[l]) * main_tile(fy[l])
            )
            if l < 3:
                grad_z[l] = accumulate(
                    grad_z[l], main_tile(mz[l]) * main_tile(dz[l]) * main_tile(fz[l])
                )
        gx_ = [mx[l] * tx[l] for l in L]
        gy_ = [my[l] * ty[l] for l in L]
        gz_ = [mz[l] * tz[l] for l in range(3)]
        hx = [gx_[l] * fx[l] for l in L]
        hy = [gy_[l] * fy[l] for l in L]
        hz = [gz_[l] * fz[l] for l in range(3)]
        pi = []
        for l in L:
            total = carried_p[l] + hx[l] - x_prev(hx[l]) + hy[l] - y_prev(hy[l])
            if l < 3:
                total = total + hz[l]
            if l > 0:
                total = total - hz[l - 1]
            pi.append(total)
        if n:
            kx = [gx_[l] * dx[l] for l in L]
            ky = [gy_[l] * dy[l] for l in L]
            kz = [gz_[l] * dz[l] for l in range(3)]
            back_s = []
            for l in L:
                here = jnp.where(bits[n][l][0], kx[l], 0.0)
                there = kx[l] - here
                total = here + x_prev(there)
                here = jnp.where(bits[n][l][1], ky[l], 0.0)
                there = ky[l] - here
                total = total + here + y_prev(there)
                if l < 3:
                    total = total + jnp.where(bits[n][l][2], kz[l], 0.0)
                if l > 0:
                    total = total + jnp.where(bits[n][l - 1][2], 0.0, kz[l - 1])
                slope = (s[l] * den[l]) * ((1.0 - s[l]) * den[l])
                back_s.append(
                    carried_s[l] + slope * total + (count[l] * s[l] - obs_s[0][l])
                )
            carried_s = back_s

        w2 = [pi[l] * inv[l] for l in L]
        w2_next = [x_next(w2[l]) for l in L]
        rho = gather(w2, w2_next, [x_prev(w2[l]) for l in L])
        w1 = [rho[l] * inv[l] for l in L]
        w1_next = [x_next(w1[l]) for l in L]
        m = main_tile
        for l in L:
            a2, a1 = m(w2[l]), m(w1[l])
            rm, qm, pm = m(r[l]), m(q[l]), m(p[l])
            grad_x[l] = (
                grad_x[l]
                + a2 * (m(x_next(q[l])) - rm)
                + m(w2_next[l]) * (qm - m(x_next(r[l])))
                + a1 * (m(x_next(p[l])) - qm)
                + m(w1_next[l]) * (pm - m(x_next(q[l])))
            )
            grad_y[l] = (
                grad_y[l]
                + a2 * (m(y_next(q[l])) - rm)
                + m(y_next(w2[l])) * (qm - m(y_next(r[l])))
                + a1 * (m(y_next(p[l])) - qm)
                + m(y_next(w1[l])) * (pm - m(y_next(q[l])))
            )
            if l < 3:
                grad_z[l] = (
                    grad_z[l]
                    + a2 * (m(q[l + 1]) - rm)
                    + m(w2[l + 1]) * (qm - m(r[l + 1]))
                    + a1 * (m(p[l + 1]) - qm)
                    + m(w1[l + 1]) * (pm - m(q[l + 1]))
                )
        if n:
            back = gather(w1, w1_next, [x_prev(w1[l]) for l in L])
            carried_p = [
                back[l] + pv[l] * (w1[l] + w2[l]) + (count[l] * p[l] - obs_p[0][l]) for l in L
            ]

    for l in L:
        out_x[l] = jnp.where(main_tile(keep_x), grad_x[l], 0.0)
        out_y[l] = jnp.where(main_tile(keep_y), grad_y[l], 0.0)
        if l < 3:
            out_z[l] = grad_z[l]


def compute(*args):
    f32 = jnp.float32
    return pl.pallas_call(
        compute_kernel,
        out_shape=(
            jax.ShapeDtypeStruct((4, 16, 128), f32),
            jax.ShapeDtypeStruct((4, 16, 128), f32),
            jax.ShapeDtypeStruct((3, 16, 128), f32),
        ),
        in_specs=[pl.BlockSpec(memory_space=pltpu.VMEM)] * 15,
        out_specs=[pl.BlockSpec(memory_space=pltpu.VMEM)] * 3,
    )(*args)


def on_device(*args):
    return compute(*exchange(*args))


def solution(mesh):
    field = P(None, "gx", "gy")
    in_specs = (field,) * 7 + (
        P("gx", "gy", None),
        P("gx", "gy", None),
        P(None, "gx", "gy", None),
        P(None, None, "gx", "gy", None),
    )
    return jax.shard_map(
        on_device, mesh=mesh, in_specs=in_specs, out_specs=(field,) * 3, check_vma=False
    )
```

```python
import jax
import jax.numpy as jnp
from jax import lax
from jax.experimental import pallas as pl
from jax.experimental.pallas import tpu as pltpu
from jax.sharding import PartitionSpec as P

MESH = pl.DeviceIdType.MESH
time_step = 0.05

P0, S0, TX, TY, TZ, PV, UP, SLOTS = 0, 4, 8, 12, 16, 19, 23, 27
GROUPS = 4
WELLS = 64


def start_exchange(args, halo, work, sems):
    p0, s0, tx, ty, tz, pv, up, cell, rate, plan, observed = args
    own, own_up, own_list, from_n, from_s, up_n, up_s, ext_n, ext_s = halo[:9]
    from_e, from_w, from_ne, from_nw, from_se, from_sw = halo[9:]
    cell_v, rate_v, plan_v, obs_v, xtra_n, xtra_s, pack_e, pack_w = work
    in_sem, send_sem, recv_sem = sems
    gx, gy = lax.axis_index("gx"), lax.axis_index("gy")
    nx, ny = lax.axis_size("gx"), lax.axis_size("gy")
    has_n, has_s = gx > 0, gx < nx - 1
    has_w, has_e = gy > 0, gy < ny - 1
    both = jnp.logical_and
    peers = (
        (has_n, (gx - 1, gy)),
        (has_s, (gx + 1, gy)),
        (has_e, (gx, gy + 1)),
        (has_w, (gx, gy - 1)),
        (both(has_n, has_e), (gx - 1, gy + 1)),
        (both(has_n, has_w), (gx - 1, gy - 1)),
        (both(has_s, has_e), (gx + 1, gy + 1)),
        (both(has_s, has_w), (gx + 1, gy - 1)),
    )
    N, S, E, W, NE, NW, SE, SW = range(8)

    barrier = pltpu.get_barrier_semaphore()
    for here, peer in peers:
        @pl.when(here)
        def _():
            pl.semaphore_signal(barrier, inc=1, device_id=peer, device_id_type=MESH)

    fields = ((p0, P0, 4), (tx, TX, 4), (ty, TY, 4), (tz, TZ, 3), (pv, PV, 4), (s0, S0, 4))
    loads = [(ref, own.at[pl.ds(slot, n)]) for ref, slot, n in fields]
    loads += [(up, own_up), (cell, cell_v), (rate, rate_v), (plan, plan_v), (observed, obs_v)]
    loads = [pltpu.make_async_copy(a, b, in_sem.at[i]) for i, (a, b) in enumerate(loads)]
    for load in loads:
        load.start()

    for load in loads:
        load.wait()

    rates = rate_v[0] * 0.5
    rows = [
        cell_v[0].astype(jnp.float32),
        rates * plan_v[0, 0].astype(jnp.float32),
        rates * plan_v[1, 0].astype(jnp.float32),
        obs_v[0, 0, 0],
        obs_v[0, 1, 0],
        obs_v[1, 0, 0],
        obs_v[1, 1, 0],
        jnp.zeros((1, WELLS), jnp.float32),
    ]
    wells = jnp.concatenate(rows, axis=0)
    wells = jnp.concatenate([wells, wells], axis=1)
    own_list[...] = wells

    for layer in range(4):
        xtra_s[0, layer : layer + 1] = own[P0 + layer, 8:9]
        xtra_s[0, 4 + layer : 5 + layer] = own[TY + layer, 8:9]
        xtra_s[1, layer : layer + 1] = own[P0 + layer, 7:8]
        xtra_s[1, 4 + layer : 5 + layer] = own[P0 + layer, 9:10]
        xtra_s[2, layer : layer + 1] = own[TX + layer, 7:8]
        xtra_s[2, 4 + layer : 5 + layer] = own[TX + layer, 8:9]
        xtra_s[3, layer : layer + 1] = own[PV + layer, 8:9]
        if layer < 3:
            xtra_s[3, 4 + layer : 5 + layer] = own[TZ + layer, 8:9]
        xtra_n[0, layer : layer + 1] = own[P0 + layer, 7:8]
        xtra_n[0, 4 + layer : 5 + layer] = own[TX + layer, 7:8]
    xtra_s[3, 7:8] = jnp.zeros((1, 128), jnp.float32)
    xtra_s[4] = wells
    xtra_n[1] = wells

    block = lax.broadcasted_iota(jnp.int32, (8, 128), 1) // 16
    for pack in (pack_e, pack_w):
        pack[0] = xtra_s[0]
        pack[1] = wells
        pack[10] = wells
    for half in range(2):
        for group in range(GROUPS):
            first = second = None
            for k in range(min(8, SLOTS - 8 * group)):
                slot = 8 * group + k
                if slot < UP:
                    tile = own[slot, 8 * half : 8 * half + 8]
                else:
                    tile = own_up[slot - UP, 8 * half : 8 * half + 8].astype(jnp.float32)
                if k:
                    tile = pltpu.roll(tile, 16 * k, axis=1)
                first = tile if first is None else jnp.where(block == k, tile, first)
                second = tile if second is None else jnp.where(block == (k + 7) % 8, tile, second)
            pack_e[2 + 4 * half + group] = first
            pack_w[2 + 4 * half + group] = second

    rows = jnp.where(has_n, 1, 0) + jnp.where(has_s, 1, 0) + 1
    columns = jnp.where(has_e, 1, 0) + jnp.where(has_w, 1, 0) + 1
    pl.semaphore_wait(barrier, rows * columns - 1)

    sends = []

    def send(src, dst, to, origin):
        at = len(sends)
        here, peer = peers[to]
        copy = pltpu.make_async_remote_copy(
            src_ref=src, dst_ref=dst, send_sem=send_sem.at[at], recv_sem=recv_sem.at[at],
            device_id=peer, device_id_type=MESH,
        )
        sends.append((copy, here, peers[origin][0]))

        @pl.when(here)
        def _():
            copy.start()

    send(pack_w.at[pl.ds(6, 5)], from_nw, SE, NW)
    send(pack_e.at[pl.ds(6, 5)], from_ne, SW, NE)
    send(pack_w.at[pl.ds(0, 6)], from_sw, NE, SW)
    send(pack_e.at[pl.ds(0, 6)], from_se, NW, SE)
    send(xtra_s, ext_s, N, S)
    send(xtra_n, ext_n, S, N)
    send(own.at[:, pl.ds(0, 8), :], from_s, N, S)
    send(own.at[:, pl.ds(8, 8), :], from_n, S, N)
    send(own_up.at[:, pl.ds(0, 8), :], up_s, N, S)
    send(own_up.at[:, pl.ds(8, 8), :], up_n, S, N)
    send(pack_w.at[pl.ds(1, 9)], from_w, E, W)
    send(pack_e.at[pl.ds(1, 9)], from_e, W, E)
    return sends


def x_next(v):
    return pltpu.roll(v, v.shape[0] - 1, axis=0)


def x_prev(v):
    return pltpu.roll(v, 1, axis=0)


def y_next(v):
    return pltpu.roll(v, v.shape[1] - 1, axis=1)


def y_prev(v):
    return pltpu.roll(v, 1, axis=1)


def main_tile(v):
    return v[8:24, 0:128]


def well_grids(lists_main, lists_side, missing_n, missing_s, missing_e, missing_w):
    lane = lax.broadcasted_iota(jnp.int32, (1, 128), 1)
    low = lane < 64
    side = [jnp.where(low, e, w) for e, w in lists_side]

    def ids(cells, drop):
        cells = cells.astype(jnp.int32)
        row = lax.shift_right_logical(cells, 7)
        col = jnp.bitwise_and(cells, 127)
        return row - 1024 * drop, col

    def columns(col):
        at = lax.broadcasted_iota(jnp.int32, (128, 128), 0)
        return jnp.where(at == col, 1.0, 0.0).astype(jnp.bfloat16)

    def split(v):
        hi = v.astype(jnp.bfloat16).astype(jnp.float32)
        mid = (v - hi).astype(jnp.bfloat16).astype(jnp.float32)
        return hi, mid, v - hi - mid

    def product(row, col_hot, value_rows, first, extra):
        count = 32 + (8 if extra else 0)
        at = lax.broadcasted_iota(jnp.int32, (32, 128), 0)
        at = lax.shift_right_logical(at, 3) * 16 + jnp.bitwise_and(at, 7) + first
        hit = row == at
        lhs = []
        for blocks in value_rows:
            lhs.append(
                jnp.concatenate([jnp.where(hit, b, 0.0) for b in blocks], axis=1)
            )
        if extra:
            at = lax.broadcasted_iota(jnp.int32, (8, 128), 0) * 16 + 8
            hit = row == at
            lhs.append(jnp.concatenate([jnp.where(hit, b, 0.0) for b in value_rows[0]], axis=1))
        lhs = jnp.concatenate(lhs, axis=0).astype(jnp.bfloat16)
        rhs = jnp.concatenate([col_hot] * len(value_rows[0]), axis=1)
        return lax.dot_general(
            lhs, rhs, (((1,), (1,)), ((), ())), preferred_element_type=jnp.float32
        )

    zero = jnp.zeros((1, 128), jnp.float32)

    def main_values(tile):
        out = []
        for q in range(1, 7):
            hi, mid, lo = split(tile[q : q + 1])
            out.append([jnp.where(low, hi, mid), jnp.where(low, lo, zero)])
        out.append([jnp.where(low, zero + 1.0, zero), zero])
        return out

    def side_values(tile):
        out = []
        for q in range(1, 7):
            out.append(list(split(tile[q : q + 1])))
        out.append([zero + 1.0, zero, zero])
        return out

    def main_part(tile, drop):
        row, col = ids(tile[0:1], drop)
        return row, columns(col), main_values(tile)

    def side_part(tile, drop):
        row, col = ids(tile[0:1], drop + jnp.where(low, missing_e, missing_w))
        col = jnp.where(low, jnp.where(col < 64, col, -1), jnp.where(col < 64, -1, col))
        return row, columns(col), side_values(tile)

    n, c, s = [main_part(t, d) for t, d in zip(lists_main, (missing_n, 0, missing_s))]
    sn, sc, ss = [side_part(t, d) for t, d in zip(side, (missing_n, 0, missing_s))]
    mains = [
        product(*n, 8, False), product(*c, 0, False), product(*c, 8, False), product(*s, 0, True)
    ]
    sides = [
        product(*sn, 8, False), product(*sc, 0, False), product(*sc, 8, False),
        product(*ss, 0, False),
    ]
    grids = []
    for q in range(7):
        layers = []
        for layer in range(4):
            at = (q * 4 + layer) * 8
            layers.append(
                jnp.concatenate(
                    [
                        jnp.concatenate([m[at : at + 8], d[at : at + 8]], axis=1)
                        for m, d in zip(mains, sides)
                    ],
                    axis=0,
                )
            )
        grids.append(layers)
    return grids, mains[3][224:232]


def adjoint_kernel(*refs):
    args, out = refs[:11], refs[11]
    halo, work, sems = refs[12:27], refs[27:35], refs[35:]
    sends = start_exchange(args, halo, work, sems)
    own, own_up, own_list, from_n, from_s, up_n, up_s, ext_n, ext_s = halo[:9]
    from_e, from_w, from_ne, from_nw, from_se, from_sw = halo[9:]
    for copy, here, origin in sends:
        @pl.when(origin)
        def _():
            copy.wait_recv()

    gx, gy = lax.axis_index("gx"), lax.axis_index("gy")
    nx, ny = lax.axis_size("gx"), lax.axis_size("gy")
    miss_n, miss_s = gx == 0, gx == nx - 1
    miss_w, miss_e = gy == 0, gy == ny - 1
    shape = (32, 256)
    row = lax.broadcasted_iota(jnp.int32, shape, 0)
    lane = lax.broadcasted_iota(jnp.int32, shape, 1)

    row_low = jnp.where(miss_n, 8, 0)
    row_high = jnp.where(miss_s, 24, 32)
    lane_low = jnp.where(miss_e, 192, 128)
    lane_high = jnp.where(miss_w, 192, 256)
    row_ok = (row >= row_low) & (row < row_high)
    lane_ok = (lane < 128) | ((lane >= lane_low) & (lane < lane_high))
    valid = row_ok & lane_ok
    keep_x = valid & jnp.logical_not((row == 23) & miss_s)
    keep_y = valid & jnp.logical_not((lane == 127) & miss_e)

    block = lax.broadcasted_iota(jnp.int32, (8, 128), 1) // 16
    even = jnp.bitwise_and(block, 1) == 0
    merged = []
    for e_ref, w_ref, base in (
        (from_ne, from_nw, 0), (from_e, from_w, 1), (from_e, from_w, 5), (from_se, from_sw, 2)
    ):
        pairs = []
        for group in range(GROUPS):
            e, w = e_ref[base + group], w_ref[base + group]
            pairs.append((jnp.where(even, e, w), jnp.where(even, w, e)))
        merged.append(pairs)

    def field(slot, mask, fill):
        group, k = slot // 8, slot % 8
        sides = []
        for j in range(4):
            tile = merged[j][group][k % 2]
            sides.append(pltpu.roll(tile, 128 - 16 * k, axis=1) if k else tile)
        if slot < UP:
            mains = [from_n[slot], own[slot], from_s[slot]]
        else:
            mains = [up_n[slot - UP], own_up[slot - UP], up_s[slot - UP]]
            sides = [side.astype(jnp.int32) for side in sides]
        whole = jnp.concatenate(
            [jnp.concatenate(mains, axis=0), jnp.concatenate(sides, axis=0)], axis=1
        )
        return jnp.where(mask, whole, fill)

    L = range(4)
    p0 = [field(P0 + l, valid, 0.0) for l in L]
    s0 = [field(S0 + l, valid, 0.0) for l in L]
    tx = [field(TX + l, keep_x, 0.0) for l in L]
    ty = [field(TY + l, keep_y, 0.0) for l in L]
    tz = [field(TZ + l, valid, 0.0) for l in range(3)]
    pv = [field(PV + l, valid, 1.0) for l in L]
    up = [field(UP + l, valid, 0) for l in L]

    (src0, src1, obs_p0, obs_s0, obs_p1, obs_s1, count), src0_extra = well_grids(
        (ext_n[1], own_list[...], ext_s[4]),
        ((from_ne[4], from_nw[4]), (from_e[0], from_w[0]), (from_se[1], from_sw[1])),
        *[jnp.where(miss, 1, 0) for miss in (miss_n, miss_s, miss_e, miss_w)],
    )
    src, obs_p, obs_s = (src0, src1), (obs_p0, obs_p1), (obs_s0, obs_s1)

    row8 = lax.broadcasted_iota(jnp.int32, (8, 256), 0)

    def first_row(v, extra):
        top = jnp.where(row8 == 0, jnp.concatenate([extra, extra], axis=1), v[0:8])
        return jnp.concatenate([top, v[8:32]], axis=0)

    def last_row(v, extra):
        tail = jnp.where(row8 == 7, jnp.concatenate([extra, extra], axis=1), v[24:32])
        return jnp.concatenate([v[0:24], tail], axis=0)

    edge_n = jnp.where(miss_n, 0.0, ext_n[0])
    txw = [first_row(x_prev(tx[l]), edge_n[4 + l : 5 + l]) for l in L]
    tyw = [y_prev(ty[l]) for l in L]

    def z_sum(faces, values, l):
        total = None
        if l < 3:
            total = faces[l] * values[l + 1]
        if l > 0:
            term = faces[l - 1] * values[l - 1]
            total = term if total is None else total + term
        return total

    ones = [None] * 4
    inv = []
    for l in L:
        den = pv[l] + tx[l] + txw[l] + ty[l] + tyw[l]
        if l < 3:
            den = den + tz[l]
        if l > 0:
            den = den + tz[l - 1]
        inv.append(1.0 / den)

    def gather(values, nexts, prevs):
        out = []
        for l in L:
            total = tx[l] * nexts[l] + txw[l] * prevs[l]
            total = total + ty[l] * y_next(values[l]) + tyw[l] * y_prev(values[l])
            out.append(total + z_sum(tz, values, l))
        return out

    sub8 = lax.broadcasted_iota(jnp.int32, (8, 128), 0)
    cut = lambda t: jnp.where(miss_s, 0.0, t)
    t0 = ext_s[0]
    lane8 = lax.broadcasted_iota(jnp.int32, (8, 128), 1)
    side0 = jnp.where(lane8 < 64, jnp.where(miss_e, 0.0, from_se[0]), jnp.where(miss_w, 0.0, from_sw[0]))
    t0 = jnp.concatenate([cut(t0), cut(side0)], axis=1)
    t0n, t0p = y_next(t0)[:, 0:128], y_prev(t0)[:, 0:128]
    t0 = t0[:, 0:128]
    t1, t2, t3 = cut(ext_s[1]), cut(ext_s[2]), cut(ext_s[3])
    low4 = lambda t: pltpu.roll(t, 4, axis=0)
    ty_x = jnp.where((lane8 == 127) & miss_e, 0.0, low4(t0))
    tyw_x = low4(t0p)
    tx_x, txw_x = low4(t2), t2
    pv_x = jnp.where(miss_s, 1.0, t3)
    tz_x = jnp.where(sub8 < 3, low4(t3), 0.0)
    tzw_x = jnp.where((sub8 >= 1) & (sub8 < 4), pltpu.roll(low4(t3), 1, axis=0), 0.0)
    num_x = (
        pv_x * t0 + src0_extra + tx_x * low4(t1) + txw_x * t1 + ty_x * t0n + tyw_x * t0p
        + tz_x * pltpu.roll(t0, 7, axis=0) + tzw_x * pltpu.roll(t0, 1, axis=0)
    )
    q_extra = num_x / (pv_x + tx_x + txw_x + ty_x + tyw_x + tz_x + tzw_x)

    bits = [[[jnp.bitwise_and(up[l], 1 << (3 * n + d)) != 0 for d in range(3)] for l in L] for n in range(2)]

    ipv = [time_step / pv[l] for l in L]
    saved = []
    p, s = p0, s0
    for n in range(2):
        p_next = [x_next(p[l]) for l in L]
        p_prev = [x_prev(p[l]) for l in L]
        if n == 0:
            p_prev = [first_row(p_prev[l], edge_n[l : l + 1]) for l in L]
        base = [pv[l] * p[l] + src[n][l] for l in L]
        total = gather(p, p_next, p_prev)
        q = [(base[l] + total[l]) * inv[l] for l in L]
        q_next = [x_next(q[l]) for l in L]
        if n == 0:
            q_next = [last_row(q_next[l], q_extra[l : l + 1]) for l in L]
        total = gather(q, q_next, [x_prev(q[l]) for l in L])
        r = [(base[l] + total[l]) * inv[l] for l in L]

        den = []
        mob = []
        for l in L:
            wet = s[l] * s[l]
            dry = 1.0 - s[l]
            scale = 1.0 / (wet + 0.5 * dry * dry)
            den.append(scale)
            mob.append(wet * scale)
        dx = [r[l] - x_next(r[l]) for l in L]
        dy = [r[l] - y_next(r[l]) for l in L]
        dz = [r[l] - r[l + 1] for l in range(3)]
        fx = [jnp.where(bits[n][l][0], mob[l], x_next(mob[l])) for l in L]
        fy = [jnp.where(bits[n][l][1], mob[l], y_next(mob[l])) for l in L]
        fz = [jnp.where(bits[n][l][2], mob[l], mob[l + 1]) for l in range(3)]
        flow_x = [tx[l] * dx[l] * fx[l] for l in L]
        flow_y = [ty[l] * dy[l] * fy[l] for l in L]
        flow_z = [tz[l] * dz[l] * fz[l] for l in range(3)]
        moved = []
        for l in L:
            net = flow_x[l] - x_prev(flow_x[l]) + flow_y[l] - y_prev(flow_y[l])
            if l < 3:
                net = net + flow_z[l]
            if l > 0:
                net = net - flow_z[l - 1]
            moved.append(s[l] - ipv[l] * net)
        saved.append((p, q, r, s, den, dx, dy, dz, fx, fy, fz))
        p, s = r, moved

    grad_x = [None] * 4
    grad_y = [None] * 4
    grad_z = [None] * 3

    def accumulate(total, term):
        return term if total is None else total + term

    carried_p = [count[l] * p[l] - obs_p[1][l] for l in L]
    carried_s = [count[l] * s[l] - obs_s[1][l] for l in L]
    for n in (1, 0):
        p, q, r, s, den, dx, dy, dz, fx, fy, fz = saved[n]
        nu = [ipv[l] * carried_s[l] for l in L]
        mx = [x_next(nu[l]) - nu[l] for l in L]
        my = [y_next(nu[l]) - nu[l] for l in L]
        mz = [nu[l + 1] - nu[l] for l in range(3)]
        for l in L:
            grad_x[l] = accumulate(
                grad_x[l], main_tile(mx[l]) * main_tile(dx[l]) * main_tile(fx[l])
            )
            grad_y[l] = accumulate(
                grad_y[l], main_tile(my[l]) * main_tile(dy[l]) * main_tile(fy[l])
            )
            if l < 3:
                grad_z[l] = accumulate(
                    grad_z[l], main_tile(mz[l]) * main_tile(dz[l]) * main_tile(fz[l])
                )
        gx_ = [mx[l] * tx[l] for l in L]
        gy_ = [my[l] * ty[l] for l in L]
        gz_ = [mz[l] * tz[l] for l in range(3)]
        hx = [gx_[l] * fx[l] for l in L]
        hy = [gy_[l] * fy[l] for l in L]
        hz = [gz_[l] * fz[l] for l in range(3)]
        pi = []
        for l in L:
            total = carried_p[l] + hx[l] - x_prev(hx[l]) + hy[l] - y_prev(hy[l])
            if l < 3:
                total = total + hz[l]
            if l > 0:
                total = total - hz[l - 1]
            pi.append(total)
        if n:
            kx = [gx_[l] * dx[l] for l in L]
            ky = [gy_[l] * dy[l] for l in L]
            kz = [gz_[l] * dz[l] for l in range(3)]
            back_s = []
            for l in L:
                here = jnp.where(bits[n][l][0], kx[l], 0.0)
                there = kx[l] - here
                total = here + x_prev(there)
                here = jnp.where(bits[n][l][1], ky[l], 0.0)
                there = ky[l] - here
                total = total + here + y_prev(there)
                if l < 3:
                    total = total + jnp.where(bits[n][l][2], kz[l], 0.0)
                if l > 0:
                    total = total + jnp.where(bits[n][l - 1][2], 0.0, kz[l - 1])
                slope = (s[l] * den[l]) * ((1.0 - s[l]) * den[l])
                back_s.append(
                    carried_s[l] + slope * total + (count[l] * s[l] - obs_s[0][l])
                )
            carried_s = back_s

        w2 = [pi[l] * inv[l] for l in L]
        w2_next = [x_next(w2[l]) for l in L]
        rho = gather(w2, w2_next, [x_prev(w2[l]) for l in L])
        w1 = [rho[l] * inv[l] for l in L]
        w1_next = [x_next(w1[l]) for l in L]
        m = main_tile
        for l in L:
            a2, a1 = m(w2[l]), m(w1[l])
            rm, qm, pm = m(r[l]), m(q[l]), m(p[l])
            grad_x[l] = (
                grad_x[l]
                + a2 * (m(x_next(q[l])) - rm)
                + m(w2_next[l]) * (qm - m(x_next(r[l])))
                + a1 * (m(x_next(p[l])) - qm)
                + m(w1_next[l]) * (pm - m(x_next(q[l])))
            )
            grad_y[l] = (
                grad_y[l]
                + a2 * (m(y_next(q[l])) - rm)
                + m(y_next(w2[l])) * (qm - m(y_next(r[l])))
                + a1 * (m(y_next(p[l])) - qm)
                + m(y_next(w1[l])) * (pm - m(y_next(q[l])))
            )
            if l < 3:
                grad_z[l] = (
                    grad_z[l]
                    + a2 * (m(q[l + 1]) - rm)
                    + m(w2[l + 1]) * (qm - m(r[l + 1]))
                    + a1 * (m(p[l + 1]) - qm)
                    + m(w1[l + 1]) * (pm - m(q[l + 1]))
                )
        if n:
            back = gather(w1, w1_next, [x_prev(w1[l]) for l in L])
            carried_p = [
                back[l] + pv[l] * (w1[l] + w2[l]) + (count[l] * p[l] - obs_p[0][l]) for l in L
            ]

    for l in L:
        out[l] = jnp.where(main_tile(keep_x), grad_x[l], 0.0)
        out[4 + l] = jnp.where(main_tile(keep_y), grad_y[l], 0.0)
        if l < 3:
            out[8 + l] = grad_z[l]

    for copy, here, origin in sends:
        @pl.when(here)
        def _():
            copy.wait_send()


def adjoint(*args):
    f32, i32 = jnp.float32, jnp.int32
    tiles = lambda n: pltpu.VMEM((n, 8, 128), f32)
    halo = [
        pltpu.VMEM((UP, 16, 128), f32),
        pltpu.VMEM((4, 16, 128), i32),
        pltpu.VMEM((8, 128), f32),
        tiles(UP), tiles(UP),
        pltpu.VMEM((4, 8, 128), i32), pltpu.VMEM((4, 8, 128), i32),
        tiles(2), tiles(5), tiles(9), tiles(9), tiles(5), tiles(5), tiles(6), tiles(6),
    ]
    work = [
        pltpu.VMEM((1, 1, WELLS), i32),
        pltpu.VMEM((1, 1, WELLS), f32),
        pltpu.VMEM((2, 1, 1, WELLS), i32),
        pltpu.VMEM((2, 2, 1, 1, WELLS), f32),
        tiles(2), tiles(5), tiles(11), tiles(11),
    ]
    sems = [pltpu.SemaphoreType.DMA((n,)) for n in (11, 12, 12)]
    return pl.pallas_call(
        adjoint_kernel,
        out_shape=jax.ShapeDtypeStruct((11, 16, 128), f32),
        in_specs=[pl.BlockSpec(memory_space=pl.ANY)] * 11,
        out_specs=pl.BlockSpec(memory_space=pltpu.VMEM),
        scratch_shapes=halo + work + sems,
        compiler_params=pltpu.CompilerParams(collective_id=0, has_side_effects=True),
    )(*args)


def deliver_kernel(stack, out_x, out_y, out_z, sem):
    copies = [
        pltpu.make_async_copy(stack.at[pl.ds(first, n)], out, sem.at[i])
        for i, (first, n, out) in enumerate(((0, 4, out_x), (4, 4, out_y), (8, 3, out_z)))
    ]
    for copy in copies:
        copy.start()
    for copy in copies:
        copy.wait()


def deliver(stack):
    return pl.pallas_call(
        deliver_kernel,
        out_shape=[jax.ShapeDtypeStruct((n, 16, 128), jnp.float32) for n in (4, 4, 3)],
        in_specs=[pl.BlockSpec(memory_space=pl.ANY)],
        out_specs=[pl.BlockSpec(memory_space=pl.ANY)] * 3,
        scratch_shapes=[pltpu.SemaphoreType.DMA((3,))],
    )(stack)


def on_device(*args):
    return tuple(deliver(adjoint(*args)))


def solution(mesh):
    field = P(None, "gx", "gy")
    in_specs = (field,) * 7 + (
        P("gx", "gy", None),
        P("gx", "gy", None),
        P(None, "gx", "gy", None),
        P(None, None, "gx", "gy", None),
    )
    return jax.shard_map(
        on_device, mesh=mesh, in_specs=in_specs, out_specs=(field,) * 3, check_vma=False
    )
```

```python
import jax
import jax.numpy as jnp
from jax import lax
from jax.experimental import pallas as pl
from jax.experimental.pallas import tpu as pltpu
from jax.sharding import PartitionSpec as P

MESH = pl.DeviceIdType.MESH
time_step = 0.05

P0, S0, TX, TY, TZ, PV, UP, SLOTS = 0, 4, 8, 12, 16, 19, 23, 27
GROUPS = 4
WELLS = 64


def start_exchange(args, halo, work, sems):
    p0, s0, tx, ty, tz, pv, up, cell, rate, plan, observed = args
    own, own_up, own_list, from_n, from_s, up_n, up_s, ext_n, ext_s = halo[:9]
    from_e, from_w, from_ne, from_nw, from_se, from_sw = halo[9:]
    cell_v, rate_v, plan_v, obs_v, xtra_n, xtra_s, pack_e, pack_w = work
    in_sem, send_sem, recv_sem, far_sem, near_sem = sems
    gx, gy = lax.axis_index("gx"), lax.axis_index("gy")
    nx, ny = lax.axis_size("gx"), lax.axis_size("gy")
    has_n, has_s = gx > 0, gx < nx - 1
    has_w, has_e = gy > 0, gy < ny - 1
    both = jnp.logical_and
    peers = (
        (has_n, (gx - 1, gy)),
        (has_s, (gx + 1, gy)),
        (has_e, (gx, gy + 1)),
        (has_w, (gx, gy - 1)),
        (both(has_n, has_e), (gx - 1, gy + 1)),
        (both(has_n, has_w), (gx - 1, gy - 1)),
        (both(has_s, has_e), (gx + 1, gy + 1)),
        (both(has_s, has_w), (gx + 1, gy - 1)),
    )
    N, S, E, W, NE, NW, SE, SW = range(8)
    far_s, far_n = gx == nx // 2 - 1, gx == nx // 2
    herald = gx == nx // 2 - 2
    near_s, near_n = jnp.logical_not(far_s), jnp.logical_not(far_n)

    barrier = pltpu.get_barrier_semaphore()
    for at, (here, peer) in enumerate(peers):
        if at in (E, W):
            here = both(here, near_s)
        elif at in (S, SE, SW):
            here = both(here, both(near_s, jnp.logical_not(herald)))

        @pl.when(here)
        def _():
            pl.semaphore_signal(barrier, inc=1, device_id=peer, device_id_type=MESH)

    fields = ((p0, P0, 4), (tx, TX, 4), (ty, TY, 4), (tz, TZ, 3), (pv, PV, 4), (s0, S0, 4))
    loads = [(ref, own.at[pl.ds(slot, n)]) for ref, slot, n in fields]
    loads += [(up, own_up), (cell, cell_v), (rate, rate_v), (plan, plan_v), (observed, obs_v)]
    loads = [pltpu.make_async_copy(a, b, in_sem.at[i]) for i, (a, b) in enumerate(loads)]
    for load in loads:
        load.start()

    rows = jnp.where(both(has_n, near_n), 1, 0) + jnp.where(has_s, 1, 0) + 1
    columns = jnp.where(has_e, 1, 0) + jnp.where(has_w, 1, 0) + 1
    pl.semaphore_wait(barrier, jnp.where(far_s, columns, rows * columns - 1))

    @pl.when(herald)
    def _():
        pl.semaphore_signal(near_sem, inc=1, device_id=(gx + 1, gy), device_id_type=MESH)

    for at in (S, SE, SW):
        here, peer = peers[at]

        @pl.when(both(here, far_s))
        def _():
            pl.semaphore_signal(far_sem, inc=1, device_id=peer, device_id_type=MESH)

    sends = []

    def send(src, dst, to, origin):
        at = len(sends)
        here, peer = peers[to]
        copy = pltpu.make_async_remote_copy(
            src_ref=src, dst_ref=dst, send_sem=send_sem.at[at], recv_sem=recv_sem.at[at],
            device_id=peer, device_id_type=MESH,
        )
        sends.append((copy, to, here, peers[origin][0]))

        if to in (N, NE, NW):
            here = both(here, near_n)

        @pl.when(here)
        def _():
            copy.start()

    for ref, slot, n in fields:
        send(ref.at[:, pl.ds(8, 8), :], from_n.at[pl.ds(slot, n)], S, N)
    send(up.at[:, pl.ds(8, 8), :], up_n, S, N)

    for load in loads:
        load.wait()

    rates = rate_v[0] * 0.5
    rows = [
        cell_v[0].astype(jnp.float32),
        rates * plan_v[0, 0].astype(jnp.float32),
        rates * plan_v[1, 0].astype(jnp.float32),
        obs_v[0, 0, 0],
        obs_v[0, 1, 0],
        obs_v[1, 0, 0],
        obs_v[1, 1, 0],
        jnp.zeros((1, WELLS), jnp.float32),
    ]
    wells = jnp.concatenate(rows, axis=0)
    wells = jnp.concatenate([wells, wells], axis=1)
    own_list[...] = wells

    for layer in range(4):
        xtra_s[0, layer : layer + 1] = own[P0 + layer, 8:9]
        xtra_s[0, 4 + layer : 5 + layer] = own[TY + layer, 8:9]
        xtra_s[1, layer : layer + 1] = own[P0 + layer, 7:8]
        xtra_s[1, 4 + layer : 5 + layer] = own[P0 + layer, 9:10]
        xtra_s[2, layer : layer + 1] = own[TX + layer, 7:8]
        xtra_s[2, 4 + layer : 5 + layer] = own[TX + layer, 8:9]
        xtra_s[3, layer : layer + 1] = own[PV + layer, 8:9]
        if layer < 3:
            xtra_s[3, 4 + layer : 5 + layer] = own[TZ + layer, 8:9]
        xtra_n[0, layer : layer + 1] = own[P0 + layer, 7:8]
        xtra_n[0, 4 + layer : 5 + layer] = own[TX + layer, 7:8]
    xtra_s[3, 7:8] = jnp.zeros((1, 128), jnp.float32)
    xtra_s[4] = wells
    xtra_n[1] = wells

    block = lax.broadcasted_iota(jnp.int32, (8, 128), 1) // 16
    for pack in (pack_e, pack_w):
        pack[0] = xtra_s[0]
        pack[1] = wells
        pack[10] = wells
    for half in range(2):
        for group in range(GROUPS):
            first = second = None
            for k in range(min(8, SLOTS - 8 * group)):
                slot = 8 * group + k
                if slot < UP:
                    tile = own[slot, 8 * half : 8 * half + 8]
                else:
                    tile = own_up[slot - UP, 8 * half : 8 * half + 8].astype(jnp.float32)
                if k:
                    tile = pltpu.roll(tile, 16 * k, axis=1)
                first = tile if first is None else jnp.where(block == k, tile, first)
                second = tile if second is None else jnp.where(block == (k + 7) % 8, tile, second)
            pack_e[2 + 4 * half + group] = first
            pack_w[2 + 4 * half + group] = second

    send(xtra_n, ext_n, S, N)
    send(pack_w.at[pl.ds(6, 5)], from_nw, SE, NW)
    send(pack_e.at[pl.ds(6, 5)], from_ne, SW, NE)

    @pl.when(far_s)
    def _():
        pl.semaphore_wait(near_sem, 1)

    send(pack_w.at[pl.ds(1, 9)], from_w, E, W)
    send(pack_e.at[pl.ds(1, 9)], from_e, W, E)
    send(pack_w.at[pl.ds(0, 6)], from_sw, NE, SW)
    send(pack_e.at[pl.ds(0, 6)], from_se, NW, SE)
    send(xtra_s, ext_s, N, S)
    send(own.at[:, pl.ds(0, 8), :], from_s, N, S)
    send(own_up.at[:, pl.ds(0, 8), :], up_s, N, S)

    @pl.when(far_n)
    def _():
        pl.semaphore_wait(far_sem, columns)

    for copy, to, here, origin in sends:
        if to in (N, NE, NW):
            @pl.when(both(here, far_n))
            def _():
                copy.start()
    return [(copy, here, origin) for copy, to, here, origin in sends]


def x_next(v):
    return pltpu.roll(v, v.shape[0] - 1, axis=0)


def x_prev(v):
    return pltpu.roll(v, 1, axis=0)


def y_next(v):
    return pltpu.roll(v, v.shape[1] - 1, axis=1)


def y_prev(v):
    return pltpu.roll(v, 1, axis=1)


def main_tile(v):
    return v[8:24, 0:128]


def well_grids(lists_main, lists_side, missing_n, missing_s, missing_e, missing_w):
    lane = lax.broadcasted_iota(jnp.int32, (1, 128), 1)
    low = lane < 64
    side = [jnp.where(low, e, w) for e, w in lists_side]

    def ids(cells, drop):
        cells = cells.astype(jnp.int32)
        row = lax.shift_right_logical(cells, 7)
        col = jnp.bitwise_and(cells, 127)
        return row - 1024 * drop, col

    def columns(col):
        at = lax.broadcasted_iota(jnp.int32, (128, 128), 0)
        return jnp.where(at == col, 1.0, 0.0).astype(jnp.bfloat16)

    def split(v):
        hi = v.astype(jnp.bfloat16).astype(jnp.float32)
        mid = (v - hi).astype(jnp.bfloat16).astype(jnp.float32)
        return hi, mid, v - hi - mid

    def product(row, col_hot, value_rows, first, extra):
        count = 32 + (8 if extra else 0)
        at = lax.broadcasted_iota(jnp.int32, (32, 128), 0)
        at = lax.shift_right_logical(at, 3) * 16 + jnp.bitwise_and(at, 7) + first
        hit = row == at
        lhs = []
        for blocks in value_rows:
            lhs.append(
                jnp.concatenate([jnp.where(hit, b, 0.0) for b in blocks], axis=1)
            )
        if extra:
            at = lax.broadcasted_iota(jnp.int32, (8, 128), 0) * 16 + 8
            hit = row == at
            lhs.append(jnp.concatenate([jnp.where(hit, b, 0.0) for b in value_rows[0]], axis=1))
        lhs = jnp.concatenate(lhs, axis=0).astype(jnp.bfloat16)
        rhs = jnp.concatenate([col_hot] * len(value_rows[0]), axis=1)
        return lax.dot_general(
            lhs, rhs, (((1,), (1,)), ((), ())), preferred_element_type=jnp.float32
        )

    zero = jnp.zeros((1, 128), jnp.float32)

    def main_values(tile):
        out = []
        for q in range(1, 7):
            hi, mid, lo = split(tile[q : q + 1])
            out.append([jnp.where(low, hi, mid), jnp.where(low, lo, zero)])
        out.append([jnp.where(low, zero + 1.0, zero), zero])
        return out

    def side_values(tile):
        out = []
        for q in range(1, 7):
            out.append(list(split(tile[q : q + 1])))
        out.append([zero + 1.0, zero, zero])
        return out

    def main_part(tile, drop):
        row, col = ids(tile[0:1], drop)
        return row, columns(col), main_values(tile)

    def side_part(tile, drop):
        row, col = ids(tile[0:1], drop + jnp.where(low, missing_e, missing_w))
        col = jnp.where(low, jnp.where(col < 64, col, -1), jnp.where(col < 64, -1, col))
        return row, columns(col), side_values(tile)

    n, c, s = [main_part(t, d) for t, d in zip(lists_main, (missing_n, 0, missing_s))]
    sn, sc, ss = [side_part(t, d) for t, d in zip(side, (missing_n, 0, missing_s))]
    mains = [
        product(*n, 8, False), product(*c, 0, False), product(*c, 8, False), product(*s, 0, True)
    ]
    sides = [
        product(*sn, 8, False), product(*sc, 0, False), product(*sc, 8, False),
        product(*ss, 0, False),
    ]
    grids = []
    for q in range(7):
        layers = []
        for layer in range(4):
            at = (q * 4 + layer) * 8
            layers.append(
                jnp.concatenate(
                    [
                        jnp.concatenate([m[at : at + 8], d[at : at + 8]], axis=1)
                        for m, d in zip(mains, sides)
                    ],
                    axis=0,
                )
            )
        grids.append(layers)
    return grids, mains[3][224:232]


def adjoint_kernel(*refs):
    args, out = refs[:11], refs[11]
    halo, work, sems = refs[12:27], refs[27:35], refs[35:]
    sends = start_exchange(args, halo, work, sems)
    own, own_up, own_list, from_n, from_s, up_n, up_s, ext_n, ext_s = halo[:9]
    from_e, from_w, from_ne, from_nw, from_se, from_sw = halo[9:]
    for copy, here, origin in sends:
        @pl.when(origin)
        def _():
            copy.wait_recv()

    gx, gy = lax.axis_index("gx"), lax.axis_index("gy")
    nx, ny = lax.axis_size("gx"), lax.axis_size("gy")
    miss_n, miss_s = gx == 0, gx == nx - 1
    miss_w, miss_e = gy == 0, gy == ny - 1
    shape = (32, 256)
    row = lax.broadcasted_iota(jnp.int32, shape, 0)
    lane = lax.broadcasted_iota(jnp.int32, shape, 1)

    row_low = jnp.where(miss_n, 8, 0)
    row_high = jnp.where(miss_s, 24, 32)
    lane_low = jnp.where(miss_e, 192, 128)
    lane_high = jnp.where(miss_w, 192, 256)
    row_ok = (row >= row_low) & (row < row_high)
    lane_ok = (lane < 128) | ((lane >= lane_low) & (lane < lane_high))
    valid = row_ok & lane_ok
    keep_x = valid & jnp.logical_not((row == 23) & miss_s)
    keep_y = valid & jnp.logical_not((lane == 127) & miss_e)

    block = lax.broadcasted_iota(jnp.int32, (8, 128), 1) // 16
    even = jnp.bitwise_and(block, 1) == 0
    merged = []
    for e_ref, w_ref, base in (
        (from_ne, from_nw, 0), (from_e, from_w, 1), (from_e, from_w, 5), (from_se, from_sw, 2)
    ):
        pairs = []
        for group in range(GROUPS):
            e, w = e_ref[base + group], w_ref[base + group]
            pairs.append((jnp.where(even, e, w), jnp.where(even, w, e)))
        merged.append(pairs)

    def field(slot, mask, fill):
        group, k = slot // 8, slot % 8
        sides = []
        for j in range(4):
            tile = merged[j][group][k % 2]
            sides.append(pltpu.roll(tile, 128 - 16 * k, axis=1) if k else tile)
        if slot < UP:
            mains = [from_n[slot], own[slot], from_s[slot]]
        else:
            mains = [up_n[slot - UP], own_up[slot - UP], up_s[slot - UP]]
            sides = [side.astype(jnp.int32) for side in sides]
        whole = jnp.concatenate(
            [jnp.concatenate(mains, axis=0), jnp.concatenate(sides, axis=0)], axis=1
        )
        return jnp.where(mask, whole, fill)

    L = range(4)
    p0 = [field(P0 + l, valid, 0.0) for l in L]
    s0 = [field(S0 + l, valid, 0.0) for l in L]
    tx = [field(TX + l, keep_x, 0.0) for l in L]
    ty = [field(TY + l, keep_y, 0.0) for l in L]
    tz = [field(TZ + l, valid, 0.0) for l in range(3)]
    pv = [field(PV + l, valid, 1.0) for l in L]
    up = [field(UP + l, valid, 0) for l in L]

    (src0, src1, obs_p0, obs_s0, obs_p1, obs_s1, count), src0_extra = well_grids(
        (ext_n[1], own_list[...], ext_s[4]),
        ((from_ne[4], from_nw[4]), (from_e[0], from_w[0]), (from_se[1], from_sw[1])),
        *[jnp.where(miss, 1, 0) for miss in (miss_n, miss_s, miss_e, miss_w)],
    )
    src, obs_p, obs_s = (src0, src1), (obs_p0, obs_p1), (obs_s0, obs_s1)

    row8 = lax.broadcasted_iota(jnp.int32, (8, 256), 0)

    def first_row(v, extra):
        top = jnp.where(row8 == 0, jnp.concatenate([extra, extra], axis=1), v[0:8])
        return jnp.concatenate([top, v[8:32]], axis=0)

    def last_row(v, extra):
        tail = jnp.where(row8 == 7, jnp.concatenate([extra, extra], axis=1), v[24:32])
        return jnp.concatenate([v[0:24], tail], axis=0)

    edge_n = jnp.where(miss_n, 0.0, ext_n[0])
    txw = [first_row(x_prev(tx[l]), edge_n[4 + l : 5 + l]) for l in L]
    tyw = [y_prev(ty[l]) for l in L]

    def z_sum(faces, values, l):
        total = None
        if l < 3:
            total = faces[l] * values[l + 1]
        if l > 0:
            term = faces[l - 1] * values[l - 1]
            total = term if total is None else total + term
        return total

    ones = [None] * 4
    inv = []
    for l in L:
        den = pv[l] + tx[l] + txw[l] + ty[l] + tyw[l]
        if l < 3:
            den = den + tz[l]
        if l > 0:
            den = den + tz[l - 1]
        inv.append(1.0 / den)

    def gather(values, nexts, prevs):
        out = []
        for l in L:
            total = tx[l] * nexts[l] + txw[l] * prevs[l]
            total = total + ty[l] * y_next(values[l]) + tyw[l] * y_prev(values[l])
            out.append(total + z_sum(tz, values, l))
        return out

    sub8 = lax.broadcasted_iota(jnp.int32, (8, 128), 0)
    cut = lambda t: jnp.where(miss_s, 0.0, t)
    t0 = ext_s[0]
    lane8 = lax.broadcasted_iota(jnp.int32, (8, 128), 1)
    side0 = jnp.where(lane8 < 64, jnp.where(miss_e, 0.0, from_se[0]), jnp.where(miss_w, 0.0, from_sw[0]))
    t0 = jnp.concatenate([cut(t0), cut(side0)], axis=1)
    t0n, t0p = y_next(t0)[:, 0:128], y_prev(t0)[:, 0:128]
    t0 = t0[:, 0:128]
    t1, t2, t3 = cut(ext_s[1]), cut(ext_s[2]), cut(ext_s[3])
    low4 = lambda t: pltpu.roll(t, 4, axis=0)
    ty_x = jnp.where((lane8 == 127) & miss_e, 0.0, low4(t0))
    tyw_x = low4(t0p)
    tx_x, txw_x = low4(t2), t2
    pv_x = jnp.where(miss_s, 1.0, t3)
    tz_x = jnp.where(sub8 < 3, low4(t3), 0.0)
    tzw_x = jnp.where((sub8 >= 1) & (sub8 < 4), pltpu.roll(low4(t3), 1, axis=0), 0.0)
    num_x = (
        pv_x * t0 + src0_extra + tx_x * low4(t1) + txw_x * t1 + ty_x * t0n + tyw_x * t0p
        + tz_x * pltpu.roll(t0, 7, axis=0) + tzw_x * pltpu.roll(t0, 1, axis=0)
    )
    q_extra = num_x / (pv_x + tx_x + txw_x + ty_x + tyw_x + tz_x + tzw_x)

    bits = [[[jnp.bitwise_and(up[l], 1 << (3 * n + d)) != 0 for d in range(3)] for l in L] for n in range(2)]

    ipv = [time_step / pv[l] for l in L]
    saved = []
    p, s = p0, s0
    for n in range(2):
        p_next = [x_next(p[l]) for l in L]
        p_prev = [x_prev(p[l]) for l in L]
        if n == 0:
            p_prev = [first_row(p_prev[l], edge_n[l : l + 1]) for l in L]
        base = [pv[l] * p[l] + src[n][l] for l in L]
        total = gather(p, p_next, p_prev)
        q = [(base[l] + total[l]) * inv[l] for l in L]
        q_next = [x_next(q[l]) for l in L]
        if n == 0:
            q_next = [last_row(q_next[l], q_extra[l : l + 1]) for l in L]
        total = gather(q, q_next, [x_prev(q[l]) for l in L])
        r = [(base[l] + total[l]) * inv[l] for l in L]

        den = []
        mob = []
        for l in L:
            wet = s[l] * s[l]
            dry = 1.0 - s[l]
            scale = 1.0 / (wet + 0.5 * dry * dry)
            den.append(scale)
            mob.append(wet * scale)
        dx = [r[l] - x_next(r[l]) for l in L]
        dy = [r[l] - y_next(r[l]) for l in L]
        dz = [r[l] - r[l + 1] for l in range(3)]
        fx = [jnp.where(bits[n][l][0], mob[l], x_next(mob[l])) for l in L]
        fy = [jnp.where(bits[n][l][1], mob[l], y_next(mob[l])) for l in L]
        fz = [jnp.where(bits[n][l][2], mob[l], mob[l + 1]) for l in range(3)]
        flow_x = [tx[l] * dx[l] * fx[l] for l in L]
        flow_y = [ty[l] * dy[l] * fy[l] for l in L]
        flow_z = [tz[l] * dz[l] * fz[l] for l in range(3)]
        moved = []
        for l in L:
            net = flow_x[l] - x_prev(flow_x[l]) + flow_y[l] - y_prev(flow_y[l])
            if l < 3:
                net = net + flow_z[l]
            if l > 0:
                net = net - flow_z[l - 1]
            moved.append(s[l] - ipv[l] * net)
        saved.append((p, q, r, s, den, dx, dy, dz, fx, fy, fz))
        p, s = r, moved

    grad_x = [None] * 4
    grad_y = [None] * 4
    grad_z = [None] * 3

    def accumulate(total, term):
        return term if total is None else total + term

    carried_p = [count[l] * p[l] - obs_p[1][l] for l in L]
    carried_s = [count[l] * s[l] - obs_s[1][l] for l in L]
    for n in (1, 0):
        p, q, r, s, den, dx, dy, dz, fx, fy, fz = saved[n]
        nu = [ipv[l] * carried_s[l] for l in L]
        mx = [x_next(nu[l]) - nu[l] for l in L]
        my = [y_next(nu[l]) - nu[l] for l in L]
        mz = [nu[l + 1] - nu[l] for l in range(3)]
        for l in L:
            grad_x[l] = accumulate(
                grad_x[l], main_tile(mx[l]) * main_tile(dx[l]) * main_tile(fx[l])
            )
            grad_y[l] = accumulate(
                grad_y[l], main_tile(my[l]) * main_tile(dy[l]) * main_tile(fy[l])
            )
            if l < 3:
                grad_z[l] = accumulate(
                    grad_z[l], main_tile(mz[l]) * main_tile(dz[l]) * main_tile(fz[l])
                )
        gx_ = [mx[l] * tx[l] for l in L]
        gy_ = [my[l] * ty[l] for l in L]
        gz_ = [mz[l] * tz[l] for l in range(3)]
        hx = [gx_[l] * fx[l] for l in L]
        hy = [gy_[l] * fy[l] for l in L]
        hz = [gz_[l] * fz[l] for l in range(3)]
        pi = []
        for l in L:
            total = carried_p[l] + hx[l] - x_prev(hx[l]) + hy[l] - y_prev(hy[l])
            if l < 3:
                total = total + hz[l]
            if l > 0:
                total = total - hz[l - 1]
            pi.append(total)
        if n:
            kx = [gx_[l] * dx[l] for l in L]
            ky = [gy_[l] * dy[l] for l in L]
            kz = [gz_[l] * dz[l] for l in range(3)]
            back_s = []
            for l in L:
                here = jnp.where(bits[n][l][0], kx[l], 0.0)
                there = kx[l] - here
                total = here + x_prev(there)
                here = jnp.where(bits[n][l][1], ky[l], 0.0)
                there = ky[l] - here
                total = total + here + y_prev(there)
                if l < 3:
                    total = total + jnp.where(bits[n][l][2], kz[l], 0.0)
                if l > 0:
                    total = total + jnp.where(bits[n][l - 1][2], 0.0, kz[l - 1])
                slope = (s[l] * den[l]) * ((1.0 - s[l]) * den[l])
                back_s.append(
                    carried_s[l] + slope * total + (count[l] * s[l] - obs_s[0][l])
                )
            carried_s = back_s

        w2 = [pi[l] * inv[l] for l in L]
        w2_next = [x_next(w2[l]) for l in L]
        rho = gather(w2, w2_next, [x_prev(w2[l]) for l in L])
        w1 = [rho[l] * inv[l] for l in L]
        w1_next = [x_next(w1[l]) for l in L]
        m = main_tile
        for l in L:
            a2, a1 = m(w2[l]), m(w1[l])
            rm, qm, pm = m(r[l]), m(q[l]), m(p[l])
            grad_x[l] = (
                grad_x[l]
                + a2 * (m(x_next(q[l])) - rm)
                + m(w2_next[l]) * (qm - m(x_next(r[l])))
                + a1 * (m(x_next(p[l])) - qm)
                + m(w1_next[l]) * (pm - m(x_next(q[l])))
            )
            grad_y[l] = (
                grad_y[l]
                + a2 * (m(y_next(q[l])) - rm)
                + m(y_next(w2[l])) * (qm - m(y_next(r[l])))
                + a1 * (m(y_next(p[l])) - qm)
                + m(y_next(w1[l])) * (pm - m(y_next(q[l])))
            )
            if l < 3:
                grad_z[l] = (
                    grad_z[l]
                    + a2 * (m(q[l + 1]) - rm)
                    + m(w2[l + 1]) * (qm - m(r[l + 1]))
                    + a1 * (m(p[l + 1]) - qm)
                    + m(w1[l + 1]) * (pm - m(q[l + 1]))
                )
        if n:
            back = gather(w1, w1_next, [x_prev(w1[l]) for l in L])
            carried_p = [
                back[l] + pv[l] * (w1[l] + w2[l]) + (count[l] * p[l] - obs_p[0][l]) for l in L
            ]

    for l in L:
        out[l] = jnp.where(main_tile(keep_x), grad_x[l], 0.0)
        out[4 + l] = jnp.where(main_tile(keep_y), grad_y[l], 0.0)
        if l < 3:
            out[8 + l] = grad_z[l]

    for copy, here, origin in sends:
        @pl.when(here)
        def _():
            copy.wait_send()


def adjoint(*args):
    f32, i32 = jnp.float32, jnp.int32
    tiles = lambda n: pltpu.VMEM((n, 8, 128), f32)
    halo = [
        pltpu.VMEM((UP, 16, 128), f32),
        pltpu.VMEM((4, 16, 128), i32),
        pltpu.VMEM((8, 128), f32),
        tiles(UP), tiles(UP),
        pltpu.VMEM((4, 8, 128), i32), pltpu.VMEM((4, 8, 128), i32),
        tiles(2), tiles(5), tiles(9), tiles(9), tiles(5), tiles(5), tiles(6), tiles(6),
    ]
    work = [
        pltpu.VMEM((1, 1, WELLS), i32),
        pltpu.VMEM((1, 1, WELLS), f32),
        pltpu.VMEM((2, 1, 1, WELLS), i32),
        pltpu.VMEM((2, 2, 1, 1, WELLS), f32),
        tiles(2), tiles(5), tiles(11), tiles(11),
    ]
    sems = [pltpu.SemaphoreType.DMA((n,)) for n in (11, 17, 17)] + [pltpu.SemaphoreType.REGULAR] * 2
    return pl.pallas_call(
        adjoint_kernel,
        out_shape=pltpu.VMEM((11, 16, 128), f32),
        in_specs=[pl.BlockSpec(memory_space=pl.ANY)] * 11,
        out_specs=pl.BlockSpec(memory_space=pltpu.VMEM),
        scratch_shapes=halo + work + sems,
        compiler_params=pltpu.CompilerParams(collective_id=0, has_side_effects=True),
    )(*args)


def deliver_kernel(stack, out_x, out_y, out_z, sem):
    copies = [
        pltpu.make_async_copy(stack.at[pl.ds(first, n)], out, sem.at[i])
        for i, (first, n, out) in enumerate(((0, 4, out_x), (4, 4, out_y), (8, 3, out_z)))
    ]
    for copy in copies:
        copy.start()
    for copy in copies:
        copy.wait()


def deliver(stack):
    return pl.pallas_call(
        deliver_kernel,
        out_shape=[jax.ShapeDtypeStruct((n, 16, 128), jnp.float32) for n in (4, 4, 3)],
        in_specs=[pl.BlockSpec(memory_space=pltpu.VMEM)],
        out_specs=[pl.BlockSpec(memory_space=pl.ANY)] * 3,
        scratch_shapes=[pltpu.SemaphoreType.DMA((3,))],
    )(pltpu.with_memory_space_constraint(stack, pltpu.VMEM))


def on_device(*args):
    return tuple(deliver(adjoint(*args)))


def solution(mesh):
    field = P(None, "gx", "gy")
    in_specs = (field,) * 7 + (
        P("gx", "gy", None),
        P("gx", "gy", None),
        P(None, "gx", "gy", None),
        P(None, None, "gx", "gy", None),
    )
    return jax.shard_map(
        on_device, mesh=mesh, in_specs=in_specs, out_specs=(field,) * 3, check_vma=False
    )
```

```python
import jax
import jax.numpy as jnp
from jax import lax
from jax.experimental import pallas as pl
from jax.experimental.pallas import tpu as pltpu
from jax.sharding import PartitionSpec as P

MESH = pl.DeviceIdType.MESH
time_step = 0.05

P0, TX, TY, TZ, PV, S0, UP, SLOTS = 0, 4, 8, 12, 15, 19, 23, 27
GROUPS = 4
WELLS = 64


def start_exchange(args, halo, work, sems):
    p0, s0, tx, ty, tz, pv, up, cell, rate, plan, observed = args
    own, own_up, own_list, from_n, from_s, up_n, up_s, ext_n, ext_s = halo[:9]
    from_e, from_w, from_ne, from_nw, from_se, from_sw = halo[9:]
    cell_v, rate_v, plan_v, obs_v, xtra_n, xtra_s, pack_e, pack_w = work
    in_sem, send_sem, recv_sem, far_sem, near_sem = sems
    gx, gy = lax.axis_index("gx"), lax.axis_index("gy")
    nx, ny = lax.axis_size("gx"), lax.axis_size("gy")
    has_n, has_s = gx > 0, gx < nx - 1
    has_w, has_e = gy > 0, gy < ny - 1
    both = jnp.logical_and
    peers = (
        (has_n, (gx - 1, gy)),
        (has_s, (gx + 1, gy)),
        (has_e, (gx, gy + 1)),
        (has_w, (gx, gy - 1)),
        (both(has_n, has_e), (gx - 1, gy + 1)),
        (both(has_n, has_w), (gx - 1, gy - 1)),
        (both(has_s, has_e), (gx + 1, gy + 1)),
        (both(has_s, has_w), (gx + 1, gy - 1)),
    )
    N, S, E, W, NE, NW, SE, SW = range(8)
    far_s, far_n = gx == nx // 2 - 1, gx == nx // 2
    herald = gx == nx // 2 - 2
    near_s, near_n = jnp.logical_not(far_s), jnp.logical_not(far_n)
    yields = both(far_s, gy < ny // 4)

    fields = ((p0, P0, 4), (tx, TX, 4), (ty, TY, 4), (tz, TZ, 3), (pv, PV, 4), (s0, S0, 4))
    loads = [(ref, own.at[pl.ds(slot, n)]) for ref, slot, n in fields]
    loads += [(up, own_up), (cell, cell_v), (rate, rate_v), (plan, plan_v), (observed, obs_v)]
    loads = [pltpu.make_async_copy(a, b, in_sem.at[i]) for i, (a, b) in enumerate(loads)]
    for load in loads:
        load.start()

    barrier = pltpu.get_barrier_semaphore()
    for at, (here, peer) in enumerate(peers):
        if at in (E, W):
            here = both(here, near_s)
        elif at in (S, SE, SW):
            here = both(here, both(near_s, jnp.logical_not(herald)))

        @pl.when(here)
        def _():
            pl.semaphore_signal(barrier, inc=1, device_id=peer, device_id_type=MESH)

    rows = jnp.where(both(has_n, near_n), 1, 0) + jnp.where(has_s, 1, 0) + 1
    columns = jnp.where(has_e, 1, 0) + jnp.where(has_w, 1, 0) + 1
    pl.semaphore_wait(barrier, jnp.where(far_s, columns, rows * columns - 1))

    @pl.when(herald)
    def _():
        pl.semaphore_signal(near_sem, inc=1, device_id=(gx + 1, gy), device_id_type=MESH)

    for at, slot in ((S, N), (SE, NW), (SW, NE)):
        here, peer = peers[at]

        @pl.when(both(here, far_s))
        def _():
            pl.semaphore_signal(
                far_sem.at[slot], inc=1, device_id=peer, device_id_type=MESH
            )

    sends = []

    def send(src, dst, to, origin, late=False):
        at = len(sends)
        here, peer = peers[to]
        copy = pltpu.make_async_remote_copy(
            src_ref=src, dst_ref=dst, send_sem=send_sem.at[at], recv_sem=recv_sem.at[at],
            device_id=peer, device_id_type=MESH,
        )
        group = 2 if late else 0 if to in (E, W) else 1
        sends.append((copy, to, here, peers[origin][0], group))

        if to in (N, NE, NW):
            here = both(here, near_n)
        if to == S and len(sends) <= 5:
            here = both(here, jnp.logical_not(yields))

        @pl.when(here)
        def _():
            copy.start()

    for ref, slot, n in fields[:5]:
        send(ref.at[:, pl.ds(8, 8), :], from_n.at[pl.ds(slot, n)], S, N)

    for load in loads[:7]:
        load.wait()

    block = lax.broadcasted_iota(jnp.int32, (8, 128), 1) // 16

    def pack_half(half):
        for group in range(GROUPS):
            first = second = None
            for k in range(min(8, SLOTS - 8 * group)):
                slot = 8 * group + k
                if slot < UP:
                    tile = own[slot, 8 * half : 8 * half + 8]
                else:
                    tile = own_up[slot - UP, 8 * half : 8 * half + 8].astype(jnp.float32)
                if k:
                    tile = pltpu.roll(tile, 16 * k, axis=1)
                first = tile if first is None else jnp.where(block == k, tile, first)
                second = tile if second is None else jnp.where(block == (k + 7) % 8, tile, second)
            pack_e[2 + 4 * half + group] = first
            pack_w[2 + 4 * half + group] = second

    pack_half(1)
    for load in loads[7:]:
        load.wait()
    rates = rate_v[0] * 0.5
    rows = [
        cell_v[0].astype(jnp.float32),
        rates * plan_v[0, 0].astype(jnp.float32),
        rates * plan_v[1, 0].astype(jnp.float32),
        obs_v[0, 0, 0],
        obs_v[0, 1, 0],
        obs_v[1, 0, 0],
        obs_v[1, 1, 0],
        jnp.zeros((1, WELLS), jnp.float32),
    ]
    wells = jnp.concatenate(rows, axis=0)
    wells = jnp.concatenate([wells, wells], axis=1)
    own_list[...] = wells
    pack_e[10] = wells
    pack_w[10] = wells
    send(pack_w.at[pl.ds(6, 5)], from_nw, SE, NW)
    send(pack_e.at[pl.ds(6, 5)], from_ne, SW, NE)

    for layer in range(4):
        xtra_n[0, layer : layer + 1] = own[P0 + layer, 7:8]
        xtra_n[0, 4 + layer : 5 + layer] = own[TX + layer, 7:8]
    xtra_n[1] = wells
    send(xtra_n, ext_n, S, N)
    send(own.at[pl.ds(S0, 4), pl.ds(8, 8), :], from_n.at[pl.ds(S0, 4)], S, N, True)
    send(own_up.at[:, pl.ds(8, 8), :], up_n, S, N, True)

    for layer in range(4):
        xtra_s[0, layer : layer + 1] = own[P0 + layer, 8:9]
        xtra_s[0, 4 + layer : 5 + layer] = own[TY + layer, 8:9]
        xtra_s[1, layer : layer + 1] = own[P0 + layer, 7:8]
        xtra_s[1, 4 + layer : 5 + layer] = own[P0 + layer, 9:10]
        xtra_s[2, layer : layer + 1] = own[TX + layer, 7:8]
        xtra_s[2, 4 + layer : 5 + layer] = own[TX + layer, 8:9]
        xtra_s[3, layer : layer + 1] = own[PV + layer, 8:9]
        if layer < 3:
            xtra_s[3, 4 + layer : 5 + layer] = own[TZ + layer, 8:9]
    xtra_s[3, 7:8] = jnp.zeros((1, 128), jnp.float32)
    xtra_s[4] = wells
    for pack in (pack_e, pack_w):
        pack[0] = xtra_s[0]
        pack[1] = wells
    pack_half(0)

    @pl.when(far_s)
    def _():
        pl.semaphore_wait(near_sem, 1)

    send(pack_w.at[pl.ds(1, 9)], from_w, E, W)
    send(pack_e.at[pl.ds(1, 9)], from_e, W, E)
    send(pack_w.at[pl.ds(0, 6)], from_sw, NE, SW)
    send(pack_e.at[pl.ds(0, 6)], from_se, NW, SE)
    send(xtra_s, ext_s, N, S)
    send(own.at[pl.ds(0, S0), pl.ds(0, 8), :], from_s.at[pl.ds(0, S0)], N, S)
    send(own.at[pl.ds(S0, 4), pl.ds(0, 8), :], from_s.at[pl.ds(S0, 4)], N, S, True)
    send(own_up.at[:, pl.ds(0, 8), :], up_s, N, S, True)

    for at in (N, NE, NW):
        @pl.when(both(peers[at][0], far_n))
        def _():
            pl.semaphore_wait(far_sem.at[at], 1)

    for copy, to, here, origin, group in sends:
        if to in (N, NE, NW):
            @pl.when(both(here, far_n))
            def _():
                copy.start()

    for copy, to, here, origin, group in sends:
        if group == 0:
            @pl.when(both(yields, here))
            def _():
                copy.wait_send()

    @pl.when(yields)
    def _():
        for copy, *_ in sends[:5]:
            copy.start()

    return [(copy, both(here, jnp.logical_not(yields)) if group == 0 else here, origin, group) for copy, to, here, origin, group in sends]


def x_next(v):
    return pltpu.roll(v, v.shape[0] - 1, axis=0)


def x_prev(v):
    return pltpu.roll(v, 1, axis=0)


def y_next(v):
    return pltpu.roll(v, v.shape[1] - 1, axis=1)


def y_prev(v):
    return pltpu.roll(v, 1, axis=1)


def main_tile(v):
    return v[8:24, 0:128]


def well_grids(lists_main, lists_side, missing_n, missing_s, missing_e, missing_w, arrive):
    lane = lax.broadcasted_iota(jnp.int32, (1, 128), 1)
    low = lane < 64

    def ids(cells, drop):
        cells = cells.astype(jnp.int32)
        row = lax.shift_right_logical(cells, 7)
        col = jnp.bitwise_and(cells, 127)
        return row - 1024 * drop, col

    def columns(col):
        at = lax.broadcasted_iota(jnp.int32, (128, 128), 0)
        return jnp.where(at == col, 1.0, 0.0).astype(jnp.bfloat16)

    def split(v):
        hi = v.astype(jnp.bfloat16).astype(jnp.float32)
        mid = (v - hi).astype(jnp.bfloat16).astype(jnp.float32)
        return hi, mid, v - hi - mid

    def product(row, col_hot, value_rows, first, extra):
        count = 32 + (8 if extra else 0)
        at = lax.broadcasted_iota(jnp.int32, (32, 128), 0)
        at = lax.shift_right_logical(at, 3) * 16 + jnp.bitwise_and(at, 7) + first
        hit = row == at
        lhs = []
        for blocks in value_rows:
            lhs.append(
                jnp.concatenate([jnp.where(hit, b, 0.0) for b in blocks], axis=1)
            )
        if extra:
            at = lax.broadcasted_iota(jnp.int32, (8, 128), 0) * 16 + 8
            hit = row == at
            lhs.append(jnp.concatenate([jnp.where(hit, b, 0.0) for b in value_rows[0]], axis=1))
        lhs = jnp.concatenate(lhs, axis=0).astype(jnp.bfloat16)
        rhs = jnp.concatenate([col_hot] * len(value_rows[0]), axis=1)
        return lax.dot_general(
            lhs, rhs, (((1,), (1,)), ((), ())), preferred_element_type=jnp.float32
        )

    zero = jnp.zeros((1, 128), jnp.float32)

    def main_values(tile):
        out = []
        for q in range(1, 7):
            hi, mid, lo = split(tile[q : q + 1])
            out.append([jnp.where(low, hi, mid), jnp.where(low, lo, zero)])
        out.append([jnp.where(low, zero + 1.0, zero), zero])
        return out

    def side_values(tile):
        out = []
        for q in range(1, 7):
            out.append(list(split(tile[q : q + 1])))
        out.append([zero + 1.0, zero, zero])
        return out

    def main_part(tile, drop):
        row, col = ids(tile[0:1], drop)
        return row, columns(col), main_values(tile)

    def side_part(tile, drop):
        row, col = ids(tile[0:1], drop + jnp.where(low, missing_e, missing_w))
        col = jnp.where(low, jnp.where(col < 64, col, -1), jnp.where(col < 64, -1, col))
        return row, columns(col), side_values(tile)

    def both_parts(at, drop):
        e, w = lists_side[at]()
        return (
            main_part(lists_main[at](), drop),
            side_part(jnp.where(low, e, w), drop),
        )

    c, sc = both_parts(1, 0)
    middle = [product(*part, first, False) for part in (c, sc) for first in (0, 8)]
    arrive()
    n, sn = both_parts(0, missing_n)
    s, ss = both_parts(2, missing_s)
    mains = [product(*n, 8, False), middle[0], middle[1], product(*s, 0, True)]
    sides = [product(*sn, 8, False), middle[2], middle[3], product(*ss, 0, False)]
    grids = []
    for q in range(7):
        layers = []
        for layer in range(4):
            at = (q * 4 + layer) * 8
            layers.append(
                jnp.concatenate(
                    [
                        jnp.concatenate([m[at : at + 8], d[at : at + 8]], axis=1)
                        for m, d in zip(mains, sides)
                    ],
                    axis=0,
                )
            )
        grids.append(layers)
    return grids, mains[3][224:232]


def adjoint_kernel(*refs):
    args, out = refs[:11], refs[11]
    halo, work, sems = refs[12:27], refs[27:35], refs[35:]
    sends = start_exchange(args, halo, work, sems)
    own, own_up, own_list, from_n, from_s, up_n, up_s, ext_n, ext_s = halo[:9]
    from_e, from_w, from_ne, from_nw, from_se, from_sw = halo[9:]

    def receive(which):
        for copy, here, origin, group in sends:
            if group == which:
                @pl.when(origin)
                def _():
                    copy.wait_recv()

    receive(0)
    gx, gy = lax.axis_index("gx"), lax.axis_index("gy")
    nx, ny = lax.axis_size("gx"), lax.axis_size("gy")
    miss_n, miss_s = gx == 0, gx == nx - 1
    miss_w, miss_e = gy == 0, gy == ny - 1
    shape = (32, 256)
    row = lax.broadcasted_iota(jnp.int32, shape, 0)
    lane = lax.broadcasted_iota(jnp.int32, shape, 1)

    row_low = jnp.where(miss_n, 8, 0)
    row_high = jnp.where(miss_s, 24, 32)
    lane_low = jnp.where(miss_e, 192, 128)
    lane_high = jnp.where(miss_w, 192, 256)
    row_ok = (row >= row_low) & (row < row_high)
    lane_ok = (lane < 128) | ((lane >= lane_low) & (lane < lane_high))
    valid = row_ok & lane_ok
    keep_x = valid & jnp.logical_not((row == 23) & miss_s)
    keep_y = valid & jnp.logical_not((lane == 127) & miss_e)

    (src0, src1, obs_p0, obs_s0, obs_p1, obs_s1, count), src0_extra = well_grids(
        (lambda: ext_n[1], lambda: own_list[...], lambda: ext_s[4]),
        (
            lambda: (from_ne[4], from_nw[4]),
            lambda: (from_e[0], from_w[0]),
            lambda: (from_se[1], from_sw[1]),
        ),
        *[jnp.where(miss, 1, 0) for miss in (miss_n, miss_s, miss_e, miss_w)],
        lambda: receive(1),
    )

    block = lax.broadcasted_iota(jnp.int32, (8, 128), 1) // 16
    even = jnp.bitwise_and(block, 1) == 0
    merged = []
    for e_ref, w_ref, base in (
        (from_ne, from_nw, 0), (from_e, from_w, 1), (from_e, from_w, 5), (from_se, from_sw, 2)
    ):
        pairs = []
        for group in range(GROUPS):
            e, w = e_ref[base + group], w_ref[base + group]
            pairs.append((jnp.where(even, e, w), jnp.where(even, w, e)))
        merged.append(pairs)

    def field(slot, mask, fill):
        group, k = slot // 8, slot % 8
        sides = []
        for j in range(4):
            tile = merged[j][group][k % 2]
            sides.append(pltpu.roll(tile, 128 - 16 * k, axis=1) if k else tile)
        if slot < UP:
            mains = [from_n[slot], own[slot], from_s[slot]]
        else:
            mains = [up_n[slot - UP], own_up[slot - UP], up_s[slot - UP]]
            sides = [side.astype(jnp.int32) for side in sides]
        whole = jnp.concatenate(
            [jnp.concatenate(mains, axis=0), jnp.concatenate(sides, axis=0)], axis=1
        )
        return jnp.where(mask, whole, fill)

    L = range(4)
    p0 = [field(P0 + l, valid, 0.0) for l in L]
    tx = [field(TX + l, keep_x, 0.0) for l in L]
    ty = [field(TY + l, keep_y, 0.0) for l in L]
    tz = [field(TZ + l, valid, 0.0) for l in range(3)]
    pv = [field(PV + l, valid, 1.0) for l in L]

    src, obs_p, obs_s = (src0, src1), (obs_p0, obs_p1), (obs_s0, obs_s1)

    row8 = lax.broadcasted_iota(jnp.int32, (8, 256), 0)

    def first_row(v, extra):
        top = jnp.where(row8 == 0, jnp.concatenate([extra, extra], axis=1), v[0:8])
        return jnp.concatenate([top, v[8:32]], axis=0)

    def last_row(v, extra):
        tail = jnp.where(row8 == 7, jnp.concatenate([extra, extra], axis=1), v[24:32])
        return jnp.concatenate([v[0:24], tail], axis=0)

    edge_n = jnp.where(miss_n, 0.0, ext_n[0])
    txw = [first_row(x_prev(tx[l]), edge_n[4 + l : 5 + l]) for l in L]
    tyw = [y_prev(ty[l]) for l in L]

    def z_sum(faces, values, l):
        total = None
        if l < 3:
            total = faces[l] * values[l + 1]
        if l > 0:
            term = faces[l - 1] * values[l - 1]
            total = term if total is None else total + term
        return total

    ones = [None] * 4
    inv = []
    for l in L:
        den = pv[l] + tx[l] + txw[l] + ty[l] + tyw[l]
        if l < 3:
            den = den + tz[l]
        if l > 0:
            den = den + tz[l - 1]
        inv.append(1.0 / den)

    def gather(values, nexts, prevs):
        out = []
        for l in L:
            total = tx[l] * nexts[l] + txw[l] * prevs[l]
            total = total + ty[l] * y_next(values[l]) + tyw[l] * y_prev(values[l])
            out.append(total + z_sum(tz, values, l))
        return out

    sub8 = lax.broadcasted_iota(jnp.int32, (8, 128), 0)
    cut = lambda t: jnp.where(miss_s, 0.0, t)
    t0 = ext_s[0]
    lane8 = lax.broadcasted_iota(jnp.int32, (8, 128), 1)
    side0 = jnp.where(lane8 < 64, jnp.where(miss_e, 0.0, from_se[0]), jnp.where(miss_w, 0.0, from_sw[0]))
    t0 = jnp.concatenate([cut(t0), cut(side0)], axis=1)
    t0n, t0p = y_next(t0)[:, 0:128], y_prev(t0)[:, 0:128]
    t0 = t0[:, 0:128]
    t1, t2, t3 = cut(ext_s[1]), cut(ext_s[2]), cut(ext_s[3])
    low4 = lambda t: pltpu.roll(t, 4, axis=0)
    ty_x = jnp.where((lane8 == 127) & miss_e, 0.0, low4(t0))
    tyw_x = low4(t0p)
    tx_x, txw_x = low4(t2), t2
    pv_x = jnp.where(miss_s, 1.0, t3)
    tz_x = jnp.where(sub8 < 3, low4(t3), 0.0)
    tzw_x = jnp.where((sub8 >= 1) & (sub8 < 4), pltpu.roll(low4(t3), 1, axis=0), 0.0)
    num_x = (
        pv_x * t0 + src0_extra + tx_x * low4(t1) + txw_x * t1 + ty_x * t0n + tyw_x * t0p
        + tz_x * pltpu.roll(t0, 7, axis=0) + tzw_x * pltpu.roll(t0, 1, axis=0)
    )
    q_extra = num_x / (pv_x + tx_x + txw_x + ty_x + tyw_x + tz_x + tzw_x)

    ipv = [time_step / pv[l] for l in L]
    saved = []
    p = p0
    for n in range(2):
        p_next = [x_next(p[l]) for l in L]
        p_prev = [x_prev(p[l]) for l in L]
        if n == 0:
            p_prev = [first_row(p_prev[l], edge_n[l : l + 1]) for l in L]
        base = [pv[l] * p[l] + src[n][l] for l in L]
        total = gather(p, p_next, p_prev)
        q = [(base[l] + total[l]) * inv[l] for l in L]
        q_next = [x_next(q[l]) for l in L]
        if n == 0:
            q_next = [last_row(q_next[l], q_extra[l : l + 1]) for l in L]
        total = gather(q, q_next, [x_prev(q[l]) for l in L])
        r = [(base[l] + total[l]) * inv[l] for l in L]

        if n == 0:
            receive(2)
            s = [field(S0 + l, valid, 0.0) for l in L]
            up = [field(UP + l, valid, 0) for l in L]
            bits = [[[jnp.bitwise_and(up[l], 1 << (3 * n + d)) != 0 for d in range(3)] for l in L] for n in range(2)]

        den = []
        mob = []
        for l in L:
            wet = s[l] * s[l]
            dry = 1.0 - s[l]
            scale = 1.0 / (wet + 0.5 * dry * dry)
            den.append(scale)
            mob.append(wet * scale)
        dx = [r[l] - x_next(r[l]) for l in L]
        dy = [r[l] - y_next(r[l]) for l in L]
        dz = [r[l] - r[l + 1] for l in range(3)]
        fx = [jnp.where(bits[n][l][0], mob[l], x_next(mob[l])) for l in L]
        fy = [jnp.where(bits[n][l][1], mob[l], y_next(mob[l])) for l in L]
        fz = [jnp.where(bits[n][l][2], mob[l], mob[l + 1]) for l in range(3)]
        flow_x = [tx[l] * dx[l] * fx[l] for l in L]
        flow_y = [ty[l] * dy[l] * fy[l] for l in L]
        flow_z = [tz[l] * dz[l] * fz[l] for l in range(3)]
        moved = []
        for l in L:
            net = flow_x[l] - x_prev(flow_x[l]) + flow_y[l] - y_prev(flow_y[l])
            if l < 3:
                net = net + flow_z[l]
            if l > 0:
                net = net - flow_z[l - 1]
            moved.append(s[l] - ipv[l] * net)
        saved.append((p, q, r, s, den, dx, dy, dz, fx, fy, fz))
        p, s = r, moved

    grad_x = [None] * 4
    grad_y = [None] * 4
    grad_z = [None] * 3

    def accumulate(total, term):
        return term if total is None else total + term

    carried_p = [count[l] * p[l] - obs_p[1][l] for l in L]
    carried_s = [count[l] * s[l] - obs_s[1][l] for l in L]
    for n in (1, 0):
        p, q, r, s, den, dx, dy, dz, fx, fy, fz = saved[n]
        nu = [ipv[l] * carried_s[l] for l in L]
        mx = [x_next(nu[l]) - nu[l] for l in L]
        my = [y_next(nu[l]) - nu[l] for l in L]
        mz = [nu[l + 1] - nu[l] for l in range(3)]
        for l in L:
            grad_x[l] = accumulate(
                grad_x[l], main_tile(mx[l]) * main_tile(dx[l]) * main_tile(fx[l])
            )
            grad_y[l] = accumulate(
                grad_y[l], main_tile(my[l]) * main_tile(dy[l]) * main_tile(fy[l])
            )
            if l < 3:
                grad_z[l] = accumulate(
                    grad_z[l], main_tile(mz[l]) * main_tile(dz[l]) * main_tile(fz[l])
                )
        gx_ = [mx[l] * tx[l] for l in L]
        gy_ = [my[l] * ty[l] for l in L]
        gz_ = [mz[l] * tz[l] for l in range(3)]
        hx = [gx_[l] * fx[l] for l in L]
        hy = [gy_[l] * fy[l] for l in L]
        hz = [gz_[l] * fz[l] for l in range(3)]
        pi = []
        for l in L:
            total = carried_p[l] + hx[l] - x_prev(hx[l]) + hy[l] - y_prev(hy[l])
            if l < 3:
                total = total + hz[l]
            if l > 0:
                total = total - hz[l - 1]
            pi.append(total)
        if n:
            kx = [gx_[l] * dx[l] for l in L]
            ky = [gy_[l] * dy[l] for l in L]
            kz = [gz_[l] * dz[l] for l in range(3)]
            back_s = []
            for l in L:
                here = jnp.where(bits[n][l][0], kx[l], 0.0)
                there = kx[l] - here
                total = here + x_prev(there)
                here = jnp.where(bits[n][l][1], ky[l], 0.0)
                there = ky[l] - here
                total = total + here + y_prev(there)
                if l < 3:
                    total = total + jnp.where(bits[n][l][2], kz[l], 0.0)
                if l > 0:
                    total = total + jnp.where(bits[n][l - 1][2], 0.0, kz[l - 1])
                slope = (s[l] * den[l]) * ((1.0 - s[l]) * den[l])
                back_s.append(
                    carried_s[l] + slope * total + (count[l] * s[l] - obs_s[0][l])
                )
            carried_s = back_s

        w2 = [pi[l] * inv[l] for l in L]
        w2_next = [x_next(w2[l]) for l in L]
        rho = gather(w2, w2_next, [x_prev(w2[l]) for l in L])
        w1 = [rho[l] * inv[l] for l in L]
        w1_next = [x_next(w1[l]) for l in L]
        m = main_tile
        for l in L:
            a2, a1 = m(w2[l]), m(w1[l])
            rm, qm, pm = m(r[l]), m(q[l]), m(p[l])
            grad_x[l] = (
                grad_x[l]
                + a2 * (m(x_next(q[l])) - rm)
                + m(w2_next[l]) * (qm - m(x_next(r[l])))
                + a1 * (m(x_next(p[l])) - qm)
                + m(w1_next[l]) * (pm - m(x_next(q[l])))
            )
            grad_y[l] = (
                grad_y[l]
                + a2 * (m(y_next(q[l])) - rm)
                + m(y_next(w2[l])) * (qm - m(y_next(r[l])))
                + a1 * (m(y_next(p[l])) - qm)
                + m(y_next(w1[l])) * (pm - m(y_next(q[l])))
            )
            if l < 3:
                grad_z[l] = (
                    grad_z[l]
                    + a2 * (m(q[l + 1]) - rm)
                    + m(w2[l + 1]) * (qm - m(r[l + 1]))
                    + a1 * (m(p[l + 1]) - qm)
                    + m(w1[l + 1]) * (pm - m(q[l + 1]))
                )
        if n:
            back = gather(w1, w1_next, [x_prev(w1[l]) for l in L])
            carried_p = [
                back[l] + pv[l] * (w1[l] + w2[l]) + (count[l] * p[l] - obs_p[0][l]) for l in L
            ]

    for l in L:
        out[l] = jnp.where(main_tile(keep_x), grad_x[l], 0.0)
        out[4 + l] = jnp.where(main_tile(keep_y), grad_y[l], 0.0)
        if l < 3:
            out[8 + l] = grad_z[l]

    for copy, here, origin, group in sends:
        @pl.when(here)
        def _():
            copy.wait_send()


def adjoint(*args):
    f32, i32 = jnp.float32, jnp.int32
    tiles = lambda n: pltpu.VMEM((n, 8, 128), f32)
    halo = [
        pltpu.VMEM((UP, 16, 128), f32),
        pltpu.VMEM((4, 16, 128), i32),
        pltpu.VMEM((8, 128), f32),
        tiles(UP), tiles(UP),
        pltpu.VMEM((4, 8, 128), i32), pltpu.VMEM((4, 8, 128), i32),
        tiles(2), tiles(5), tiles(9), tiles(9), tiles(5), tiles(5), tiles(6), tiles(6),
    ]
    work = [
        pltpu.VMEM((1, 1, WELLS), i32),
        pltpu.VMEM((1, 1, WELLS), f32),
        pltpu.VMEM((2, 1, 1, WELLS), i32),
        pltpu.VMEM((2, 2, 1, 1, WELLS), f32),
        tiles(2), tiles(5), tiles(11), tiles(11),
    ]
    sems = [pltpu.SemaphoreType.DMA((n,)) for n in (11, 18, 18)] + [
        pltpu.SemaphoreType.REGULAR((8,)), pltpu.SemaphoreType.REGULAR
    ]
    return pl.pallas_call(
        adjoint_kernel,
        out_shape=pltpu.VMEM((11, 16, 128), f32),
        in_specs=[pl.BlockSpec(memory_space=pl.ANY)] * 11,
        out_specs=pl.BlockSpec(memory_space=pltpu.VMEM),
        scratch_shapes=halo + work + sems,
        compiler_params=pltpu.CompilerParams(collective_id=0, has_side_effects=True),
    )(*args)


def deliver_kernel(stack, out_x, out_y, out_z, sem):
    copies = [
        pltpu.make_async_copy(stack.at[pl.ds(first, n)], out, sem.at[i])
        for i, (first, n, out) in enumerate(((0, 4, out_x), (4, 4, out_y), (8, 3, out_z)))
    ]
    for copy in copies:
        copy.start()
    for copy in copies:
        copy.wait()


def deliver(stack):
    return pl.pallas_call(
        deliver_kernel,
        out_shape=[jax.ShapeDtypeStruct((n, 16, 128), jnp.float32) for n in (4, 4, 3)],
        in_specs=[pl.BlockSpec(memory_space=pltpu.VMEM)],
        out_specs=[pl.BlockSpec(memory_space=pl.ANY)] * 3,
        scratch_shapes=[pltpu.SemaphoreType.DMA((3,))],
    )(pltpu.with_memory_space_constraint(stack, pltpu.VMEM))


def on_device(*args):
    return tuple(deliver(adjoint(*args)))


def solution(mesh):
    field = P(None, "gx", "gy")
    in_specs = (field,) * 7 + (
        P("gx", "gy", None),
        P("gx", "gy", None),
        P(None, "gx", "gy", None),
        P(None, None, "gx", "gy", None),
    )
    return jax.shard_map(
        on_device, mesh=mesh, in_specs=in_specs, out_specs=(field,) * 3, check_vma=False
    )
```

```python
import jax
import jax.numpy as jnp
from jax import lax
from jax.experimental import pallas as pl
from jax.experimental.pallas import tpu as pltpu
from jax.sharding import PartitionSpec as P

MESH = pl.DeviceIdType.MESH
time_step = 0.05

P0, TX, TY, TZ, PV, S0, UP, SLOTS = 0, 4, 8, 12, 15, 19, 23, 27
GROUPS = 4
WELLS = 64


def start_exchange(args, halo, work, sems):
    p0, s0, tx, ty, tz, pv, up, cell, rate, plan, observed = args
    own, own_up, own_list, from_n, from_s, up_n, up_s, ext_n, ext_s = halo[:9]
    from_e, from_w, from_ne, from_nw, from_se, from_sw = halo[9:]
    cell_v, rate_v, plan_v, obs_v, xtra_n, xtra_s, pack_e, pack_w = work
    in_sem, send_sem, recv_sem, far_sem, near_sem = sems
    gx, gy = lax.axis_index("gx"), lax.axis_index("gy")
    nx, ny = lax.axis_size("gx"), lax.axis_size("gy")
    has_n, has_s = gx > 0, gx < nx - 1
    has_w, has_e = gy > 0, gy < ny - 1
    both = jnp.logical_and
    peers = (
        (has_n, (gx - 1, gy)),
        (has_s, (gx + 1, gy)),
        (has_e, (gx, gy + 1)),
        (has_w, (gx, gy - 1)),
        (both(has_n, has_e), (gx - 1, gy + 1)),
        (both(has_n, has_w), (gx - 1, gy - 1)),
        (both(has_s, has_e), (gx + 1, gy + 1)),
        (both(has_s, has_w), (gx + 1, gy - 1)),
    )
    N, S, E, W, NE, NW, SE, SW = range(8)
    far_s, far_n = gx == nx // 2 - 1, gx == nx // 2
    herald = gx == nx // 2 - 2
    near_s, near_n = jnp.logical_not(far_s), jnp.logical_not(far_n)
    yields = both(far_s, gy < ny // 4)

    fields = ((p0, P0, 4), (tx, TX, 4), (ty, TY, 4), (tz, TZ, 3), (pv, PV, 4), (s0, S0, 4))
    loads = [(ref, own.at[pl.ds(slot, n)]) for ref, slot, n in fields]
    loads += [(up, own_up), (cell, cell_v), (rate, rate_v), (plan, plan_v), (observed, obs_v)]
    loads = [pltpu.make_async_copy(a, b, in_sem.at[i]) for i, (a, b) in enumerate(loads)]
    for load in loads:
        load.start()

    barrier = pltpu.get_barrier_semaphore()
    for at, (here, peer) in enumerate(peers):
        if at in (E, W):
            here = both(here, near_s)
        elif at in (S, SE, SW):
            here = both(here, both(near_s, jnp.logical_not(herald)))

        @pl.when(here)
        def _():
            pl.semaphore_signal(barrier, inc=1, device_id=peer, device_id_type=MESH)

    rows = jnp.where(both(has_n, near_n), 1, 0) + jnp.where(has_s, 1, 0) + 1
    columns = jnp.where(has_e, 1, 0) + jnp.where(has_w, 1, 0) + 1
    pl.semaphore_wait(barrier, jnp.where(far_s, columns, rows * columns - 1))

    @pl.when(herald)
    def _():
        pl.semaphore_signal(near_sem, inc=1, device_id=(gx + 1, gy), device_id_type=MESH)

    for at, slot in ((S, N), (SE, NW), (SW, NE)):
        here, peer = peers[at]

        @pl.when(both(here, far_s))
        def _():
            pl.semaphore_signal(
                far_sem.at[slot], inc=1, device_id=peer, device_id_type=MESH
            )

    sends = []

    def send(src, dst, to, origin, late=False):
        at = len(sends)
        here, peer = peers[to]
        copy = pltpu.make_async_remote_copy(
            src_ref=src, dst_ref=dst, send_sem=send_sem.at[at], recv_sem=recv_sem.at[at],
            device_id=peer, device_id_type=MESH,
        )
        group = 2 if late else 0 if to in (E, W) else 1
        sends.append((copy, to, here, peers[origin][0], group))

        if to in (N, NE, NW):
            here = both(here, near_n)
        if to == S and len(sends) <= 5:
            here = both(here, jnp.logical_not(yields))

        @pl.when(here)
        def _():
            copy.start()

    for ref, slot, n in fields[:5]:
        send(ref.at[:, pl.ds(8, 8), :], from_n.at[pl.ds(slot, n)], S, N)

    for load in loads[:7]:
        load.wait()

    block = lax.broadcasted_iota(jnp.int32, (8, 128), 1) // 16

    def pack_half(half):
        for group in range(GROUPS):
            first = second = None
            for k in range(min(8, SLOTS - 8 * group)):
                slot = 8 * group + k
                if slot < UP:
                    tile = own[slot, 8 * half : 8 * half + 8]
                else:
                    tile = own_up[slot - UP, 8 * half : 8 * half + 8].astype(jnp.float32)
                if k:
                    tile = pltpu.roll(tile, 16 * k, axis=1)
                first = tile if first is None else jnp.where(block == k, tile, first)
                second = tile if second is None else jnp.where(block == (k + 7) % 8, tile, second)
            pack_e[2 + 4 * half + group] = first
            pack_w[2 + 4 * half + group] = second

    pack_half(1)
    for load in loads[7:]:
        load.wait()
    rates = rate_v[0] * 0.5
    rows = [
        cell_v[0].astype(jnp.float32),
        rates * plan_v[0, 0].astype(jnp.float32),
        rates * plan_v[1, 0].astype(jnp.float32),
        obs_v[0, 0, 0],
        obs_v[0, 1, 0],
        obs_v[1, 0, 0],
        obs_v[1, 1, 0],
        jnp.zeros((1, WELLS), jnp.float32),
    ]
    wells = jnp.concatenate(rows, axis=0)
    wells = jnp.concatenate([wells, wells], axis=1)
    own_list[...] = wells
    pack_e[10] = wells
    pack_w[10] = wells
    send(pack_w.at[pl.ds(6, 5)], from_nw, SE, NW)
    send(pack_e.at[pl.ds(6, 5)], from_ne, SW, NE)

    for layer in range(4):
        xtra_n[0, layer : layer + 1] = own[P0 + layer, 7:8]
        xtra_n[0, 4 + layer : 5 + layer] = own[TX + layer, 7:8]
    xtra_n[1] = wells
    send(xtra_n, ext_n, S, N)
    send(own.at[pl.ds(S0, 4), pl.ds(8, 8), :], from_n.at[pl.ds(S0, 4)], S, N, True)
    send(own_up.at[:, pl.ds(8, 8), :], up_n, S, N, True)

    for layer in range(4):
        xtra_s[0, layer : layer + 1] = own[P0 + layer, 8:9]
        xtra_s[0, 4 + layer : 5 + layer] = own[TY + layer, 8:9]
        xtra_s[1, layer : layer + 1] = own[P0 + layer, 7:8]
        xtra_s[1, 4 + layer : 5 + layer] = own[P0 + layer, 9:10]
        xtra_s[2, layer : layer + 1] = own[TX + layer, 7:8]
        xtra_s[2, 4 + layer : 5 + layer] = own[TX + layer, 8:9]
        xtra_s[3, layer : layer + 1] = own[PV + layer, 8:9]
        if layer < 3:
            xtra_s[3, 4 + layer : 5 + layer] = own[TZ + layer, 8:9]
    xtra_s[3, 7:8] = jnp.zeros((1, 128), jnp.float32)
    xtra_s[4] = wells
    for pack in (pack_e, pack_w):
        pack[0] = xtra_s[0]
        pack[1] = wells
    pack_half(0)

    @pl.when(far_s)
    def _():
        pl.semaphore_wait(near_sem, 1)

    send(pack_w.at[pl.ds(1, 9)], from_w, E, W)
    send(pack_e.at[pl.ds(1, 9)], from_e, W, E)
    send(pack_w.at[pl.ds(0, 6)], from_sw, NE, SW)
    send(pack_e.at[pl.ds(0, 6)], from_se, NW, SE)
    send(xtra_s, ext_s, N, S)
    send(own.at[pl.ds(0, S0), pl.ds(0, 8), :], from_s.at[pl.ds(0, S0)], N, S)
    send(own.at[pl.ds(S0, 4), pl.ds(0, 8), :], from_s.at[pl.ds(S0, 4)], N, S, True)
    send(own_up.at[:, pl.ds(0, 8), :], up_s, N, S, True)

    for at in (N, NE, NW):
        @pl.when(both(peers[at][0], far_n))
        def _():
            pl.semaphore_wait(far_sem.at[at], 1)

    for copy, to, here, origin, group in sends:
        if to in (N, NE, NW):
            @pl.when(both(here, far_n))
            def _():
                copy.start()

    for copy, to, here, origin, group in sends:
        if group == 0:
            @pl.when(both(yields, here))
            def _():
                copy.wait_send()

    @pl.when(yields)
    def _():
        for copy, *_ in sends[:5]:
            copy.start()

    return [(copy, both(here, jnp.logical_not(yields)) if group == 0 else here, origin, group) for copy, to, here, origin, group in sends]


def x_next(v):
    return pltpu.roll(v, v.shape[0] - 1, axis=0)


def x_prev(v):
    return pltpu.roll(v, 1, axis=0)


def y_next(v):
    return pltpu.roll(v, v.shape[1] - 1, axis=1)


def y_prev(v):
    return pltpu.roll(v, 1, axis=1)


def main_tile(v):
    return v[8:24, 0:128]


def well_grids(lists_main, lists_side, missing_n, missing_s, missing_e, missing_w, arrive):
    lane = lax.broadcasted_iota(jnp.int32, (1, 128), 1)
    low = lane < 64

    def ids(cells, drop):
        cells = cells.astype(jnp.int32)
        row = lax.shift_right_logical(cells, 7)
        col = jnp.bitwise_and(cells, 127)
        return row * (1 - drop) - drop, col

    def columns(col):
        at = lax.broadcasted_iota(jnp.int32, (128, 128), 0)
        return jnp.where(at == col, 1.0, 0.0).astype(jnp.bfloat16)

    def split(v):
        hi = v.astype(jnp.bfloat16).astype(jnp.float32)
        mid = (v - hi).astype(jnp.bfloat16).astype(jnp.float32)
        return hi, mid, v - hi - mid

    def product(row, col_hot, value_rows, first, extra):
        count = 32 + (8 if extra else 0)
        at = lax.broadcasted_iota(jnp.int32, (32, 128), 0)
        at = lax.shift_right_logical(at, 3) * 16 + jnp.bitwise_and(at, 7) + first
        hit = row == at
        lhs = []
        for blocks in value_rows:
            lhs.append(
                jnp.concatenate([jnp.where(hit, b, 0.0) for b in blocks], axis=1)
            )
        if extra:
            at = lax.broadcasted_iota(jnp.int32, (8, 128), 0) * 16 + 8
            hit = row == at
            lhs.append(jnp.concatenate([jnp.where(hit, b, 0.0) for b in value_rows[0]], axis=1))
        lhs = jnp.concatenate(lhs, axis=0).astype(jnp.bfloat16)
        rhs = jnp.concatenate([col_hot] * len(value_rows[0]), axis=1)
        return lax.dot_general(
            lhs, rhs, (((1,), (1,)), ((), ())), preferred_element_type=jnp.float32
        )

    zero = jnp.zeros((1, 128), jnp.float32)

    def main_values(tile):
        out = []
        for q in range(1, 7):
            hi, mid, lo = split(tile[q : q + 1])
            out.append([jnp.where(low, hi, mid), jnp.where(low, lo, zero)])
        out.append([jnp.where(low, zero + 1.0, zero), zero])
        return out

    def side_values(tile):
        out = []
        for q in range(1, 7):
            out.append(list(split(tile[q : q + 1])))
        out.append([zero + 1.0, zero, zero])
        return out

    def main_part(tile, drop):
        row, col = ids(tile[0:1], drop)
        return row, columns(col), main_values(tile)

    def side_part(tile, drop):
        row, col = ids(tile[0:1], drop + jnp.where(low, missing_e, missing_w))
        col = jnp.where(low, jnp.where(col < 64, col, -1), jnp.where(col < 64, -1, col))
        return row, columns(col), side_values(tile)

    def both_parts(at, drop):
        e, w = lists_side[at]()
        return (
            main_part(lists_main[at](), drop),
            side_part(jnp.where(low, e, w), drop),
        )

    c, sc = both_parts(1, 0)
    middle = [product(*part, first, False) for part in (c, sc) for first in (0, 8)]
    arrive()
    n, sn = both_parts(0, missing_n)
    s, ss = both_parts(2, missing_s)
    mains = [product(*n, 8, False), middle[0], middle[1], product(*s, 0, True)]
    sides = [product(*sn, 8, False), middle[2], middle[3], product(*ss, 0, False)]
    grids = []
    for q in range(7):
        layers = []
        for layer in range(4):
            at = (q * 4 + layer) * 8
            layers.append(
                jnp.concatenate(
                    [
                        jnp.concatenate([m[at : at + 8], d[at : at + 8]], axis=1)
                        for m, d in zip(mains, sides)
                    ],
                    axis=0,
                )
            )
        grids.append(layers)
    return grids, mains[3][224:232]


def adjoint_kernel(*refs):
    args, out = refs[:11], refs[11]
    halo, work, sems = refs[12:27], refs[27:35], refs[35:]
    sends = start_exchange(args, halo, work, sems)
    own, own_up, own_list, from_n, from_s, up_n, up_s, ext_n, ext_s = halo[:9]
    from_e, from_w, from_ne, from_nw, from_se, from_sw = halo[9:]

    def receive(which):
        for copy, here, origin, group in sends:
            if group == which:
                @pl.when(origin)
                def _():
                    copy.wait_recv()

    receive(0)
    gx, gy = lax.axis_index("gx"), lax.axis_index("gy")
    nx, ny = lax.axis_size("gx"), lax.axis_size("gy")
    miss_n, miss_s = gx == 0, gx == nx - 1
    miss_w, miss_e = gy == 0, gy == ny - 1
    shape = (32, 256)
    row = lax.broadcasted_iota(jnp.int32, shape, 0)
    lane = lax.broadcasted_iota(jnp.int32, shape, 1)

    row_low = jnp.where(miss_n, 8, 0)
    row_high = jnp.where(miss_s, 24, 32)
    lane_low = jnp.where(miss_e, 192, 128)
    lane_high = jnp.where(miss_w, 192, 256)
    row_ok = (row >= row_low) & (row < row_high)
    lane_ok = (lane < 128) | ((lane >= lane_low) & (lane < lane_high))
    valid = row_ok & lane_ok
    keep_x = valid & jnp.logical_not((row == 23) & miss_s)
    keep_y = valid & jnp.logical_not((lane == 127) & miss_e)

    (src0, src1, obs_p0, obs_s0, obs_p1, obs_s1, count), src0_extra = well_grids(
        (lambda: ext_n[1], lambda: own_list[...], lambda: ext_s[4]),
        (
            lambda: (from_ne[4], from_nw[4]),
            lambda: (from_e[0], from_w[0]),
            lambda: (from_se[1], from_sw[1]),
        ),
        *[jnp.where(miss, 1, 0) for miss in (miss_n, miss_s, miss_e, miss_w)],
        lambda: receive(1),
    )

    block = lax.broadcasted_iota(jnp.int32, (8, 128), 1) // 16
    even = jnp.bitwise_and(block, 1) == 0
    merged = []
    for e_ref, w_ref, base in (
        (from_ne, from_nw, 0), (from_e, from_w, 1), (from_e, from_w, 5), (from_se, from_sw, 2)
    ):
        pairs = []
        for group in range(GROUPS):
            e, w = e_ref[base + group], w_ref[base + group]
            pairs.append((jnp.where(even, e, w), jnp.where(even, w, e)))
        merged.append(pairs)

    def field(slot, mask, fill):
        group, k = slot // 8, slot % 8
        sides = []
        for j in range(4):
            tile = merged[j][group][k % 2]
            sides.append(pltpu.roll(tile, 128 - 16 * k, axis=1) if k else tile)
        if slot < UP:
            mains = [from_n[slot], own[slot], from_s[slot]]
        else:
            mains = [up_n[slot - UP], own_up[slot - UP], up_s[slot - UP]]
            sides = [side.astype(jnp.int32) for side in sides]
        whole = jnp.concatenate(
            [jnp.concatenate(mains, axis=0), jnp.concatenate(sides, axis=0)], axis=1
        )
        return jnp.where(mask, whole, fill)

    L = range(4)
    p0 = [field(P0 + l, valid, 0.0) for l in L]
    tx = [field(TX + l, keep_x, 0.0) for l in L]
    ty = [field(TY + l, keep_y, 0.0) for l in L]
    tz = [field(TZ + l, valid, 0.0) for l in range(3)]
    pv = [field(PV + l, valid, 1.0) for l in L]

    src, obs_p, obs_s = (src0, src1), (obs_p0, obs_p1), (obs_s0, obs_s1)

    row8 = lax.broadcasted_iota(jnp.int32, (8, 256), 0)

    def first_row(v, extra):
        top = jnp.where(row8 == 0, jnp.concatenate([extra, extra], axis=1), v[0:8])
        return jnp.concatenate([top, v[8:32]], axis=0)

    def last_row(v, extra):
        tail = jnp.where(row8 == 7, jnp.concatenate([extra, extra], axis=1), v[24:32])
        return jnp.concatenate([v[0:24], tail], axis=0)

    edge_n = jnp.where(miss_n, 0.0, ext_n[0])
    txw = [first_row(x_prev(tx[l]), edge_n[4 + l : 5 + l]) for l in L]
    tyw = [y_prev(ty[l]) for l in L]

    def z_sum(faces, values, l):
        total = None
        if l < 3:
            total = faces[l] * values[l + 1]
        if l > 0:
            term = faces[l - 1] * values[l - 1]
            total = term if total is None else total + term
        return total

    ones = [None] * 4
    inv = []
    for l in L:
        den = pv[l] + tx[l] + txw[l] + ty[l] + tyw[l]
        if l < 3:
            den = den + tz[l]
        if l > 0:
            den = den + tz[l - 1]
        inv.append(1.0 / den)

    def gather(values, nexts, prevs):
        out = []
        for l in L:
            total = tx[l] * nexts[l] + txw[l] * prevs[l]
            total = total + ty[l] * y_next(values[l]) + tyw[l] * y_prev(values[l])
            out.append(total + z_sum(tz, values, l))
        return out

    sub8 = lax.broadcasted_iota(jnp.int32, (8, 128), 0)
    cut = lambda t: jnp.where(miss_s, 0.0, t)
    t0 = ext_s[0]
    lane8 = lax.broadcasted_iota(jnp.int32, (8, 128), 1)
    side0 = jnp.where(lane8 < 64, jnp.where(miss_e, 0.0, from_se[0]), jnp.where(miss_w, 0.0, from_sw[0]))
    t0 = jnp.concatenate([cut(t0), cut(side0)], axis=1)
    t0n, t0p = y_next(t0)[:, 0:128], y_prev(t0)[:, 0:128]
    t0 = t0[:, 0:128]
    t1, t2, t3 = cut(ext_s[1]), cut(ext_s[2]), cut(ext_s[3])
    low4 = lambda t: pltpu.roll(t, 4, axis=0)
    ty_x = jnp.where((lane8 == 127) & miss_e, 0.0, low4(t0))
    tyw_x = low4(t0p)
    tx_x, txw_x = low4(t2), t2
    pv_x = jnp.where(miss_s, 1.0, t3)
    tz_x = jnp.where(sub8 < 3, low4(t3), 0.0)
    tzw_x = jnp.where((sub8 >= 1) & (sub8 < 4), pltpu.roll(low4(t3), 1, axis=0), 0.0)
    num_x = (
        pv_x * t0 + src0_extra + tx_x * low4(t1) + txw_x * t1 + ty_x * t0n + tyw_x * t0p
        + tz_x * pltpu.roll(t0, 7, axis=0) + tzw_x * pltpu.roll(t0, 1, axis=0)
    )
    q_extra = num_x / (pv_x + tx_x + txw_x + ty_x + tyw_x + tz_x + tzw_x)

    ipv = [time_step / pv[l] for l in L]
    saved = []
    p = p0
    for n in range(2):
        p_next = [x_next(p[l]) for l in L]
        p_prev = [x_prev(p[l]) for l in L]
        if n == 0:
            p_prev = [first_row(p_prev[l], edge_n[l : l + 1]) for l in L]
        base = [pv[l] * p[l] + src[n][l] for l in L]
        total = gather(p, p_next, p_prev)
        q = [(base[l] + total[l]) * inv[l] for l in L]
        q_next = [x_next(q[l]) for l in L]
        if n == 0:
            q_next = [last_row(q_next[l], q_extra[l : l + 1]) for l in L]
        total = gather(q, q_next, [x_prev(q[l]) for l in L])
        r = [(base[l] + total[l]) * inv[l] for l in L]

        if n == 0:
            receive(2)
            s = [field(S0 + l, valid, 0.0) for l in L]
            up = [field(UP + l, valid, 0) for l in L]
            bits = [[[jnp.bitwise_and(up[l], 1 << (3 * n + d)) != 0 for d in range(3)] for l in L] for n in range(2)]

        den = []
        mob = []
        for l in L:
            wet = s[l] * s[l]
            dry = 1.0 - s[l]
            scale = 1.0 / (wet + 0.5 * dry * dry)
            den.append(scale)
            mob.append(wet * scale)
        dx = [r[l] - x_next(r[l]) for l in L]
        dy = [r[l] - y_next(r[l]) for l in L]
        dz = [r[l] - r[l + 1] for l in range(3)]
        fx = [jnp.where(bits[n][l][0], mob[l], x_next(mob[l])) for l in L]
        fy = [jnp.where(bits[n][l][1], mob[l], y_next(mob[l])) for l in L]
        fz = [jnp.where(bits[n][l][2], mob[l], mob[l + 1]) for l in range(3)]
        flow_x = [tx[l] * dx[l] * fx[l] for l in L]
        flow_y = [ty[l] * dy[l] * fy[l] for l in L]
        flow_z = [tz[l] * dz[l] * fz[l] for l in range(3)]
        moved = []
        for l in L:
            net = flow_x[l] - x_prev(flow_x[l]) + flow_y[l] - y_prev(flow_y[l])
            if l < 3:
                net = net + flow_z[l]
            if l > 0:
                net = net - flow_z[l - 1]
            moved.append(s[l] - ipv[l] * net)
        saved.append((p, q, r, s, den, dx, dy, dz, fx, fy, fz))
        p, s = r, moved

    grad_x = [None] * 4
    grad_y = [None] * 4
    grad_z = [None] * 3

    def accumulate(total, term):
        return term if total is None else total + term

    carried_p = [count[l] * p[l] - obs_p[1][l] for l in L]
    carried_s = [count[l] * s[l] - obs_s[1][l] for l in L]
    for n in (1, 0):
        p, q, r, s, den, dx, dy, dz, fx, fy, fz = saved[n]
        nu = [ipv[l] * carried_s[l] for l in L]
        mx = [x_next(nu[l]) - nu[l] for l in L]
        my = [y_next(nu[l]) - nu[l] for l in L]
        mz = [nu[l + 1] - nu[l] for l in range(3)]
        for l in L:
            grad_x[l] = accumulate(
                grad_x[l], main_tile(mx[l]) * main_tile(dx[l]) * main_tile(fx[l])
            )
            grad_y[l] = accumulate(
                grad_y[l], main_tile(my[l]) * main_tile(dy[l]) * main_tile(fy[l])
            )
            if l < 3:
                grad_z[l] = accumulate(
                    grad_z[l], main_tile(mz[l]) * main_tile(dz[l]) * main_tile(fz[l])
                )
        gx_ = [mx[l] * tx[l] for l in L]
        gy_ = [my[l] * ty[l] for l in L]
        gz_ = [mz[l] * tz[l] for l in range(3)]
        hx = [gx_[l] * fx[l] for l in L]
        hy = [gy_[l] * fy[l] for l in L]
        hz = [gz_[l] * fz[l] for l in range(3)]
        pi = []
        for l in L:
            total = carried_p[l] + hx[l] - x_prev(hx[l]) + hy[l] - y_prev(hy[l])
            if l < 3:
                total = total + hz[l]
            if l > 0:
                total = total - hz[l - 1]
            pi.append(total)
        if n:
            kx = [gx_[l] * dx[l] for l in L]
            ky = [gy_[l] * dy[l] for l in L]
            kz = [gz_[l] * dz[l] for l in range(3)]
            back_s = []
            for l in L:
                here = jnp.where(bits[n][l][0], kx[l], 0.0)
                there = kx[l] - here
                total = here + x_prev(there)
                here = jnp.where(bits[n][l][1], ky[l], 0.0)
                there = ky[l] - here
                total = total + here + y_prev(there)
                if l < 3:
                    total = total + jnp.where(bits[n][l][2], kz[l], 0.0)
                if l > 0:
                    total = total + jnp.where(bits[n][l - 1][2], 0.0, kz[l - 1])
                slope = (s[l] * den[l]) * ((1.0 - s[l]) * den[l])
                back_s.append(
                    carried_s[l] + slope * total + (count[l] * s[l] - obs_s[0][l])
                )
            carried_s = back_s

        w2 = [pi[l] * inv[l] for l in L]
        w2_next = [x_next(w2[l]) for l in L]
        rho = gather(w2, w2_next, [x_prev(w2[l]) for l in L])
        w1 = [rho[l] * inv[l] for l in L]
        w1_next = [x_next(w1[l]) for l in L]
        m = main_tile
        for l in L:
            a2, a1 = m(w2[l]), m(w1[l])
            rm, qm, pm = m(r[l]), m(q[l]), m(p[l])
            grad_x[l] = (
                grad_x[l]
                + a2 * (m(x_next(q[l])) - rm)
                + m(w2_next[l]) * (qm - m(x_next(r[l])))
                + a1 * (m(x_next(p[l])) - qm)
                + m(w1_next[l]) * (pm - m(x_next(q[l])))
            )
            grad_y[l] = (
                grad_y[l]
                + a2 * (m(y_next(q[l])) - rm)
                + m(y_next(w2[l])) * (qm - m(y_next(r[l])))
                + a1 * (m(y_next(p[l])) - qm)
                + m(y_next(w1[l])) * (pm - m(y_next(q[l])))
            )
            if l < 3:
                grad_z[l] = (
                    grad_z[l]
                    + a2 * (m(q[l + 1]) - rm)
                    + m(w2[l + 1]) * (qm - m(r[l + 1]))
                    + a1 * (m(p[l + 1]) - qm)
                    + m(w1[l + 1]) * (pm - m(q[l + 1]))
                )
        if n:
            back = gather(w1, w1_next, [x_prev(w1[l]) for l in L])
            carried_p = [
                back[l] + pv[l] * (w1[l] + w2[l]) + (count[l] * p[l] - obs_p[0][l]) for l in L
            ]

    for l in L:
        out[l] = jnp.where(main_tile(keep_x), grad_x[l], 0.0)
        out[4 + l] = jnp.where(main_tile(keep_y), grad_y[l], 0.0)
        if l < 3:
            out[8 + l] = grad_z[l]

    for copy, here, origin, group in sends:
        @pl.when(here)
        def _():
            copy.wait_send()


def adjoint(*args):
    f32, i32 = jnp.float32, jnp.int32
    tiles = lambda n: pltpu.VMEM((n, 8, 128), f32)
    halo = [
        pltpu.VMEM((UP, 16, 128), f32),
        pltpu.VMEM((4, 16, 128), i32),
        pltpu.VMEM((8, 128), f32),
        tiles(UP), tiles(UP),
        pltpu.VMEM((4, 8, 128), i32), pltpu.VMEM((4, 8, 128), i32),
        tiles(2), tiles(5), tiles(9), tiles(9), tiles(5), tiles(5), tiles(6), tiles(6),
    ]
    work = [
        pltpu.VMEM((1, 1, WELLS), i32),
        pltpu.VMEM((1, 1, WELLS), f32),
        pltpu.VMEM((2, 1, 1, WELLS), i32),
        pltpu.VMEM((2, 2, 1, 1, WELLS), f32),
        tiles(2), tiles(5), tiles(11), tiles(11),
    ]
    sems = [pltpu.SemaphoreType.DMA((n,)) for n in (11, 18, 18)] + [
        pltpu.SemaphoreType.REGULAR((8,)), pltpu.SemaphoreType.REGULAR
    ]
    return pl.pallas_call(
        adjoint_kernel,
        out_shape=pltpu.VMEM((11, 16, 128), f32),
        in_specs=[pl.BlockSpec(memory_space=pl.ANY)] * 11,
        out_specs=pl.BlockSpec(memory_space=pltpu.VMEM),
        scratch_shapes=halo + work + sems,
        compiler_params=pltpu.CompilerParams(collective_id=0, has_side_effects=True),
    )(*args)


def deliver_kernel(stack, out_x, out_y, out_z, sem):
    copies = [
        pltpu.make_async_copy(stack.at[pl.ds(first, n)], out, sem.at[i])
        for i, (first, n, out) in enumerate(((0, 4, out_x), (4, 4, out_y), (8, 3, out_z)))
    ]
    for copy in copies:
        copy.start()
    for copy in copies:
        copy.wait()


def deliver(stack):
    return pl.pallas_call(
        deliver_kernel,
        out_shape=[jax.ShapeDtypeStruct((n, 16, 128), jnp.float32) for n in (4, 4, 3)],
        in_specs=[pl.BlockSpec(memory_space=pltpu.VMEM)],
        out_specs=[pl.BlockSpec(memory_space=pl.ANY)] * 3,
        scratch_shapes=[pltpu.SemaphoreType.DMA((3,))],
    )(pltpu.with_memory_space_constraint(stack, pltpu.VMEM))


def on_device(*args):
    return tuple(deliver(adjoint(*args)))


def solution(mesh):
    field = P(None, "gx", "gy")
    in_specs = (field,) * 7 + (
        P("gx", "gy", None),
        P("gx", "gy", None),
        P(None, "gx", "gy", None),
        P(None, None, "gx", "gy", None),
    )
    return jax.shard_map(
        on_device, mesh=mesh, in_specs=in_specs, out_specs=(field,) * 3, check_vma=False
    )
```

```python
import jax
import jax.numpy as jnp
from jax import lax
from jax.experimental import pallas as pl
from jax.experimental.pallas import tpu as pltpu
from jax.sharding import PartitionSpec as P

MESH = pl.DeviceIdType.MESH
time_step = 0.05

P0, TX, TY, TZ, PV, S0, UP, SLOTS = 0, 4, 8, 12, 15, 19, 23, 27
GROUPS = 4
WELLS = 64


def start_exchange(args, halo, work, sems):
    p0, s0, tx, ty, tz, pv, up, cell, rate, plan, observed = args
    own, own_up, own_list, from_n, from_s, up_n, up_s, ext_n, ext_s = halo[:9]
    from_e, from_w, from_ne, from_nw, from_se, from_sw = halo[9:]
    cell_v, rate_v, plan_v, obs_v, xtra_n, xtra_s, pack_e, pack_w = work
    in_sem, send_sem, recv_sem, far_sem, near_sem = sems
    gx, gy = lax.axis_index("gx"), lax.axis_index("gy")
    nx, ny = lax.axis_size("gx"), lax.axis_size("gy")
    has_n, has_s = gx > 0, gx < nx - 1
    has_w, has_e = gy > 0, gy < ny - 1
    both = jnp.logical_and
    peers = (
        (has_n, (gx - 1, gy)),
        (has_s, (gx + 1, gy)),
        (has_e, (gx, gy + 1)),
        (has_w, (gx, gy - 1)),
        (both(has_n, has_e), (gx - 1, gy + 1)),
        (both(has_n, has_w), (gx - 1, gy - 1)),
        (both(has_s, has_e), (gx + 1, gy + 1)),
        (both(has_s, has_w), (gx + 1, gy - 1)),
    )
    N, S, E, W, NE, NW, SE, SW = range(8)
    far_s, far_n = gx == nx // 2 - 1, gx == nx // 2
    herald = gx == nx // 2 - 2
    near_s, near_n = jnp.logical_not(far_s), jnp.logical_not(far_n)
    yields = both(far_s, gy < ny // 4)

    fields = ((p0, P0, 4), (tx, TX, 4), (ty, TY, 4), (tz, TZ, 3), (pv, PV, 4), (s0, S0, 4))
    loads = [(ref, own.at[pl.ds(slot, n)]) for ref, slot, n in fields]
    loads += [(up, own_up), (cell, cell_v), (rate, rate_v), (plan, plan_v), (observed, obs_v)]
    loads = [pltpu.make_async_copy(a, b, in_sem.at[i]) for i, (a, b) in enumerate(loads)]
    for load in loads:
        load.start()

    barrier = pltpu.get_barrier_semaphore()
    for at, (here, peer) in enumerate(peers):
        if at in (E, W):
            here = both(here, near_s)
        elif at in (S, SE, SW):
            here = both(here, both(near_s, jnp.logical_not(herald)))

        @pl.when(here)
        def _():
            pl.semaphore_signal(barrier, inc=1, device_id=peer, device_id_type=MESH)

    rows = jnp.where(both(has_n, near_n), 1, 0) + jnp.where(has_s, 1, 0) + 1
    columns = jnp.where(has_e, 1, 0) + jnp.where(has_w, 1, 0) + 1
    pl.semaphore_wait(barrier, jnp.where(far_s, columns, rows * columns - 1))

    @pl.when(herald)
    def _():
        pl.semaphore_signal(near_sem, inc=1, device_id=(gx + 1, gy), device_id_type=MESH)

    for at, slot in ((S, N), (SE, NW), (SW, NE)):
        here, peer = peers[at]

        @pl.when(both(here, far_s))
        def _():
            pl.semaphore_signal(
                far_sem.at[slot], inc=1, device_id=peer, device_id_type=MESH
            )

    sends = []

    def send(src, dst, to, origin, late=False):
        at = len(sends)
        here, peer = peers[to]
        copy = pltpu.make_async_remote_copy(
            src_ref=src, dst_ref=dst, send_sem=send_sem.at[at], recv_sem=recv_sem.at[at],
            device_id=peer, device_id_type=MESH,
        )
        group = 2 if late else 0 if to in (E, W) else 3 if to in (N, NE, NW) else 1
        sends.append((copy, to, here, peers[origin][0], group))

        if to in (N, NE, NW):
            here = both(here, near_n)
        if to == S and len(sends) <= 5:
            here = both(here, jnp.logical_not(yields))

        @pl.when(here)
        def _():
            copy.start()

    for ref, slot, n in fields[:5]:
        send(ref.at[:, pl.ds(8, 8), :], from_n.at[pl.ds(slot, n)], S, N)

    for load in loads[:7]:
        load.wait()

    block = lax.broadcasted_iota(jnp.int32, (8, 128), 1) // 16

    def pack_half(half):
        for group in range(GROUPS):
            first = second = None
            for k in range(min(8, SLOTS - 8 * group)):
                slot = 8 * group + k
                if slot < UP:
                    tile = own[slot, 8 * half : 8 * half + 8]
                else:
                    tile = own_up[slot - UP, 8 * half : 8 * half + 8].astype(jnp.float32)
                if k:
                    tile = pltpu.roll(tile, 16 * k, axis=1)
                first = tile if first is None else jnp.where(block == k, tile, first)
                second = tile if second is None else jnp.where(block == (k + 7) % 8, tile, second)
            pack_e[2 + 4 * half + group] = first
            pack_w[2 + 4 * half + group] = second

    pack_half(1)
    for load in loads[7:]:
        load.wait()
    rates = rate_v[0] * 0.5
    rows = [
        cell_v[0].astype(jnp.float32),
        rates * plan_v[0, 0].astype(jnp.float32),
        rates * plan_v[1, 0].astype(jnp.float32),
        obs_v[0, 0, 0],
        obs_v[0, 1, 0],
        obs_v[1, 0, 0],
        obs_v[1, 1, 0],
        jnp.zeros((1, WELLS), jnp.float32),
    ]
    wells = jnp.concatenate(rows, axis=0)
    wells = jnp.concatenate([wells, wells], axis=1)
    own_list[...] = wells
    pack_e[10] = wells
    pack_w[10] = wells
    send(pack_w.at[pl.ds(6, 5)], from_nw, SE, NW)
    send(pack_e.at[pl.ds(6, 5)], from_ne, SW, NE)

    for layer in range(4):
        xtra_n[0, layer : layer + 1] = own[P0 + layer, 7:8]
        xtra_n[0, 4 + layer : 5 + layer] = own[TX + layer, 7:8]
    xtra_n[1] = wells
    send(xtra_n, ext_n, S, N)
    send(own.at[pl.ds(S0, 4), pl.ds(8, 8), :], from_n.at[pl.ds(S0, 4)], S, N, True)
    send(own_up.at[:, pl.ds(8, 8), :], up_n, S, N, True)

    for layer in range(4):
        xtra_s[0, layer : layer + 1] = own[P0 + layer, 8:9]
        xtra_s[0, 4 + layer : 5 + layer] = own[TY + layer, 8:9]
        xtra_s[1, layer : layer + 1] = own[P0 + layer, 7:8]
        xtra_s[1, 4 + layer : 5 + layer] = own[P0 + layer, 9:10]
        xtra_s[2, layer : layer + 1] = own[TX + layer, 7:8]
        xtra_s[2, 4 + layer : 5 + layer] = own[TX + layer, 8:9]
        xtra_s[3, layer : layer + 1] = own[PV + layer, 8:9]
        if layer < 3:
            xtra_s[3, 4 + layer : 5 + layer] = own[TZ + layer, 8:9]
    xtra_s[3, 7:8] = jnp.zeros((1, 128), jnp.float32)
    xtra_s[4] = wells
    for pack in (pack_e, pack_w):
        pack[0] = xtra_s[0]
        pack[1] = wells
    pack_half(0)

    @pl.when(far_s)
    def _():
        pl.semaphore_wait(near_sem, 1)

    send(pack_w.at[pl.ds(1, 9)], from_w, E, W)
    send(pack_e.at[pl.ds(1, 9)], from_e, W, E)
    send(pack_w.at[pl.ds(0, 6)], from_sw, NE, SW)
    send(pack_e.at[pl.ds(0, 6)], from_se, NW, SE)
    send(xtra_s, ext_s, N, S)
    send(own.at[pl.ds(0, S0), pl.ds(0, 8), :], from_s.at[pl.ds(0, S0)], N, S)
    send(own.at[pl.ds(S0, 4), pl.ds(0, 8), :], from_s.at[pl.ds(S0, 4)], N, S, True)
    send(own_up.at[:, pl.ds(0, 8), :], up_s, N, S, True)

    for at in (N, NE, NW):
        @pl.when(both(peers[at][0], far_n))
        def _():
            pl.semaphore_wait(far_sem.at[at], 1)

    for copy, to, here, origin, group in sends:
        if to in (N, NE, NW):
            @pl.when(both(here, far_n))
            def _():
                copy.start()

    for copy, to, here, origin, group in sends:
        if group == 0:
            @pl.when(both(yields, here))
            def _():
                copy.wait_send()

    @pl.when(yields)
    def _():
        for copy, *_ in sends[:5]:
            copy.start()

    return [(copy, both(here, jnp.logical_not(yields)) if group == 0 else here, origin, group) for copy, to, here, origin, group in sends]


def x_next(v):
    return pltpu.roll(v, v.shape[0] - 1, axis=0)


def x_prev(v):
    return pltpu.roll(v, 1, axis=0)


def y_next(v):
    return pltpu.roll(v, v.shape[1] - 1, axis=1)


def y_prev(v):
    return pltpu.roll(v, 1, axis=1)


def main_tile(v):
    return v[8:24, 0:128]


def well_grids(lists_main, lists_side, missing_n, missing_s, missing_e, missing_w, arrive):
    lane = lax.broadcasted_iota(jnp.int32, (1, 128), 1)
    low = lane < 64

    def ids(cells, drop):
        cells = cells.astype(jnp.int32)
        row = lax.shift_right_logical(cells, 7)
        col = jnp.bitwise_and(cells, 127)
        return row * (1 - drop) - drop, col

    def columns(col):
        at = lax.broadcasted_iota(jnp.int32, (128, 128), 0)
        return jnp.where(at == col, 1.0, 0.0).astype(jnp.bfloat16)

    def split(v):
        hi = v.astype(jnp.bfloat16).astype(jnp.float32)
        mid = (v - hi).astype(jnp.bfloat16).astype(jnp.float32)
        return hi, mid, v - hi - mid

    def product(row, col_hot, value_rows, first, extra):
        count = 32 + (8 if extra else 0)
        at = lax.broadcasted_iota(jnp.int32, (32, 128), 0)
        at = lax.shift_right_logical(at, 3) * 16 + jnp.bitwise_and(at, 7) + first
        hit = row == at
        lhs = []
        for blocks in value_rows:
            lhs.append(
                jnp.concatenate([jnp.where(hit, b, 0.0) for b in blocks], axis=1)
            )
        if extra:
            at = lax.broadcasted_iota(jnp.int32, (8, 128), 0) * 16 + 8
            hit = row == at
            lhs.append(jnp.concatenate([jnp.where(hit, b, 0.0) for b in value_rows[0]], axis=1))
        lhs = jnp.concatenate(lhs, axis=0).astype(jnp.bfloat16)
        rhs = jnp.concatenate([col_hot] * len(value_rows[0]), axis=1)
        return lax.dot_general(
            lhs, rhs, (((1,), (1,)), ((), ())), preferred_element_type=jnp.float32
        )

    zero = jnp.zeros((1, 128), jnp.float32)

    def main_values(tile):
        out = []
        for q in range(1, 7):
            hi, mid, lo = split(tile[q : q + 1])
            out.append([jnp.where(low, hi, mid), jnp.where(low, lo, zero)])
        out.append([jnp.where(low, zero + 1.0, zero), zero])
        return out

    def side_values(tile):
        out = []
        for q in range(1, 7):
            out.append(list(split(tile[q : q + 1])))
        out.append([zero + 1.0, zero, zero])
        return out

    def main_part(tile, drop):
        row, col = ids(tile[0:1], drop)
        return row, columns(col), main_values(tile)

    def side_part(tile, drop):
        row, col = ids(tile[0:1], drop + jnp.where(low, missing_e, missing_w))
        col = jnp.where(low, jnp.where(col < 64, col, -1), jnp.where(col < 64, -1, col))
        return row, columns(col), side_values(tile)

    def both_parts(at, drop):
        e, w = lists_side[at]()
        return (
            main_part(lists_main[at](), drop),
            side_part(jnp.where(low, e, w), drop),
        )

    c, sc = both_parts(1, 0)
    middle = [product(*part, first, False) for part in (c, sc) for first in (0, 8)]
    arrive(3)
    s, ss = both_parts(2, missing_s)
    lower = [product(*s, 0, True), product(*ss, 0, False)]
    arrive(1)
    n, sn = both_parts(0, missing_n)
    mains = [product(*n, 8, False), middle[0], middle[1], lower[0]]
    sides = [product(*sn, 8, False), middle[2], middle[3], lower[1]]
    grids = []
    for q in range(7):
        layers = []
        for layer in range(4):
            at = (q * 4 + layer) * 8
            layers.append(
                jnp.concatenate(
                    [
                        jnp.concatenate([m[at : at + 8], d[at : at + 8]], axis=1)
                        for m, d in zip(mains, sides)
                    ],
                    axis=0,
                )
            )
        grids.append(layers)
    return grids, mains[3][224:232]


def adjoint_kernel(*refs):
    args, out = refs[:11], refs[11]
    halo, work, sems = refs[12:27], refs[27:35], refs[35:]
    sends = start_exchange(args, halo, work, sems)
    own, own_up, own_list, from_n, from_s, up_n, up_s, ext_n, ext_s = halo[:9]
    from_e, from_w, from_ne, from_nw, from_se, from_sw = halo[9:]

    def receive(which):
        for copy, here, origin, group in sends:
            if group == which:
                @pl.when(origin)
                def _():
                    copy.wait_recv()

    receive(0)
    gx, gy = lax.axis_index("gx"), lax.axis_index("gy")
    nx, ny = lax.axis_size("gx"), lax.axis_size("gy")
    miss_n, miss_s = gx == 0, gx == nx - 1
    miss_w, miss_e = gy == 0, gy == ny - 1
    shape = (32, 256)
    row = lax.broadcasted_iota(jnp.int32, shape, 0)
    lane = lax.broadcasted_iota(jnp.int32, shape, 1)

    row_low = jnp.where(miss_n, 8, 0)
    row_high = jnp.where(miss_s, 24, 32)
    lane_low = jnp.where(miss_e, 192, 128)
    lane_high = jnp.where(miss_w, 192, 256)
    row_ok = (row >= row_low) & (row < row_high)
    lane_ok = (lane < 128) | ((lane >= lane_low) & (lane < lane_high))
    valid = row_ok & lane_ok
    keep_x = valid & jnp.logical_not((row == 23) & miss_s)
    keep_y = valid & jnp.logical_not((lane == 127) & miss_e)

    block = lax.broadcasted_iota(jnp.int32, (8, 128), 1) // 16
    even = jnp.bitwise_and(block, 1) == 0
    side_tiles = {}

    def unpack(j):
        e_ref, w_ref, base = (
            (from_ne, from_nw, 0), (from_e, from_w, 1), (from_e, from_w, 5), (from_se, from_sw, 2)
        )[j]
        for group in range(GROUPS):
            e, w = e_ref[base + group], w_ref[base + group]
            pair = jnp.where(even, e, w), jnp.where(even, w, e)
            for k in range(min(8, SLOTS - 8 * group)):
                tile = pair[k % 2]
                side_tiles[8 * group + k, j] = (
                    pltpu.roll(tile, 128 - 16 * k, axis=1) if k else tile
                )

    def arrive(which):
        receive(which)
        for j in (3,) if which == 3 else (0,):
            unpack(j)

    unpack(1)
    unpack(2)
    (src0, src1, obs_p0, obs_s0, obs_p1, obs_s1, count), src0_extra = well_grids(
        (lambda: ext_n[1], lambda: own_list[...], lambda: ext_s[4]),
        (
            lambda: (from_ne[4], from_nw[4]),
            lambda: (from_e[0], from_w[0]),
            lambda: (from_se[1], from_sw[1]),
        ),
        *[jnp.where(miss, 1, 0) for miss in (miss_n, miss_s, miss_e, miss_w)],
        arrive,
    )

    def field(slot, mask, fill):
        sides = [side_tiles[slot, j] for j in range(4)]
        if slot < UP:
            mains = [from_n[slot], own[slot], from_s[slot]]
        else:
            mains = [up_n[slot - UP], own_up[slot - UP], up_s[slot - UP]]
            sides = [side.astype(jnp.int32) for side in sides]
        whole = jnp.concatenate(
            [jnp.concatenate(mains, axis=0), jnp.concatenate(sides, axis=0)], axis=1
        )
        return jnp.where(mask, whole, fill)

    L = range(4)
    p0 = [field(P0 + l, valid, 0.0) for l in L]
    tx = [field(TX + l, keep_x, 0.0) for l in L]
    ty = [field(TY + l, keep_y, 0.0) for l in L]
    tz = [field(TZ + l, valid, 0.0) for l in range(3)]
    pv = [field(PV + l, valid, 1.0) for l in L]

    src, obs_p, obs_s = (src0, src1), (obs_p0, obs_p1), (obs_s0, obs_s1)

    row8 = lax.broadcasted_iota(jnp.int32, (8, 256), 0)

    def first_row(v, extra):
        top = jnp.where(row8 == 0, jnp.concatenate([extra, extra], axis=1), v[0:8])
        return jnp.concatenate([top, v[8:32]], axis=0)

    def last_row(v, extra):
        tail = jnp.where(row8 == 7, jnp.concatenate([extra, extra], axis=1), v[24:32])
        return jnp.concatenate([v[0:24], tail], axis=0)

    edge_n = jnp.where(miss_n, 0.0, ext_n[0])
    txw = [first_row(x_prev(tx[l]), edge_n[4 + l : 5 + l]) for l in L]
    tyw = [y_prev(ty[l]) for l in L]

    def z_sum(faces, values, l):
        total = None
        if l < 3:
            total = faces[l] * values[l + 1]
        if l > 0:
            term = faces[l - 1] * values[l - 1]
            total = term if total is None else total + term
        return total

    ones = [None] * 4
    inv = []
    for l in L:
        den = pv[l] + tx[l] + txw[l] + ty[l] + tyw[l]
        if l < 3:
            den = den + tz[l]
        if l > 0:
            den = den + tz[l - 1]
        inv.append(1.0 / den)

    def gather(values, nexts, prevs):
        out = []
        for l in L:
            total = tx[l] * nexts[l] + txw[l] * prevs[l]
            total = total + ty[l] * y_next(values[l]) + tyw[l] * y_prev(values[l])
            out.append(total + z_sum(tz, values, l))
        return out

    sub8 = lax.broadcasted_iota(jnp.int32, (8, 128), 0)
    cut = lambda t: jnp.where(miss_s, 0.0, t)
    t0 = ext_s[0]
    lane8 = lax.broadcasted_iota(jnp.int32, (8, 128), 1)
    side0 = jnp.where(lane8 < 64, jnp.where(miss_e, 0.0, from_se[0]), jnp.where(miss_w, 0.0, from_sw[0]))
    t0 = jnp.concatenate([cut(t0), cut(side0)], axis=1)
    t0n, t0p = y_next(t0)[:, 0:128], y_prev(t0)[:, 0:128]
    t0 = t0[:, 0:128]
    t1, t2, t3 = cut(ext_s[1]), cut(ext_s[2]), cut(ext_s[3])
    low4 = lambda t: pltpu.roll(t, 4, axis=0)
    ty_x = jnp.where((lane8 == 127) & miss_e, 0.0, low4(t0))
    tyw_x = low4(t0p)
    tx_x, txw_x = low4(t2), t2
    pv_x = jnp.where(miss_s, 1.0, t3)
    tz_x = jnp.where(sub8 < 3, low4(t3), 0.0)
    tzw_x = jnp.where((sub8 >= 1) & (sub8 < 4), pltpu.roll(low4(t3), 1, axis=0), 0.0)
    num_x = (
        pv_x * t0 + src0_extra + tx_x * low4(t1) + txw_x * t1 + ty_x * t0n + tyw_x * t0p
        + tz_x * pltpu.roll(t0, 7, axis=0) + tzw_x * pltpu.roll(t0, 1, axis=0)
    )
    q_extra = num_x / (pv_x + tx_x + txw_x + ty_x + tyw_x + tz_x + tzw_x)

    ipv = [time_step / pv[l] for l in L]
    saved = []
    p = p0
    for n in range(2):
        p_next = [x_next(p[l]) for l in L]
        p_prev = [x_prev(p[l]) for l in L]
        if n == 0:
            p_prev = [first_row(p_prev[l], edge_n[l : l + 1]) for l in L]
        base = [pv[l] * p[l] + src[n][l] for l in L]
        total = gather(p, p_next, p_prev)
        q = [(base[l] + total[l]) * inv[l] for l in L]
        q_next = [x_next(q[l]) for l in L]
        if n == 0:
            q_next = [last_row(q_next[l], q_extra[l : l + 1]) for l in L]
        total = gather(q, q_next, [x_prev(q[l]) for l in L])
        r = [(base[l] + total[l]) * inv[l] for l in L]

        if n == 0:
            receive(2)
            s = [field(S0 + l, valid, 0.0) for l in L]
            up = [field(UP + l, valid, 0) for l in L]
            bits = [[[jnp.bitwise_and(up[l], 1 << (3 * n + d)) != 0 for d in range(3)] for l in L] for n in range(2)]

        den = []
        mob = []
        for l in L:
            wet = s[l] * s[l]
            dry = 1.0 - s[l]
            scale = 1.0 / (wet + 0.5 * dry * dry)
            den.append(scale)
            mob.append(wet * scale)
        dx = [r[l] - x_next(r[l]) for l in L]
        dy = [r[l] - y_next(r[l]) for l in L]
        dz = [r[l] - r[l + 1] for l in range(3)]
        fx = [jnp.where(bits[n][l][0], mob[l], x_next(mob[l])) for l in L]
        fy = [jnp.where(bits[n][l][1], mob[l], y_next(mob[l])) for l in L]
        fz = [jnp.where(bits[n][l][2], mob[l], mob[l + 1]) for l in range(3)]
        flow_x = [tx[l] * dx[l] * fx[l] for l in L]
        flow_y = [ty[l] * dy[l] * fy[l] for l in L]
        flow_z = [tz[l] * dz[l] * fz[l] for l in range(3)]
        moved = []
        for l in L:
            net = flow_x[l] - x_prev(flow_x[l]) + flow_y[l] - y_prev(flow_y[l])
            if l < 3:
                net = net + flow_z[l]
            if l > 0:
                net = net - flow_z[l - 1]
            moved.append(s[l] - ipv[l] * net)
        saved.append((p, q, r, s, den, dx, dy, dz, fx, fy, fz))
        p, s = r, moved

    grad_x = [None] * 4
    grad_y = [None] * 4
    grad_z = [None] * 3

    def accumulate(total, term):
        return term if total is None else total + term

    carried_p = [count[l] * p[l] - obs_p[1][l] for l in L]
    carried_s = [count[l] * s[l] - obs_s[1][l] for l in L]
    for n in (1, 0):
        p, q, r, s, den, dx, dy, dz, fx, fy, fz = saved[n]
        nu = [ipv[l] * carried_s[l] for l in L]
        mx = [x_next(nu[l]) - nu[l] for l in L]
        my = [y_next(nu[l]) - nu[l] for l in L]
        mz = [nu[l + 1] - nu[l] for l in range(3)]
        for l in L:
            grad_x[l] = accumulate(
                grad_x[l], main_tile(mx[l]) * main_tile(dx[l]) * main_tile(fx[l])
            )
            grad_y[l] = accumulate(
                grad_y[l], main_tile(my[l]) * main_tile(dy[l]) * main_tile(fy[l])
            )
            if l < 3:
                grad_z[l] = accumulate(
                    grad_z[l], main_tile(mz[l]) * main_tile(dz[l]) * main_tile(fz[l])
                )
        gx_ = [mx[l] * tx[l] for l in L]
        gy_ = [my[l] * ty[l] for l in L]
        gz_ = [mz[l] * tz[l] for l in range(3)]
        hx = [gx_[l] * fx[l] for l in L]
        hy = [gy_[l] * fy[l] for l in L]
        hz = [gz_[l] * fz[l] for l in range(3)]
        pi = []
        for l in L:
            total = carried_p[l] + hx[l] - x_prev(hx[l]) + hy[l] - y_prev(hy[l])
            if l < 3:
                total = total + hz[l]
            if l > 0:
                total = total - hz[l - 1]
            pi.append(total)
        if n:
            kx = [gx_[l] * dx[l] for l in L]
            ky = [gy_[l] * dy[l] for l in L]
            kz = [gz_[l] * dz[l] for l in range(3)]
            back_s = []
            for l in L:
                here = jnp.where(bits[n][l][0], kx[l], 0.0)
                there = kx[l] - here
                total = here + x_prev(there)
                here = jnp.where(bits[n][l][1], ky[l], 0.0)
                there = ky[l] - here
                total = total + here + y_prev(there)
                if l < 3:
                    total = total + jnp.where(bits[n][l][2], kz[l], 0.0)
                if l > 0:
                    total = total + jnp.where(bits[n][l - 1][2], 0.0, kz[l - 1])
                slope = (s[l] * den[l]) * ((1.0 - s[l]) * den[l])
                back_s.append(
                    carried_s[l] + slope * total + (count[l] * s[l] - obs_s[0][l])
                )
            carried_s = back_s

        w2 = [pi[l] * inv[l] for l in L]
        w2_next = [x_next(w2[l]) for l in L]
        rho = gather(w2, w2_next, [x_prev(w2[l]) for l in L])
        w1 = [rho[l] * inv[l] for l in L]
        w1_next = [x_next(w1[l]) for l in L]
        m = main_tile
        for l in L:
            a2, a1 = m(w2[l]), m(w1[l])
            rm, qm, pm = m(r[l]), m(q[l]), m(p[l])
            grad_x[l] = (
                grad_x[l]
                + a2 * (m(x_next(q[l])) - rm)
                + m(w2_next[l]) * (qm - m(x_next(r[l])))
                + a1 * (m(x_next(p[l])) - qm)
                + m(w1_next[l]) * (pm - m(x_next(q[l])))
            )
            grad_y[l] = (
                grad_y[l]
                + a2 * (m(y_next(q[l])) - rm)
                + m(y_next(w2[l])) * (qm - m(y_next(r[l])))
                + a1 * (m(y_next(p[l])) - qm)
                + m(y_next(w1[l])) * (pm - m(y_next(q[l])))
            )
            if l < 3:
                grad_z[l] = (
                    grad_z[l]
                    + a2 * (m(q[l + 1]) - rm)
                    + m(w2[l + 1]) * (qm - m(r[l + 1]))
                    + a1 * (m(p[l + 1]) - qm)
                    + m(w1[l + 1]) * (pm - m(q[l + 1]))
                )
        if n:
            back = gather(w1, w1_next, [x_prev(w1[l]) for l in L])
            carried_p = [
                back[l] + pv[l] * (w1[l] + w2[l]) + (count[l] * p[l] - obs_p[0][l]) for l in L
            ]

    for l in L:
        out[l] = jnp.where(main_tile(keep_x), grad_x[l], 0.0)
        out[4 + l] = jnp.where(main_tile(keep_y), grad_y[l], 0.0)
        if l < 3:
            out[8 + l] = grad_z[l]

    for copy, here, origin, group in sends:
        @pl.when(here)
        def _():
            copy.wait_send()


def adjoint(*args):
    f32, i32 = jnp.float32, jnp.int32
    tiles = lambda n: pltpu.VMEM((n, 8, 128), f32)
    halo = [
        pltpu.VMEM((UP, 16, 128), f32),
        pltpu.VMEM((4, 16, 128), i32),
        pltpu.VMEM((8, 128), f32),
        tiles(UP), tiles(UP),
        pltpu.VMEM((4, 8, 128), i32), pltpu.VMEM((4, 8, 128), i32),
        tiles(2), tiles(5), tiles(9), tiles(9), tiles(5), tiles(5), tiles(6), tiles(6),
    ]
    work = [
        pltpu.VMEM((1, 1, WELLS), i32),
        pltpu.VMEM((1, 1, WELLS), f32),
        pltpu.VMEM((2, 1, 1, WELLS), i32),
        pltpu.VMEM((2, 2, 1, 1, WELLS), f32),
        tiles(2), tiles(5), tiles(11), tiles(11),
    ]
    sems = [pltpu.SemaphoreType.DMA((n,)) for n in (11, 18, 18)] + [
        pltpu.SemaphoreType.REGULAR((8,)), pltpu.SemaphoreType.REGULAR
    ]
    return pl.pallas_call(
        adjoint_kernel,
        out_shape=pltpu.VMEM((11, 16, 128), f32),
        in_specs=[pl.BlockSpec(memory_space=pl.ANY)] * 11,
        out_specs=pl.BlockSpec(memory_space=pltpu.VMEM),
        scratch_shapes=halo + work + sems,
        compiler_params=pltpu.CompilerParams(collective_id=0, has_side_effects=True),
    )(*args)


def deliver_kernel(stack, out_x, out_y, out_z, sem):
    copies = [
        pltpu.make_async_copy(stack.at[pl.ds(first, n)], out, sem.at[i])
        for i, (first, n, out) in enumerate(((0, 4, out_x), (4, 4, out_y), (8, 3, out_z)))
    ]
    for copy in copies:
        copy.start()
    for copy in copies:
        copy.wait()


def deliver(stack):
    return pl.pallas_call(
        deliver_kernel,
        out_shape=[jax.ShapeDtypeStruct((n, 16, 128), jnp.float32) for n in (4, 4, 3)],
        in_specs=[pl.BlockSpec(memory_space=pltpu.VMEM)],
        out_specs=[pl.BlockSpec(memory_space=pl.ANY)] * 3,
        scratch_shapes=[pltpu.SemaphoreType.DMA((3,))],
    )(pltpu.with_memory_space_constraint(stack, pltpu.VMEM))


def on_device(*args):
    return tuple(deliver(adjoint(*args)))


def solution(mesh):
    field = P(None, "gx", "gy")
    in_specs = (field,) * 7 + (
        P("gx", "gy", None),
        P("gx", "gy", None),
        P(None, "gx", "gy", None),
        P(None, None, "gx", "gy", None),
    )
    return jax.shard_map(
        on_device, mesh=mesh, in_specs=in_specs, out_specs=(field,) * 3, check_vma=False
    )
```
